256 devices in a mesh: slab: 16 (over y, x), energy: 8 (over z), mom: 2 (over core).
Axes of the slice: x: 4, y: 4, z: 8, core: 2. Of those that a mesh axis runs over, the one named last changes fastest.
Arguments:
- onsite: float32 [2, 16, 256], P('mom', 'slab'), may hold values from -0.5 to 0.5
- hop: float32 [2, 16, 2, 256, 256], P('mom', 'slab'), may hold values from -0.0234375 to 0.0234375
- couple: float32 [2, 16, 2, 256, 256], P('mom', 'slab'), may hold values from -2 to 2
- sigma_in: float32 [16, 16, 2, 256, 256], P('energy', 'slab'), may hold values from -0.03125 to 0.03125
- shifts: int32 [4], replicated, may hold values from 1 to 15
- mode_weight: float32 [2, 4], replicated, may hold values from 0.2 to 1
Outputs:
- sigma_out: float32 [16, 16, 2, 256, 256], P(None, 'slab', None, 'energy')
The draws below stay inside these ranges and needn't reach their ends.
Inputs may be any that keep to these rules, and one draw needn't show every extreme that they name: `shifts`: energy-index offsets of the phonon modes.
All inputs are finite; a program needn't handle non-finite values.
Results may differ from the reference program's by a relative error of at most 0.00025.
Values sent between devices are 32-bit elements; how exact they have to be, the bound alone decides.
A program may use at most 128 MiB of HBM per device.

```python
import math
import jax
import jax.numpy as jnp
from jax import lax

O = 256
NMODE = 4
NE = 16
NS = 16
NK = 2


def draw_couple(key, part):
    key_size = jax.random.fold_in(key, 11)
    key_phase = jax.random.fold_in(key, 12)
    key_noise = jax.random.fold_in(key, 13)
    magnitude = jnp.exp(jax.random.uniform(key_size, (NK, NS, O), jnp.float32, math.log(1.6), math.log(2.0)))
    phase = jax.random.uniform(key_phase, (NK, NS, O), jnp.float32, -math.pi, math.pi)
    noise = jnp.clip(jax.random.normal(key_noise, (NK, NS, 2, O, O), jnp.float32), -4.0, 4.0)
    noise = noise * (0.03 / math.sqrt(O))
    identity = jnp.eye(O, dtype=jnp.float32)
    outside = 1.0 - identity
    real_part = noise[:, :, 0] * outside + identity * (magnitude * jnp.cos(phase))[..., None, :]
    imag_part = noise[:, :, 1] * outside + identity * (magnitude * jnp.sin(phase))[..., None, :]
    return jnp.stack([real_part, imag_part], axis=2).astype(jnp.float32)


def touch_ends(array, key, least, high):
    longest = array.shape.index(max(array.shape))
    spots = []
    for shift in (0, 1):
        where = [jax.random.randint(jax.random.fold_in(key, axis), (), 0, length) for axis, length in enumerate(array.shape)]
        where[longest] = (where[longest] + shift) % array.shape[longest]
        spots.append(tuple(where))
    return array.at[spots[0]].set(least).at[spots[1]].set(high)


def block_scale(own_key, shape, pieces, least, top_value):
    gain, own = 1.0, jax.random.fold_in(own_key, 6)
    for position, shards_of in pieces:
        draws = jnp.exp(jax.random.uniform(jax.random.fold_in(own, position), (shards_of,), jnp.float32, least / len(pieces), top_value / len(pieces)))
        gain = gain * jnp.repeat(draws, shape[position] // shards_of).reshape([-1 if axis == position else 1 for axis in range(len(shape))])
    return gain


def normal_values(own_key, extent, width, reach, shards=(), kind=jnp.bfloat16):
    values = width * jax.random.normal(own_key, extent, jnp.float32)
    if shards:
        values = values * block_scale(own_key, extent, shards, -0.22, 0.18)
    return jnp.clip(values, -reach, reach).astype(kind)


def setup_inputs(seed: int = 0) -> dict:
    key_list = jax.random.split(jax.random.key(seed), 7)
    onsite = jnp.clip(jax.random.uniform(key_list[0], (NK, NS, O), jnp.float32, -0.5, 0.5) * block_scale(key_list[0], (NK, NS, O), ((0, 2), (1, 16)), -0.4, 0.0), -0.5, 0.5)
    hop = normal_values(key_list[1], (NK, NS, 2, O, O), (256 * O) ** -0.5, 0.0234375, ((0, 2), (1, 16)), jnp.float32)
    couple = draw_couple(jax.random.fold_in(key_list[6], 71), 0)
    sigma_in = normal_values(key_list[3], (NE, NS, 2, O, O), (128 * O) ** -0.5, 0.03125, ((0, 8), (1, 16)), jnp.float32)
    shifts = touch_ends(jax.random.randint(key_list[4], (NMODE,), 1, NE), jax.random.fold_in(key_list[4], 1), 1, NE - 1).astype(jnp.int32)
    mode_weight = jnp.clip(jnp.exp(jax.random.uniform(key_list[5], (2, NMODE), jnp.float32, math.log(0.2), math.log(1.0))), 0.2, 1.0)
    return dict(onsite=onsite, hop=hop, couple=couple, sigma_in=sigma_in, shifts=shifts, mode_weight=mode_weight)


ETA = 0.5
HIGH = lax.Precision.HIGHEST


def complex_mul(form, left, right):
    def product(first, second):
        return jnp.einsum(form, first, second, precision=HIGH)
    return (product(left[0], right[0]) - product(left[1], right[1]),
            product(left[0], right[1]) + product(left[1], right[0]))


def newton_inverse(mat_real, mat_imag, form, identity):
    diag_real = jnp.diagonal(mat_real, axis1=-2, axis2=-1)
    diag_imag = jnp.diagonal(mat_imag, axis1=-2, axis2=-1)
    denom = diag_real * diag_real + diag_imag * diag_imag
    x_real = diag_real / denom
    x_imag = -diag_imag / denom
    rows_real = x_real[..., :, None] * mat_real - x_imag[..., :, None] * mat_imag
    rows_imag = x_real[..., :, None] * mat_imag + x_imag[..., :, None] * mat_real
    both_real = rows_real * x_real[..., None, :] - rows_imag * x_imag[..., None, :]
    both_imag = rows_real * x_imag[..., None, :] + rows_imag * x_real[..., None, :]
    first = (2.0 * identity * x_real[..., None, :] - both_real, 2.0 * identity * x_imag[..., None, :] - both_imag)
    resid = complex_mul(form, (mat_real, mat_imag), first)
    second = complex_mul(form, first, resid)
    return (2.0 * first[0] - second[0], 2.0 * first[1] - second[1])


def phonon_matrix(shifts, mode_weight, count):
    rows = jnp.arange(count)[:, None, None]
    cols = jnp.arange(count)[None, :, None]
    offset = shifts[None, None, :]
    upper = (cols == rows + offset).astype(jnp.float32)
    lower = (cols == rows - offset).astype(jnp.float32)
    return jnp.sum(upper * mode_weight[0] + lower * mode_weight[1], axis=2)


def reference(onsite, hop, couple, sigma_in, shifts, mode_weight):
    identity = jnp.eye(O, dtype=jnp.float32)
    energy = -0.5 + (jnp.arange(NE).astype(jnp.float32) + 0.5) / NE
    greens = []
    previous = None
    for slab_no in range(NS):
        coupling = (couple[:, slab_no, 0], couple[:, slab_no, 1])
        adjoint = (jnp.swapaxes(coupling[0], -1, -2), -jnp.swapaxes(coupling[1], -1, -2))
        if previous is None:
            left_real = jnp.zeros((NK, NE, O, O), jnp.float32)
            left_imag = jnp.zeros((NK, NE, O, O), jnp.float32)
        else:
            temp = complex_mul('kij,kejl->keil', coupling, previous)
            left_real, left_imag = complex_mul('keij,kjl->keil', temp, adjoint)
        z_real = energy[None, :, None] - onsite[:, slab_no][:, None, :]
        mat_real = identity * z_real[..., None, :] - hop[:, slab_no, 0][:, None] - sigma_in[:, slab_no, 0][None] - left_real
        mat_imag = identity * ETA - hop[:, slab_no, 1][:, None] - sigma_in[:, slab_no, 1][None] - left_imag
        green = newton_inverse(mat_real, mat_imag, 'keij,kejl->keil', identity)
        greens.append(green)
        previous = green
    phonon = phonon_matrix(shifts, mode_weight, NE)
    outputs = [None] * NS
    coupled = None
    for slab_no in range(NS - 1, -1, -1):
        green = greens[slab_no]
        if coupled is None:
            full = green
        else:
            temp = complex_mul('keij,kejl->keil', green, coupled)
            extra = complex_mul('keij,kejl->keil', temp, green)
            full = (green[0] + extra[0], green[1] + extra[1])
        stacked = jnp.stack(full, axis=2)
        outputs[slab_no] = jnp.einsum('ef,kfsjl->esjl', phonon, stacked, precision=HIGH) / NK
        coupling = (couple[:, slab_no, 0], couple[:, slab_no, 1])
        adjoint = (jnp.swapaxes(coupling[0], -1, -2), -jnp.swapaxes(coupling[1], -1, -2))
        temp = complex_mul('kij,kejl->keil', adjoint, full)
        coupled = complex_mul('keij,kjl->keil', temp, coupling)
    return jnp.stack(outputs, axis=1)
```

```python
import jax
import jax.numpy as jnp
from jax import lax
from jax.experimental import pallas as pl
from jax.experimental.pallas import tpu as pltpu
from jax.sharding import PartitionSpec as P

ETA = 0.5
HIGH = lax.Precision.HIGHEST
ROW = 4


def split(mat):
    top = mat.astype(jnp.bfloat16)
    return top, (mat - top.astype(jnp.float32)).astype(jnp.bfloat16)


def dot(left, right):
    return jnp.dot(left, right, preferred_element_type=jnp.float32)


def complex_mul(left, right):
    width = left[0].shape[0]
    left_top, left_low = split(jnp.concatenate(left, axis=0))
    outs = []
    for part in right:
        top, low = split(part)
        outs.append(dot(left_top, top) + (dot(left_top, low) + dot(left_low, top)))
    real, imag = outs
    return real[:width] - imag[width:], imag[:width] + real[width:]


def newton_inverse(mat, eye):
    diag_row = tuple(jnp.sum(jnp.where(eye, part, 0.0), axis=0, keepdims=True) for part in mat)
    diag_col = tuple(jnp.sum(jnp.where(eye, part, 0.0), axis=1, keepdims=True) for part in mat)

    def inverse(diag):
        denom = diag[0] * diag[0] + diag[1] * diag[1]
        return diag[0] / denom, -diag[1] / denom

    row, col = inverse(diag_row), inverse(diag_col)
    off = tuple(jnp.where(eye, 0.0, part) for part in mat)
    first = (off[0] * row[0] - off[1] * row[1], off[0] * row[1] + off[1] * row[0])
    second = complex_mul(first, first)
    third = complex_mul(first, second)
    series = (
        jnp.where(eye, 1.0, 0.0) - first[0] + second[0] - third[0],
        second[1] - first[1] - third[1],
    )
    return (
        col[0] * series[0] - col[1] * series[1],
        col[0] * series[1] + col[1] * series[0],
    )


def eye_mask(width):
    shape = (width, width)
    return lax.broadcasted_iota(jnp.int32, shape, 0) == lax.broadcasted_iota(jnp.int32, shape, 1)


def forward_kernel(place, received, bundle, green):
    eye = eye_mask(received.shape[-1])

    def step(j, carry):
        slot = lax.rem(place[0] - j + ROW, ROW)
        coupling = (bundle[slot, 2], bundle[slot, 3])
        adjoint = (bundle[slot, 2].T, -bundle[slot, 3].T)
        left = complex_mul(complex_mul(coupling, carry), adjoint)
        mat = (bundle[slot, 0] - left[0], bundle[slot, 1] - left[1])
        result = newton_inverse(mat, eye)
        green[j, 0] = result[0]
        green[j, 1] = result[1]
        return result

    lax.fori_loop(0, ROW, step, (received[0], received[1]))


def backward_kernel(place, received, bundle, green, full, coupled):

    def step(back, carry):
        j = ROW - 1 - back
        slot = lax.rem(place[0] - j + ROW, ROW)
        pair = (green[j, 0], green[j, 1])
        extra = complex_mul(complex_mul(pair, carry), pair)
        total = (pair[0] + extra[0], pair[1] + extra[1])
        full[j, 0] = total[0]
        full[j, 1] = total[1]
        adjoint = (bundle[slot, 2].T, -bundle[slot, 3].T)
        return complex_mul(complex_mul(adjoint, total), (bundle[slot, 2], bundle[slot, 3]))

    result = lax.fori_loop(0, ROW, step, (received[0], received[1]))
    coupled[0] = result[0]
    coupled[1] = result[1]


def call(kernel, shapes, args):
    specs = [pl.BlockSpec(memory_space=pltpu.SMEM)]
    specs += [pl.BlockSpec(memory_space=pltpu.VMEM)] * (len(args) - 1)
    return pl.pallas_call(
        kernel,
        out_shape=[jax.ShapeDtypeStruct(shape, jnp.float32) for shape in shapes],
        in_specs=specs,
        out_specs=[pl.BlockSpec(memory_space=pltpu.VMEM)] * len(shapes),
        compiler_params=pltpu.CompilerParams(vmem_limit_bytes=48 << 20),
    )(*args)


def phonon_matrix(shifts, mode_weight, count):
    rows = jnp.arange(count)[:, None, None]
    cols = jnp.arange(count)[None, :, None]
    offset = shifts[None, None, :]
    upper = (cols == rows + offset).astype(jnp.float32)
    lower = (cols == rows - offset).astype(jnp.float32)
    return jnp.sum(upper * mode_weight[0] + lower * mode_weight[1], axis=2)


def body(onsite, hop, couple, sigma_in, shifts, mode_weight):
    e_local = sigma_in.shape[0]
    width = onsite.shape[-1]
    slab_count = lax.axis_size("slab")
    rows = slab_count // ROW
    slab = lax.axis_index("slab")
    row, place = slab // ROW, lax.rem(slab, ROW)
    mom = lax.axis_index("mom")
    energy_count = lax.axis_size("energy")
    mom_count = lax.axis_size("mom")
    total = e_local * energy_count
    identity = jnp.eye(width, dtype=jnp.float32)
    global_index = lax.axis_index("energy") * e_local + jnp.arange(e_local)
    energies = -0.5 + (global_index.astype(jnp.float32) + 0.5) / total
    z_real = energies[:, None] - onsite[0, 0][None, :]
    base_real = identity * z_real[:, None, :] - hop[0, 0, 0] - sigma_in[:, 0, 0]
    base_imag = identity * ETA - hop[0, 0, 1] - sigma_in[:, 0, 1]

    def hosts(turn):
        found = []
        for r in range(rows):
            for k in range(mom_count):
                for e in range(e_local):
                    x = e_local * k + e
                    found.append((r * ROW + x, r * ROW + (x - turn) % ROW, k))
        return found

    def bundle_for(e):
        return jnp.stack(
            [
                lax.dynamic_index_in_dim(base_real, e, 0, False),
                lax.dynamic_index_in_dim(base_imag, e, 0, False),
                couple[0, 0, 0],
                couple[0, 0, 1],
            ]
        )

    parts = []
    for turn in range(ROW):
        target = lax.rem(place + turn, ROW)
        bundle = bundle_for(jnp.clip(target - e_local * mom, 0, e_local - 1))
        if turn:
            pairs = [(s * mom_count + k, h * mom_count + k) for h, s, k in hosts(turn)]
            bundle = lax.ppermute(bundle, ("slab", "mom"), pairs)
        parts.append(bundle)
    bundles = jnp.stack(parts)
    is_host = place // e_local == mom
    where = place[None]
    block = (2, width, width)
    green = jnp.zeros((ROW,) + block, jnp.float32)
    full = green
    received = jnp.zeros(block, jnp.float32)
    for r in range(rows):
        if r:
            pairs = [((r - 1) * ROW + x, r * ROW + x) for x in range(ROW)]
            received = lax.ppermute(green[ROW - 1], "slab", pairs)
        green = lax.cond(
            jnp.logical_and(is_host, row == r),
            lambda got: call(forward_kernel, [(ROW,) + block], (where, got, bundles))[0],
            lambda got: green,
            received,
        )
    received = jnp.zeros(block, jnp.float32)
    coupled = received
    for r in range(rows - 1, -1, -1):
        if r < rows - 1:
            pairs = [((r + 1) * ROW + x, r * ROW + x) for x in range(ROW)]
            received = lax.ppermute(coupled, "slab", pairs)
        full, coupled = lax.cond(
            jnp.logical_and(is_host, row == r),
            lambda got: tuple(call(backward_kernel, [(ROW,) + block, block], (where, got, bundles, green))),
            lambda got: (full, coupled),
            received,
        )
    mine = lax.dynamic_index_in_dim(full, place, 0, False)
    energy_at = place - e_local * mom
    blocks = [jnp.where(energy_at == e, mine, 0.0) for e in range(e_local)]
    for turn in range(1, ROW):
        pairs = [(h * mom_count + k, s * mom_count + k) for h, s, k in hosts(turn)]
        piece = lax.dynamic_index_in_dim(full, lax.rem(place - turn + ROW, ROW), 0, False)
        piece = lax.ppermute(piece, ("slab", "mom"), pairs)
        energy_at = lax.rem(place + turn, ROW) - e_local * mom
        blocks = [jnp.where(energy_at == e, piece, blocks[e]) for e in range(e_local)]
    own = jnp.stack(blocks)[:, None]
    phonon = phonon_matrix(shifts, mode_weight, total)
    mixed = jnp.einsum(
        "ef,fsrjl->esrjl",
        phonon,
        lax.all_to_all(own, "energy", split_axis=3, concat_axis=0, tiled=True),
        precision=HIGH,
    )
    return lax.psum(mixed, "mom") / mom_count


def solution(mesh):
    in_specs = (
        P("mom", "slab", None),
        P("mom", "slab", None, None, None),
        P("mom", "slab", None, None, None),
        P("energy", "slab", None, None, None),
        P(),
        P(),
    )
    out_specs = P(None, "slab", None, "energy", None)
    return jax.shard_map(body, mesh=mesh, in_specs=in_specs, out_specs=out_specs, check_vma=False)
```

```python
import functools

import jax
import jax.numpy as jnp
from jax import lax
from jax.experimental import pallas as pl
from jax.experimental.pallas import tpu as pltpu
from jax.sharding import PartitionSpec as P

ETA = 0.5
ROW = 4
MESH = pl.DeviceIdType.MESH


def split(mat):
    top = mat.astype(jnp.bfloat16)
    return top, (mat - top.astype(jnp.float32)).astype(jnp.bfloat16)


def prep(pair):
    return split(pair[0]), split(pair[1]), split(pair[0] + pair[1])


def prep_adjoint(pair):
    return prep((pair[0].T, -pair[1].T))


def mul(left, right):
    outs = []
    for (left_top, left_low), (top, low) in zip(left, right):
        outs.append(
            jnp.dot(
                jnp.concatenate([left_top, left_top, left_low], axis=1),
                jnp.concatenate([top, low, top], axis=0),
                preferred_element_type=jnp.float32,
            )
        )
    return outs[0] - outs[1], outs[2] - (outs[0] + outs[1])


def eye_mask(size):
    shape = (size, size)
    return lax.broadcasted_iota(jnp.int32, shape, 0) == lax.broadcasted_iota(jnp.int32, shape, 1)


def on_diagonal(mat, change):
    half = mat.shape[0] // 2
    upper = jnp.concatenate([change(mat[:half, :half], 0), mat[:half, half:]], axis=1)
    lower = jnp.concatenate([mat[half:, :half], change(mat[half:, half:], 1)], axis=1)
    return jnp.concatenate([upper, lower], axis=0)


def newton_inverse(mat):
    half = mat[0].shape[0] // 2
    eye = eye_mask(half)
    blocks = [
        [jnp.where(eye, part[:half, :half], 0.0), jnp.where(eye, part[half:, half:], 0.0)]
        for part in mat
    ]

    def inverse(diag):
        scale = 1.0 / (diag[0] * diag[0] + diag[1] * diag[1])
        return diag[0] * scale, -diag[1] * scale

    row = inverse(
        [jnp.concatenate([jnp.sum(b, axis=0, keepdims=True) for b in pair], axis=1) for pair in blocks]
    )
    col = inverse(
        [jnp.concatenate([jnp.sum(b, axis=1, keepdims=True) for b in pair], axis=0) for pair in blocks]
    )
    off = [on_diagonal(part, lambda block, n: jnp.where(eye, 0.0, block)) for part in mat]
    first = (off[0] * row[0] - off[1] * row[1], off[0] * row[1] + off[1] * row[0])
    fixed = prep(first)
    second = mul(fixed, fixed)
    third = mul(prep(second), fixed)
    real = second[0] - first[0] - third[0]
    imag = second[1] - first[1] - third[1]
    real = on_diagonal(real, lambda block, n: block + jnp.where(eye, 1.0, 0.0))
    return col[0] * real - col[1] * imag, col[0] * imag + col[1] * real


def load(ref):
    return ref[0], ref[1]


def store(ref, pair):
    ref[0] = pair[0]
    ref[1] = pair[1]


def kernel(
    rows, depth, e_local,
    mix, levels, hop, couple, sigma, out,
    outgoing, base, coup, green, left, h_coup, h_green, h_adj, h_first, h_second,
    h_chain, chain, full, gathered, summed, mixed,
    s_base, r_base, s_coup, r_coup, s_hcoup, r_hcoup, s_hgreen, r_hgreen,
    s_hop, r_hop, s_chain, r_chain, s_back, r_back, s_first, r_first,
    s_second, r_second, s_last, r_last,
):
    slab = lax.axis_index("slab")
    plane = lax.axis_index("energy")
    mom = lax.axis_index("mom")
    y, x = slab // ROW, lax.rem(slab, ROW)
    other = 1 - mom
    width = hop.shape[-1]
    share = width // depth
    is_main = x // e_local == mom
    at_start = jnp.logical_and(y == 0, x == 0)

    def send(src, dst, send_sem, recv_sem, **where):
        return pltpu.make_async_remote_copy(
            src_ref=src, dst_ref=dst, send_sem=send_sem, recv_sem=recv_sem,
            device_id=where, device_id_type=MESH,
        )

    def arrived(dst, recv_sem):
        send(dst, dst, s_hop.at[0], recv_sem, mom=other).wait_recv()

    barrier = pltpu.get_barrier_semaphore()

    def greet(**where):
        pl.semaphore_signal(barrier, inc=1, device_id=where, device_id_type=MESH)

    greet(mom=other)
    for turn in range(1, ROW):
        peer = y * ROW + lax.rem(x + turn, ROW)
        greet(slab=peer, mom=mom)
        greet(slab=peer, mom=other)
    for turn in (1, rows - 1):
        greet(slab=lax.rem(y + turn, rows) * ROW + x)
    for turn in range(1, depth):
        greet(energy=lax.rem(plane + turn, depth))
    pl.semaphore_wait(barrier, 1 + 2 * (ROW - 1) + 2 + depth - 1)

    half = width // 2
    eye = eye_mask(half)

    def base_copy(e):
        return send(
            outgoing.at[e], base.at[x], s_base.at[e], r_base.at[x], slab=y * ROW + e_local * mom + e
        )

    def coup_copy(e):
        return send(couple, coup.at[x], s_coup.at[e], r_coup.at[x], slab=y * ROW + e_local * mom + e)

    def is_remote(e):
        return e_local * mom + e != x

    def sends_coup(e):
        return jnp.logical_and(is_remote(e), jnp.logical_not(at_start))

    for e in range(e_local):
        level = levels[e : e + 1]
        real = on_diagonal(
            -hop[0] - sigma[e, 0],
            lambda block, n: block + jnp.where(eye, level[:, n * half : (n + 1) * half], 0.0),
        )
        imag = on_diagonal(
            -hop[1] - sigma[e, 1], lambda block, n: block + jnp.where(eye, ETA, 0.0)
        )

        @pl.when(is_remote(e))
        def _():
            store(outgoing.at[e], (real, imag))
            base_copy(e).start()

        @pl.when(jnp.logical_not(is_remote(e)))
        def _():
            store(base.at[x], (real, imag))
            store(coup.at[x], load(couple))

    for e in range(e_local):

        @pl.when(sends_coup(e))
        def _():
            coup_copy(e).start()

    def hcoup_copy(j):
        return send(coup.at[j], h_coup.at[j], s_hcoup.at[j], r_hcoup.at[j], mom=other)

    def hgreen_copy(j):
        return send(green.at[j + 1], h_green.at[j], s_hgreen.at[j], r_hgreen.at[j], mom=other)

    def hop_copy():
        return send(green.at[ROW], green.at[0], s_hop.at[0], r_hop.at[0], slab=slab + ROW)

    def chain_copy(j):
        return send(h_chain.at[j + 1], chain.at[j], s_chain.at[j], r_chain.at[j], mom=other)

    def back_copy():
        return send(h_chain.at[0], h_chain.at[ROW], s_back.at[0], r_back.at[0], slab=slab - ROW)

    def first_copy(j, part):
        return send(
            full.at[j, part], gathered.at[x], s_first.at[j, part], r_first.at[x],
            slab=y * ROW + j, mom=part,
        )

    def is_first(j):
        return jnp.logical_and(y == 0, j == 0)

    def is_last(j):
        return jnp.logical_and(y == rows - 1, j == ROW - 1)

    def first_remote(j, part):
        return jnp.logical_or(j != x, part != mom)

    @pl.when(is_main)
    def _():
        @pl.when(y > 0)
        def _():
            arrived(green.at[0], r_hop.at[0])

        def forward(j, carry):
            @pl.when(j != x)
            def _():
                arrived(base.at[j], r_base.at[j])

            @pl.when(is_first(j))
            def _():
                left[...] = jnp.zeros_like(left)

            @pl.when(jnp.logical_not(is_first(j)))
            def _():
                @pl.when(j != x)
                def _():
                    arrived(coup.at[j], r_coup.at[j])

                hcoup_copy(j).start()
                coupling = load(coup.at[j])
                half_way = mul(prep(load(green.at[j])), prep_adjoint(coupling))
                store(left, mul(prep(coupling), prep(half_way)))

            store(
                green.at[j + 1],
                newton_inverse((base[j, 0] - left[0], base[j, 1] - left[1])),
            )

            @pl.when(jnp.logical_not(is_first(j)))
            def _():
                hgreen_copy(j).start()

            return carry

        lax.fori_loop(0, ROW, forward, 0)

        @pl.when(y < rows - 1)
        def _():
            hop_copy().start()

        def backward(turn, carry):
            j = ROW - 1 - turn

            @pl.when(is_last(j))
            def _():
                full[j] = green[j + 1]

            @pl.when(jnp.logical_not(is_last(j)))
            def _():
                arrived(chain.at[j], r_chain.at[j])
                pair = load(green.at[j + 1])
                ready = prep(pair)
                extra = mul(prep(mul(ready, prep(load(chain.at[j])))), ready)
                store(full.at[j], (pair[0] + extra[0], pair[1] + extra[1]))

            for part in range(2):

                @pl.when(first_remote(j, part))
                def _():
                    first_copy(j, part).start()

                @pl.when(jnp.logical_not(first_remote(j, part)))
                def _():
                    gathered[x] = full[j, part]

            return carry

        lax.fori_loop(0, ROW, backward, 0)

    @pl.when(jnp.logical_not(is_main))
    def _():
        def forward(j, carry):
            @pl.when(jnp.logical_not(is_first(j)))
            def _():
                arrived(h_coup.at[j], r_hcoup.at[j])
                coupling = load(h_coup.at[j])
                adjoint = (coupling[0].T, -coupling[1].T)
                store(h_adj.at[j], adjoint)
                arrived(h_green.at[j], r_hgreen.at[j])
                ready = prep(load(h_green.at[j]))
                store(h_first.at[j], mul(prep(adjoint), ready))
                store(h_second.at[j], mul(ready, prep(coupling)))

            return carry

        lax.fori_loop(0, ROW, forward, 0)

        @pl.when(y == rows - 1)
        def _():
            h_chain[ROW] = jnp.zeros_like(h_chain.at[ROW])

        @pl.when(y < rows - 1)
        def _():
            arrived(h_chain.at[ROW], r_back.at[0])

        def backward(turn, carry):
            j = ROW - 1 - turn

            @pl.when(jnp.logical_not(is_last(j)))
            def _():
                chain_copy(j).start()

            @pl.when(jnp.logical_not(is_first(j)))
            def _():
                extra = mul(prep(load(h_first.at[j])), prep(load(h_chain.at[j + 1])))
                adjoint = load(h_adj.at[j])
                sums = (adjoint[0] + extra[0], adjoint[1] + extra[1])
                store(h_chain.at[j], mul(prep(sums), prep(load(h_second.at[j]))))

            return carry

        lax.fori_loop(0, ROW, backward, 0)

        @pl.when(y > 0)
        def _():
            back_copy().start()

    for c in range(ROW):

        @pl.when(jnp.logical_or(c != x, jnp.logical_not(is_main)))
        def _():
            arrived(gathered.at[c], r_first.at[c])

    for e in range(e_local):
        summed[e] = gathered[e] + gathered[e_local + e]

    def second_copy(turn):
        target = lax.rem(plane + turn, depth)
        return send(
            summed.at[:, pl.ds(pl.multiple_of(target * share, 8), share)], mixed.at[plane],
            s_second.at[turn], r_second.at[plane], energy=target,
        )

    for turn in range(1, depth):
        second_copy(turn).start()
    mixed[plane] = summed[:, pl.ds(pl.multiple_of(plane * share, 8), share)]
    for turn in range(1, depth):
        source = lax.rem(plane + turn, depth)
        arrived(mixed.at[source], r_second.at[source])

    def mixing(e, carry):
        total = jnp.zeros((share, width), jnp.float32)
        for f in range(depth * e_local):
            total = total + mix[e, f] * mixed[f // e_local, f % e_local]
        out[e, mom] = total
        return carry

    lax.fori_loop(0, depth * e_local, mixing, 0)
    last_copy = send(out.at[:, mom], out.at[:, mom], s_last.at[0], r_last.at[0], mom=other)
    last_copy.start()

    for e in range(e_local):

        @pl.when(is_remote(e))
        def _():
            base_copy(e).wait_send()

        @pl.when(sends_coup(e))
        def _():
            coup_copy(e).wait_send()

    @pl.when(is_main)
    def _():
        for j in range(ROW):

            @pl.when(jnp.logical_not(is_first(j)))
            def _():
                hcoup_copy(j).wait_send()
                hgreen_copy(j).wait_send()

            for part in range(2):

                @pl.when(first_remote(j, part))
                def _():
                    first_copy(j, part).wait_send()

        @pl.when(y < rows - 1)
        def _():
            hop_copy().wait_send()

    @pl.when(jnp.logical_not(is_main))
    def _():
        for j in range(ROW):

            @pl.when(jnp.logical_not(is_last(j)))
            def _():
                chain_copy(j).wait_send()

        @pl.when(y > 0)
        def _():
            back_copy().wait_send()

    for turn in range(1, depth):
        second_copy(turn).wait_send()
    last_copy.wait_send()
    arrived(out.at[:, other], r_last.at[0])


def phonon_matrix(shifts, mode_weight, count):
    rows = jnp.arange(count)[:, None, None]
    cols = jnp.arange(count)[None, :, None]
    offset = shifts[None, None, :]
    upper = (cols == rows + offset).astype(jnp.float32)
    lower = (cols == rows - offset).astype(jnp.float32)
    return jnp.sum(upper * mode_weight[0] + lower * mode_weight[1], axis=2)


def body(onsite, hop, couple, sigma_in, shifts, mode_weight):
    e_local = sigma_in.shape[0]
    width = onsite.shape[-1]
    rows = lax.axis_size("slab") // ROW
    depth = lax.axis_size("energy")
    mom_count = lax.axis_size("mom")
    total = e_local * depth
    share = width // depth
    global_index = lax.axis_index("energy") * e_local + jnp.arange(e_local)
    energies = -0.5 + (global_index.astype(jnp.float32) + 0.5) / total
    levels = energies[:, None] - onsite[0, 0][None, :]
    mix = phonon_matrix(shifts, mode_weight, total) / mom_count
    block = (2, width, width)

    def buffer(*shape):
        return pltpu.VMEM(shape, jnp.float32)

    def sems(*shape):
        return pltpu.SemaphoreType.DMA(shape)

    vmem = pl.BlockSpec(memory_space=pltpu.VMEM)
    result = pl.pallas_call(
        functools.partial(kernel, rows, depth, e_local),
        out_shape=jax.ShapeDtypeStruct((total, 2, share, width), jnp.float32),
        in_specs=[pl.BlockSpec(memory_space=pltpu.SMEM)] + [vmem] * 4,
        out_specs=vmem,
        scratch_shapes=[
            buffer(e_local, *block),
            buffer(ROW, *block),
            buffer(ROW, *block),
            buffer(ROW + 1, *block),
            buffer(*block),
            buffer(ROW, *block),
            buffer(ROW, *block),
            buffer(ROW, *block),
            buffer(ROW, *block),
            buffer(ROW, *block),
            buffer(ROW + 1, *block),
            buffer(ROW, *block),
            buffer(ROW, *block),
            buffer(ROW, width, width),
            buffer(e_local, width, width),
            buffer(depth, e_local, share, width),
            sems(e_local), sems(ROW), sems(e_local), sems(ROW),
            sems(ROW), sems(ROW), sems(ROW), sems(ROW),
            sems(1), sems(1), sems(ROW), sems(ROW), sems(1), sems(1),
            sems(ROW, 2), sems(ROW), sems(depth), sems(depth), sems(1), sems(1),
        ],
        compiler_params=pltpu.CompilerParams(
            collective_id=0, has_side_effects=True, vmem_limit_bytes=56 << 20
        ),
    )(mix, levels, hop[0, 0], couple[0, 0], sigma_in[:, 0])
    return result[:, None]


def solution(mesh):
    in_specs = (
        P("mom", "slab", None),
        P("mom", "slab", None, None, None),
        P("mom", "slab", None, None, None),
        P("energy", "slab", None, None, None),
        P(),
        P(),
    )
    out_specs = P(None, "slab", None, "energy", None)
    return jax.shard_map(body, mesh=mesh, in_specs=in_specs, out_specs=out_specs, check_vma=False)
```

```python
import functools

import jax
import jax.numpy as jnp
from jax import lax
from jax.experimental import pallas as pl
from jax.experimental.pallas import tpu as pltpu
from jax.sharding import PartitionSpec as P

ETA = 0.5
ROW = 4
CUT = 6
PIECES = 4
MESH = pl.DeviceIdType.MESH


def split(mat):
    top = mat.astype(jnp.bfloat16)
    return top, (mat - top.astype(jnp.float32)).astype(jnp.bfloat16)


def prep(pair):
    return split(pair[0]), split(pair[1]), split(pair[0] + pair[1])


def prep_adjoint(pair):
    return prep((pair[0].T, -pair[1].T))


def mul(left, right):
    outs = []
    for (left_top, left_low), (top, low) in zip(left, right):
        outs.append(
            jnp.dot(
                jnp.concatenate([left_top, left_top, left_low], axis=1),
                jnp.concatenate([top, low, top], axis=0),
                preferred_element_type=jnp.float32,
            )
        )
    return outs[0] - outs[1], outs[2] - (outs[0] + outs[1])


def eye_mask(size):
    shape = (size, size)
    return lax.broadcasted_iota(jnp.int32, shape, 0) == lax.broadcasted_iota(jnp.int32, shape, 1)


def on_diagonal(mat, change):
    half = mat.shape[0] // 2
    upper = jnp.concatenate([change(mat[:half, :half], 0), mat[:half, half:]], axis=1)
    lower = jnp.concatenate([mat[half:, :half], change(mat[half:, half:], 1)], axis=1)
    return jnp.concatenate([upper, lower], axis=0)


def newton_inverse(mat):
    half = mat[0].shape[0] // 2
    eye = eye_mask(half)
    blocks = [
        [jnp.where(eye, part[:half, :half], 0.0), jnp.where(eye, part[half:, half:], 0.0)]
        for part in mat
    ]

    def inverse(diag):
        scale = 1.0 / (diag[0] * diag[0] + diag[1] * diag[1])
        return diag[0] * scale, -diag[1] * scale

    row = inverse(
        [jnp.concatenate([jnp.sum(b, axis=0, keepdims=True) for b in pair], axis=1) for pair in blocks]
    )
    col = inverse(
        [jnp.concatenate([jnp.sum(b, axis=1, keepdims=True) for b in pair], axis=0) for pair in blocks]
    )
    off = [on_diagonal(part, lambda block, n: jnp.where(eye, 0.0, block)) for part in mat]
    first = (off[0] * row[0] - off[1] * row[1], off[0] * row[1] + off[1] * row[0])
    fixed = prep(first)
    second = mul(fixed, fixed)
    third = mul(prep(second), fixed)
    real = second[0] - first[0] - third[0]
    imag = second[1] - first[1] - third[1]
    real = on_diagonal(real, lambda block, n: block + jnp.where(eye, 1.0, 0.0))
    return col[0] * real - col[1] * imag, col[0] * imag + col[1] * real


def load(ref):
    return ref[0], ref[1]


def store(ref, pair):
    ref[0] = pair[0]
    ref[1] = pair[1]


def kernel(
    cut, slabs, depth, e_local,
    shifts, weights, onsite, hop_in, couple, sigma_in, out,
    hop, sigma, outgoing, left, box_a, box_b, box_c, box_d, box_e, gathered, summed, mixed, total,
    mix, s_in,
    s_base, r_base, s_coup, r_coup, s_hcoup, r_hcoup, s_hgreen, r_hgreen,
    s_hop, r_hop, s_chain, r_chain, s_back, r_back, s_first, r_first,
    s_second, r_second, s_last, r_last,
):
    base = h_coup = h_adj = box_a
    coup = h_green = h_first = box_b
    green = h_chain = box_c
    chain = h_second = box_d
    full = box_e
    slab = lax.axis_index("slab")
    plane = lax.axis_index("energy")
    mom = lax.axis_index("mom")
    y, x = slab // ROW, lax.rem(slab, ROW)
    other = 1 - mom
    width = hop.shape[-1]
    share = width // depth
    span = width // PIECES
    half = width // 2
    near, far = 0, 2 * ROW
    in_far = jnp.where(slab >= cut, 1, 0)
    host_row = jnp.where(slab >= cut, far, near)
    is_near, is_far = y == 0, y == 2
    is_host = jnp.logical_or(is_near, is_far)
    is_main = jnp.logical_and(is_host, x // e_local == mom)
    is_helper = jnp.logical_and(is_host, x // e_local != mom)
    at_start = slab == 0
    offset = jnp.where(is_near, 0, cut)
    count = jnp.where(is_near, cut, slabs - cut)

    def send(src, dst, send_sem, recv_sem, **where):
        return pltpu.make_async_remote_copy(
            src_ref=src, dst_ref=dst, send_sem=send_sem, recv_sem=recv_sem,
            device_id=where, device_id_type=MESH,
        )

    def arrived(dst, recv_sem):
        send(dst, dst, s_hop.at[0], recv_sem, mom=other).wait_recv()

    hop_load = pltpu.make_async_copy(hop_in, hop, s_in.at[0])
    sigma_load = pltpu.make_async_copy(sigma_in, sigma, s_in.at[1])
    hop_load.start()
    sigma_load.start()
    barrier = pltpu.get_barrier_semaphore()

    def greet(**where):
        pl.semaphore_signal(barrier, inc=1, device_id=where, device_id_type=MESH)

    def hosted_here():
        return jnp.logical_and(is_host, y * ROW == host_row)

    greet(mom=other)
    for turn in range(1, depth):
        greet(energy=lax.rem(plane + turn, depth))
    for c in range(ROW):

        @pl.when(host_row + c != slab)
        def _():
            greet(slab=host_row + c, mom=c // e_local)

    @pl.when(is_host)
    def _():
        greet(slab=far - y * ROW + x)

    @pl.when(is_main)
    def _():
        def call(j, carry):
            @pl.when(offset + j != slab)
            def _():
                greet(slab=offset + j, mom=mom)
                greet(slab=offset + j, mom=other)

            return carry

        lax.fori_loop(0, count, call, 0)

    expected = depth + ROW - jnp.where(hosted_here(), 1, 0) + jnp.where(is_host, 1, 0)
    pl.semaphore_wait(barrier, expected + jnp.where(is_main, 2 * (count - 1), 0))
    hop_load.wait()
    sigma_load.wait()
    eye = eye_mask(half)
    place = slab - in_far * cut

    def host_of(e):
        return host_row + e_local * mom + e

    def base_copy(e):
        return send(outgoing.at[e], base.at[place], s_base.at[e], r_base.at[place], slab=host_of(e))

    def coup_copy(e):
        return send(couple, coup.at[place], s_coup.at[e], r_coup.at[place], slab=host_of(e))

    def is_remote(e):
        return host_of(e) != slab

    def sends_coup(e):
        return jnp.logical_and(is_remote(e), jnp.logical_not(at_start))

    own_coup = pltpu.make_async_copy(couple, coup.at[place], s_in.at[0])

    @pl.when(is_main)
    def _():
        own_coup.start()

    for e in range(e_local):
        level = -0.5 + ((plane * e_local + e).astype(jnp.float32) + 0.5) / (depth * e_local) - onsite[...]
        real = on_diagonal(
            -hop[0] - sigma[e, 0],
            lambda block, n: block + jnp.where(eye, level[:, n * half : (n + 1) * half], 0.0),
        )
        imag = on_diagonal(
            -hop[1] - sigma[e, 1], lambda block, n: block + jnp.where(eye, ETA, 0.0)
        )

        @pl.when(is_remote(e))
        def _():
            store(outgoing.at[e], (real, imag))
            base_copy(e).start()

        @pl.when(jnp.logical_not(is_remote(e)))
        def _():
            store(base.at[place], (real, imag))

    for e in range(e_local):

        @pl.when(sends_coup(e))
        def _():
            coup_copy(e).start()

    def fill(e, carry):
        def entry(f, inner):
            value = jnp.float32(0.0)
            for mode in range(shifts.shape[0]):
                value = value + jnp.where(f == e + shifts[mode], weights[0, mode], 0.0)
                value = value + jnp.where(f == e - shifts[mode], weights[1, mode], 0.0)
            mix[e, f] = value * 0.5
            return inner

        return lax.fori_loop(0, depth * e_local, entry, carry)

    lax.fori_loop(0, depth * e_local, fill, 0)

    @pl.when(is_main)
    def _():
        own_coup.wait()

    def hcoup_copy(j):
        return send(coup.at[j], h_coup.at[j], s_hcoup.at[j], r_hcoup.at[j], mom=other)

    def hgreen_copy(j):
        return send(green.at[j + 1], h_green.at[j], s_hgreen.at[j], r_hgreen.at[j], mom=other)

    def hop_copy():
        return send(green.at[cut], green.at[0], s_hop.at[0], r_hop.at[0], slab=slab + far)

    def chain_copy(j):
        return send(h_chain.at[j + 1], chain.at[j], s_chain.at[j], r_chain.at[j], mom=other)

    def back_copy():
        return send(h_chain.at[0], h_chain.at[cut], s_back.at[0], r_back.at[0], slab=slab - far)

    def piece(n):
        return pl.ds(pl.multiple_of(lax.rem(plane * PIECES // depth + 1 + n, PIECES) * span, 8), span)

    def first_copy(j, part, n):
        return send(
            full.at[j, part, piece(n)], gathered.at[x, piece(n)], s_first.at[j, part, n],
            r_first.at[x, n], slab=offset + j, mom=part,
        )

    def is_first(j):
        return jnp.logical_and(is_near, j == 0)

    def is_last(j):
        return jnp.logical_and(is_far, j == count - 1)

    def first_remote(j, part):
        return jnp.logical_or(offset + j != slab, part != mom)

    @pl.when(is_main)
    def _():
        @pl.when(is_far)
        def _():
            arrived(green.at[0], r_hop.at[0])

        def forward(j, carry):
            @pl.when(j != place)
            def _():
                arrived(base.at[j], r_base.at[j])

            @pl.when(is_first(j))
            def _():
                left[...] = jnp.zeros_like(left)

            @pl.when(jnp.logical_not(is_first(j)))
            def _():
                @pl.when(j != place)
                def _():
                    arrived(coup.at[j], r_coup.at[j])

                hcoup_copy(j).start()
                coupling = load(coup.at[j])
                half_way = mul(prep(load(green.at[j])), prep_adjoint(coupling))
                store(left, mul(prep(coupling), prep(half_way)))

            store(
                green.at[j + 1],
                newton_inverse((base[j, 0] - left[0], base[j, 1] - left[1])),
            )

            @pl.when(jnp.logical_not(is_first(j)))
            def _():
                hgreen_copy(j).start()

            return carry

        lax.fori_loop(0, count, forward, 0)

        @pl.when(is_near)
        def _():
            hop_copy().start()

        def backward(turn, carry):
            j = count - 1 - turn

            @pl.when(is_last(j))
            def _():
                full[j] = green[j + 1]

            @pl.when(jnp.logical_not(is_last(j)))
            def _():
                arrived(chain.at[j], r_chain.at[j])
                pair = load(green.at[j + 1])
                ready = prep(pair)
                extra = mul(prep(mul(ready, prep(load(chain.at[j])))), ready)
                store(full.at[j], (pair[0] + extra[0], pair[1] + extra[1]))

            for n in range(PIECES):
                for part in range(2):

                    @pl.when(first_remote(j, part))
                    def _():
                        first_copy(j, part, n).start()

            for part in range(2):

                @pl.when(jnp.logical_not(first_remote(j, part)))
                def _():
                    gathered[x] = full[j, part]

            return carry

        lax.fori_loop(0, count, backward, 0)

    @pl.when(is_helper)
    def _():
        def forward(j, carry):
            @pl.when(jnp.logical_not(is_first(j)))
            def _():
                arrived(h_coup.at[j], r_hcoup.at[j])
                coupling = load(h_coup.at[j])
                adjoint = (coupling[0].T, -coupling[1].T)
                ready_left, ready_right = prep(adjoint), prep(coupling)
                store(h_adj.at[j], adjoint)
                arrived(h_green.at[j], r_hgreen.at[j])
                ready = prep(load(h_green.at[j]))
                store(h_first.at[j], mul(ready_left, ready))
                store(h_second.at[j], mul(ready, ready_right))

            return carry

        lax.fori_loop(0, count, forward, 0)

        @pl.when(is_far)
        def _():
            h_chain[slabs - cut] = jnp.zeros_like(h_chain.at[slabs - cut])

        @pl.when(is_near)
        def _():
            arrived(h_chain.at[cut], r_back.at[0])

        def backward(turn, carry):
            j = count - 1 - turn

            @pl.when(jnp.logical_not(is_last(j)))
            def _():
                chain_copy(j).start()

            @pl.when(jnp.logical_not(is_first(j)))
            def _():
                extra = mul(prep(load(h_first.at[j])), prep(load(h_chain.at[j + 1])))
                adjoint = load(h_adj.at[j])
                sums = (adjoint[0] + extra[0], adjoint[1] + extra[1])
                store(h_chain.at[j], mul(prep(sums), prep(load(h_second.at[j]))))

            return carry

        lax.fori_loop(0, count, backward, 0)

        @pl.when(is_far)
        def _():
            back_copy().start()

    def second_copy(target):
        return send(
            summed.at[:, pl.ds(pl.multiple_of(target * share, 8), share)], mixed.at[plane],
            s_second.at[target], r_second.at[plane], energy=target,
        )

    local_first = jnp.logical_and(is_main, hosted_here())
    per = depth // PIECES
    for n in range(PIECES):
        for c in range(ROW):

            @pl.when(jnp.logical_or(c != x, jnp.logical_not(local_first)))
            def _():
                arrived(gathered.at[c, piece(n)], r_first.at[c, n])

        for e in range(e_local):
            summed[e, piece(n)] = gathered[e, piece(n)] + gathered[e_local + e, piece(n)]
        for k in range(per):
            target = lax.rem(plane * PIECES // depth + 1 + n, PIECES) * per + k

            @pl.when(target != plane)
            def _():
                second_copy(target).start()

    def mixing(source, start):
        values = [mixed[source, e] for e in range(e_local)]

        def row(e, carry):
            value = mix[e, source * e_local] * values[0]
            for k in range(1, e_local):
                value = value + mix[e, source * e_local + k] * values[k]
            if start:
                total[e] = value
            else:
                total[e] = total[e] + value
            return carry

        lax.fori_loop(0, depth * e_local, row, 0)

    mixed[plane] = summed[:, pl.ds(pl.multiple_of(plane * share, 8), share)]
    mixing(plane, True)
    reach = [turn for step in range(1, depth // 2 + 1) for turn in sorted({step, depth - step})]
    for turn in reach:
        source = lax.rem(plane + turn, depth)
        arrived(mixed.at[source], r_second.at[source])
        mixing(source, False)

    out[:, mom] = total[...]
    last_copy = send(total, out.at[:, mom], s_last.at[0], r_last.at[0], mom=other)
    last_copy.start()

    for e in range(e_local):

        @pl.when(is_remote(e))
        def _():
            base_copy(e).wait_send()

        @pl.when(sends_coup(e))
        def _():
            coup_copy(e).wait_send()

    @pl.when(is_main)
    def _():
        def drain(j, carry):
            @pl.when(jnp.logical_not(is_first(j)))
            def _():
                hcoup_copy(j).wait_send()
                hgreen_copy(j).wait_send()

            for part in range(2):

                @pl.when(first_remote(j, part))
                def _():
                    for n in range(PIECES):
                        first_copy(j, part, n).wait_send()

            return carry

        lax.fori_loop(0, count, drain, 0)

        @pl.when(is_near)
        def _():
            hop_copy().wait_send()

    @pl.when(is_helper)
    def _():
        def drain(j, carry):
            @pl.when(jnp.logical_not(is_last(j)))
            def _():
                chain_copy(j).wait_send()

            return carry

        lax.fori_loop(0, count, drain, 0)

        @pl.when(is_far)
        def _():
            back_copy().wait_send()

    for turn in range(1, depth):
        second_copy(lax.rem(plane + turn, depth)).wait_send()
    last_copy.wait_send()
    arrived(out.at[:, other], r_last.at[0])


def body(onsite, hop, couple, sigma_in, shifts, mode_weight):
    e_local = sigma_in.shape[0]
    width = onsite.shape[-1]
    slabs = lax.axis_size("slab")
    depth = lax.axis_size("energy")
    total = e_local * depth
    share = width // depth
    block = (2, width, width)
    slots = max(CUT, slabs - CUT)

    def buffer(*shape):
        return pltpu.VMEM(shape, jnp.float32)

    def sems(*shape):
        return pltpu.SemaphoreType.DMA(shape)

    vmem = pl.BlockSpec(memory_space=pltpu.VMEM)
    smem = pl.BlockSpec(memory_space=pltpu.SMEM)
    stay = pl.BlockSpec(memory_space=pl.ANY)
    result = pl.pallas_call(
        functools.partial(kernel, CUT, slabs, depth, e_local),
        out_shape=jax.ShapeDtypeStruct((total, 2, share, width), jnp.float32),
        in_specs=[smem, smem, vmem, stay, stay, stay],
        out_specs=vmem,
        scratch_shapes=[
            buffer(*block),
            buffer(e_local, *block),
            buffer(e_local, *block),
            buffer(*block),
            buffer(slots, *block),
            buffer(slots, *block),
            buffer(slots + 1, *block),
            buffer(slots, *block),
            buffer(slots, *block),
            buffer(ROW, width, width),
            buffer(e_local, width, width),
            buffer(depth, e_local, share, width),
            buffer(total, share, width),
            pltpu.SMEM((total, total), jnp.float32),
            sems(2),
            sems(e_local), sems(slots), sems(e_local), sems(slots),
            sems(slots), sems(slots), sems(slots), sems(slots),
            sems(1), sems(1), sems(slots), sems(slots), sems(1), sems(1),
            sems(slots, 2, PIECES), sems(ROW, PIECES), sems(depth), sems(depth), sems(1), sems(1),
        ],
        compiler_params=pltpu.CompilerParams(
            collective_id=0, has_side_effects=True, vmem_limit_bytes=50 << 20
        ),
    )(shifts, mode_weight, onsite[0], hop[0, 0], couple[0, 0], sigma_in[:, 0])
    return result[:, None]


def solution(mesh):
    in_specs = (
        P("mom", "slab", None),
        P("mom", "slab", None, None, None),
        P("mom", "slab", None, None, None),
        P("energy", "slab", None, None, None),
        P(),
        P(),
    )
    out_specs = P(None, "slab", None, "energy", None)
    return jax.shard_map(body, mesh=mesh, in_specs=in_specs, out_specs=out_specs, check_vma=False)
```

```python
import functools

import jax
import jax.numpy as jnp
from jax import lax
from jax.experimental import pallas as pl
from jax.experimental.pallas import tpu as pltpu
from jax.sharding import PartitionSpec as P

ETA = 0.5
ROW = 4
CUT = 6
BACK = 4
PIECES = 4
MESH = pl.DeviceIdType.MESH


def split(mat):
    top = mat.astype(jnp.bfloat16)
    return top, (mat - top.astype(jnp.float32)).astype(jnp.bfloat16)


def prep(pair):
    return split(pair[0]), split(pair[1]), split(pair[0] + pair[1])


def prep_adjoint(pair):
    return prep((pair[0].T, -pair[1].T))


def mul(left, right):
    outs = []
    for (left_top, left_low), (top, low) in zip(left, right):
        outs.append(
            jnp.dot(
                jnp.concatenate([left_top, left_top, left_low], axis=1),
                jnp.concatenate([top, low, top], axis=0),
                preferred_element_type=jnp.float32,
            )
        )
    return outs[0] - outs[1], outs[2] - (outs[0] + outs[1])


def eye_mask(size):
    shape = (size, size)
    return lax.broadcasted_iota(jnp.int32, shape, 0) == lax.broadcasted_iota(jnp.int32, shape, 1)


def on_diagonal(mat, change):
    half = mat.shape[0] // 2
    upper = jnp.concatenate([change(mat[:half, :half], 0), mat[:half, half:]], axis=1)
    lower = jnp.concatenate([mat[half:, :half], change(mat[half:, half:], 1)], axis=1)
    return jnp.concatenate([upper, lower], axis=0)


def newton_inverse(mat):
    half = mat[0].shape[0] // 2
    eye = eye_mask(half)
    blocks = [
        [jnp.where(eye, part[:half, :half], 0.0), jnp.where(eye, part[half:, half:], 0.0)]
        for part in mat
    ]

    def inverse(diag):
        scale = 1.0 / (diag[0] * diag[0] + diag[1] * diag[1])
        return diag[0] * scale, -diag[1] * scale

    row = inverse(
        [jnp.concatenate([jnp.sum(b, axis=0, keepdims=True) for b in pair], axis=1) for pair in blocks]
    )
    col = inverse(
        [jnp.concatenate([jnp.sum(b, axis=1, keepdims=True) for b in pair], axis=0) for pair in blocks]
    )
    off = [on_diagonal(part, lambda block, n: jnp.where(eye, 0.0, block)) for part in mat]
    first = (off[0] * row[0] - off[1] * row[1], off[0] * row[1] + off[1] * row[0])
    fixed = prep(first)
    second = mul(fixed, fixed)
    third = mul(prep(second), fixed)
    real = second[0] - first[0] - third[0]
    imag = second[1] - first[1] - third[1]
    real = on_diagonal(real, lambda block, n: block + jnp.where(eye, 1.0, 0.0))
    return col[0] * real - col[1] * imag, col[0] * imag + col[1] * real


def load(ref):
    return ref[0], ref[1]


def store(ref, pair):
    ref[0] = pair[0]
    ref[1] = pair[1]


def kernel(
    cut, turn_at, slabs, depth, e_local,
    shifts, weights, onsite, hop_in, couple, sigma_in, out,
    hop, sigma, outgoing, left, box_a, box_b, box_c, box_d, box_e, gathered, summed, mixed, total,
    mix, s_in,
    s_base, r_base, s_coup, r_coup, s_hcoup, r_hcoup, s_hgreen, r_hgreen,
    s_hop, r_hop, s_chain, r_chain, s_back, r_back, s_first, r_first,
    s_second, r_second, s_last, r_last, s_adopt, r_adopt, token,
):
    base = h_coup = h_adj = box_a
    coup = h_green = h_first = box_b
    green = h_chain = box_c
    chain = h_second = box_d
    full = box_e
    slab = lax.axis_index("slab")
    plane = lax.axis_index("energy")
    mom = lax.axis_index("mom")
    y, x = slab // ROW, lax.rem(slab, ROW)
    other = 1 - mom
    width = hop.shape[-1]
    share = width // depth
    span = width // PIECES
    half = width // 2
    near, far = 0, 2 * ROW
    in_far = jnp.where(slab >= cut, 1, 0)
    host_row = jnp.where(slab >= cut, far, near)
    adopt = cut - turn_at
    wide = slabs - turn_at
    is_near, is_far = y == 0, y == 2
    is_host = jnp.logical_or(is_near, is_far)
    is_main = jnp.logical_and(is_host, x // e_local == mom)
    is_helper = jnp.logical_and(is_host, x // e_local != mom)
    at_start = slab == 0
    offset = jnp.where(is_near, 0, turn_at)
    count = jnp.where(is_near, turn_at, wide)
    reach = jnp.where(is_near, cut, wide)

    def send(src, dst, send_sem, recv_sem, **where):
        return pltpu.make_async_remote_copy(
            src_ref=src, dst_ref=dst, send_sem=send_sem, recv_sem=recv_sem,
            device_id=where, device_id_type=MESH,
        )

    def arrived(dst, recv_sem):
        send(dst, dst, s_hop.at[0], recv_sem, mom=other).wait_recv()

    hop_load = pltpu.make_async_copy(hop_in, hop, s_in.at[0])
    sigma_load = pltpu.make_async_copy(sigma_in, sigma, s_in.at[1])
    hop_load.start()
    sigma_load.start()
    barrier = pltpu.get_barrier_semaphore()

    def greet(**where):
        pl.semaphore_signal(barrier, inc=1, device_id=where, device_id_type=MESH)

    greet(mom=other)
    for turn in range(1, depth):
        greet(energy=lax.rem(plane + turn, depth))
    for c in range(ROW):

        @pl.when(jnp.logical_and(slab < cut, near + c != slab))
        def _():
            greet(slab=near + c, mom=c // e_local)

        @pl.when(jnp.logical_and(slab >= turn_at, far + c != slab))
        def _():
            greet(slab=far + c, mom=c // e_local)

    @pl.when(is_host)
    def _():
        greet(slab=far - y * ROW + x)

    @pl.when(is_main)
    def _():
        def call(j, carry):
            @pl.when(offset + j != slab)
            def _():
                greet(slab=offset + j, mom=mom)
                greet(slab=offset + j, mom=other)

            return carry

        lax.fori_loop(0, reach, call, 0)

    expected = depth + ROW * (jnp.where(slab < cut, 1, 0) + jnp.where(slab >= turn_at, 1, 0))
    pl.semaphore_wait(barrier, expected + jnp.where(is_main, 2 * (reach - 1), 0))
    hop_load.wait()
    sigma_load.wait()
    eye = eye_mask(half)
    place = slab - in_far * turn_at

    def host_of(e):
        return host_row + e_local * mom + e

    def base_copy(e):
        return send(outgoing.at[e], base.at[place], s_base.at[e], r_base.at[place], slab=host_of(e))

    def coup_copy(e):
        return send(couple, coup.at[place], s_coup.at[e], r_coup.at[place], slab=host_of(e))

    def is_remote(e):
        return host_of(e) != slab

    def sends_coup(e):
        return jnp.logical_and(is_remote(e), jnp.logical_not(at_start))

    own_coup = pltpu.make_async_copy(couple, coup.at[place], s_in.at[0])

    @pl.when(is_main)
    def _():
        own_coup.start()

    for e in range(e_local):
        level = -0.5 + ((plane * e_local + e).astype(jnp.float32) + 0.5) / (depth * e_local) - onsite[...]
        real = on_diagonal(
            -hop[0] - sigma[e, 0],
            lambda block, n: block + jnp.where(eye, level[:, n * half : (n + 1) * half], 0.0),
        )
        imag = on_diagonal(
            -hop[1] - sigma[e, 1], lambda block, n: block + jnp.where(eye, ETA, 0.0)
        )

        @pl.when(is_remote(e))
        def _():
            store(outgoing.at[e], (real, imag))
            base_copy(e).start()

        @pl.when(jnp.logical_not(is_remote(e)))
        def _():
            store(base.at[place], (real, imag))

    for e in range(e_local):

        @pl.when(sends_coup(e))
        def _():
            coup_copy(e).start()

    def fill(e, carry):
        def entry(f, inner):
            value = jnp.float32(0.0)
            for mode in range(shifts.shape[0]):
                value = value + jnp.where(f == e + shifts[mode], weights[0, mode], 0.0)
                value = value + jnp.where(f == e - shifts[mode], weights[1, mode], 0.0)
            mix[e, f] = value * 0.5
            return inner

        return lax.fori_loop(0, depth * e_local, entry, carry)

    lax.fori_loop(0, depth * e_local, fill, 0)

    @pl.when(is_main)
    def _():
        own_coup.wait()

    def hcoup_copy(j):
        return send(coup.at[j], h_coup.at[j], s_hcoup.at[j], r_hcoup.at[j], mom=other)

    def hgreen_copy(j):
        return send(green.at[j + 1], h_green.at[j], s_hgreen.at[j], r_hgreen.at[j], mom=other)

    def hop_copy():
        return send(green.at[cut], green.at[adopt], s_hop.at[0], r_hop.at[0], slab=slab + far)

    def adopt_coup(a):
        return send(coup.at[turn_at + a], coup.at[a], s_adopt.at[a], r_coup.at[a], slab=slab + far)

    def adopt_green(a):
        return send(
            green.at[turn_at + a + 1], green.at[a + 1], s_adopt.at[adopt + a], r_adopt.at[a],
            slab=slab + far,
        )

    def used(j):
        return jnp.logical_and(
            jnp.logical_not(is_first(j)), jnp.logical_or(is_far, j < turn_at)
        )

    def held(j, part):
        late = offset + j >= slabs - ROW
        return jnp.logical_and(late, part == 1)

    def chain_copy(j):
        return send(h_chain.at[j + 1], chain.at[j], s_chain.at[j], r_chain.at[j], mom=other)

    def back_copy():
        return send(h_chain.at[0], h_chain.at[turn_at], s_back.at[0], r_back.at[0], slab=slab - far)

    def piece(n):
        return pl.ds(pl.multiple_of(lax.rem(plane * PIECES // depth + 1 + n, PIECES) * span, 8), span)

    def first_copy(j, part, n):
        return send(
            full.at[j, part, piece(n)], gathered.at[x, piece(n)], s_first.at[j, part, n],
            r_first.at[x, n], slab=offset + j, mom=part,
        )

    def is_first(j):
        return jnp.logical_and(is_near, j == 0)

    def is_last(j):
        return jnp.logical_and(is_far, j == count - 1)

    def first_remote(j, part):
        return jnp.logical_or(offset + j != slab, part != mom)

    @pl.when(is_main)
    def _():
        @pl.when(is_far)
        def _():
            arrived(green.at[adopt], r_hop.at[0])

        def forward(j, carry):
            @pl.when(j != place)
            def _():
                arrived(base.at[j], r_base.at[j])

            @pl.when(is_first(j))
            def _():
                left[...] = jnp.zeros_like(left)

            @pl.when(jnp.logical_not(is_first(j)))
            def _():
                @pl.when(j != place)
                def _():
                    arrived(coup.at[j], r_coup.at[j])

                @pl.when(used(j))
                def _():
                    hcoup_copy(j).start()

                coupling = load(coup.at[j])
                half_way = mul(prep(load(green.at[j])), prep_adjoint(coupling))
                store(left, mul(prep(coupling), prep(half_way)))

            store(
                green.at[j + 1],
                newton_inverse((base[j, 0] - left[0], base[j, 1] - left[1])),
            )

            @pl.when(used(j))
            def _():
                hgreen_copy(j).start()

            @pl.when(jnp.logical_and(is_far, j == wide - 3))
            def _():
                for a in range(adopt):
                    arrived(coup.at[a], r_coup.at[a])
                    if a < adopt - 1:
                        arrived(green.at[a + 1], r_adopt.at[a])
                    hcoup_copy(a).start()
                    hgreen_copy(a).start()

            return carry

        lax.fori_loop(jnp.where(is_near, 0, adopt), reach, forward, 0)

        @pl.when(is_near)
        def _():
            hop_copy().start()
            hop_copy().wait_send()
            for a in range(adopt):
                adopt_coup(a).start()
                if a < adopt - 1:
                    adopt_green(a).start()

        def backward(turn, carry):
            j = count - 1 - turn

            @pl.when(is_last(j))
            def _():
                full[j] = green[j + 1]

            @pl.when(jnp.logical_not(is_last(j)))
            def _():
                arrived(chain.at[j], r_chain.at[j])
                pair = load(green.at[j + 1])
                ready = prep(pair)
                extra = mul(prep(mul(ready, prep(load(chain.at[j])))), ready)
                store(full.at[j], (pair[0] + extra[0], pair[1] + extra[1]))

            for n in range(PIECES):
                for part in range(2):
                    now = jnp.logical_and(is_far, jnp.logical_not(held(j, part)))
                    if n == 0:
                        now = jnp.logical_or(is_near, now)

                    @pl.when(jnp.logical_and(first_remote(j, part), now))
                    def _():
                        first_copy(j, part, n).start()

            for part in range(2):

                @pl.when(jnp.logical_not(first_remote(j, part)))
                def _():
                    gathered[x] = full[j, part]

            return carry

        lax.fori_loop(0, count, backward, 0)

        @pl.when(is_near)
        def _():
            def sweep(n, act):
                def one(j, carry):
                    for part in range(2):

                        @pl.when(first_remote(j, part))
                        def _():
                            act(first_copy(j, part, n))

                    return carry

                lax.fori_loop(0, count, one, 0)

            for n in range(1, PIECES):
                sweep(n, lambda copy: copy.start())
                sweep(n - 1, lambda copy: copy.wait_send())
            sweep(PIECES - 1, lambda copy: copy.wait_send())

        @pl.when(is_far)
        def _():
            pl.semaphore_wait(token, 1)

            def release(j, carry):
                for part in range(2):

                    @pl.when(jnp.logical_and(first_remote(j, part), held(j, part)))
                    def _():
                        for n in range(PIECES):
                            first_copy(j, part, n).start()

                return carry

            lax.fori_loop(0, count, release, 0)

    @pl.when(is_helper)
    def _():
        def forward(step, carry):
            early = wide - 2 - adopt
            late = jnp.where(step < early + adopt, step - early, step)
            j = jnp.where(is_near, step, jnp.where(step < early, step + adopt, late))

            @pl.when(jnp.logical_not(is_first(j)))
            def _():
                arrived(h_coup.at[j], r_hcoup.at[j])
                coupling = load(h_coup.at[j])
                adjoint = (coupling[0].T, -coupling[1].T)
                ready_left, ready_right = prep(adjoint), prep(coupling)
                store(h_adj.at[j], adjoint)
                arrived(h_green.at[j], r_hgreen.at[j])
                ready = prep(load(h_green.at[j]))
                store(h_first.at[j], mul(ready_left, ready))
                store(h_second.at[j], mul(ready, ready_right))

            return carry

        lax.fori_loop(0, count, forward, 0)

        @pl.when(is_far)
        def _():
            h_chain[wide] = jnp.zeros_like(h_chain.at[wide])

        @pl.when(is_near)
        def _():
            arrived(h_chain.at[turn_at], r_back.at[0])

        def backward(turn, carry):
            j = count - 1 - turn

            @pl.when(jnp.logical_not(is_last(j)))
            def _():
                chain_copy(j).start()

            @pl.when(jnp.logical_not(is_first(j)))
            def _():
                extra = mul(prep(load(h_first.at[j])), prep(load(h_chain.at[j + 1])))
                adjoint = load(h_adj.at[j])
                sums = (adjoint[0] + extra[0], adjoint[1] + extra[1])
                store(h_chain.at[j], mul(prep(sums), prep(load(h_second.at[j]))))

            return carry

        lax.fori_loop(0, count, backward, 0)

        @pl.when(is_far)
        def _():
            back_copy().start()
            back_copy().wait_send()
            pl.semaphore_signal(token, inc=1, device_id={"mom": other}, device_id_type=MESH)

    def second_copy(target):
        return send(
            summed.at[:, pl.ds(pl.multiple_of(target * share, 8), share)], mixed.at[plane],
            s_second.at[target], r_second.at[plane], energy=target,
        )

    local_first = is_main
    per = depth // PIECES
    for n in range(PIECES):
        for c in range(ROW):

            @pl.when(jnp.logical_or(c != x, jnp.logical_not(local_first)))
            def _():
                arrived(gathered.at[c, piece(n)], r_first.at[c, n])

        for e in range(e_local):
            summed[e, piece(n)] = gathered[e, piece(n)] + gathered[e_local + e, piece(n)]
        for k in range(per):
            target = lax.rem(plane * PIECES // depth + 1 + n, PIECES) * per + k

            @pl.when(target != plane)
            def _():
                second_copy(target).start()

    def mixing(source, start):
        values = [mixed[source, e] for e in range(e_local)]

        def row(e, carry):
            value = mix[e, source * e_local] * values[0]
            for k in range(1, e_local):
                value = value + mix[e, source * e_local + k] * values[k]
            if start:
                total[e] = value
            else:
                total[e] = total[e] + value
            return carry

        lax.fori_loop(0, depth * e_local, row, 0)

    mixed[plane] = summed[:, pl.ds(pl.multiple_of(plane * share, 8), share)]
    mixing(plane, True)
    order = [turn for step in range(1, depth // 2 + 1) for turn in sorted({step, depth - step})]
    for turn in order:
        source = lax.rem(plane + turn, depth)
        arrived(mixed.at[source], r_second.at[source])
        mixing(source, False)

    out[:, mom] = total[...]
    last_copy = send(total, out.at[:, mom], s_last.at[0], r_last.at[0], mom=other)
    last_copy.start()

    for e in range(e_local):

        @pl.when(is_remote(e))
        def _():
            base_copy(e).wait_send()

        @pl.when(sends_coup(e))
        def _():
            coup_copy(e).wait_send()

    @pl.when(is_main)
    def _():
        def drain(j, carry):
            @pl.when(used(j))
            def _():
                hcoup_copy(j).wait_send()
                hgreen_copy(j).wait_send()

            for part in range(2):

                @pl.when(jnp.logical_and(is_far, first_remote(j, part)))
                def _():
                    for n in range(PIECES):
                        first_copy(j, part, n).wait_send()

            return carry

        lax.fori_loop(0, count, drain, 0)

        @pl.when(is_near)
        def _():
            for a in range(adopt):
                adopt_coup(a).wait_send()
                if a < adopt - 1:
                    adopt_green(a).wait_send()

    @pl.when(is_helper)
    def _():
        def drain(j, carry):
            @pl.when(jnp.logical_not(is_last(j)))
            def _():
                chain_copy(j).wait_send()

            return carry

        lax.fori_loop(0, count, drain, 0)

    for turn in range(1, depth):
        second_copy(lax.rem(plane + turn, depth)).wait_send()
    last_copy.wait_send()
    arrived(out.at[:, other], r_last.at[0])


def body(onsite, hop, couple, sigma_in, shifts, mode_weight):
    e_local = sigma_in.shape[0]
    width = onsite.shape[-1]
    slabs = lax.axis_size("slab")
    depth = lax.axis_size("energy")
    total = e_local * depth
    share = width // depth
    block = (2, width, width)
    slots = max(CUT, slabs - BACK)

    def buffer(*shape):
        return pltpu.VMEM(shape, jnp.float32)

    def sems(*shape):
        return pltpu.SemaphoreType.DMA(shape)

    vmem = pl.BlockSpec(memory_space=pltpu.VMEM)
    smem = pl.BlockSpec(memory_space=pltpu.SMEM)
    stay = pl.BlockSpec(memory_space=pltpu.HBM)
    result = pl.pallas_call(
        functools.partial(kernel, CUT, BACK, slabs, depth, e_local),
        out_shape=jax.ShapeDtypeStruct((total, 2, share, width), jnp.float32),
        in_specs=[smem, smem, vmem, stay, stay, stay],
        out_specs=vmem,
        scratch_shapes=[
            buffer(*block),
            buffer(e_local, *block),
            buffer(e_local, *block),
            buffer(*block),
            buffer(slots, *block),
            buffer(slots, *block),
            buffer(slots + 1, *block),
            buffer(slots, *block),
            buffer(slots, *block),
            buffer(ROW, width, width),
            buffer(e_local, width, width),
            buffer(depth, e_local, share, width),
            buffer(total, share, width),
            pltpu.SMEM((total, total), jnp.float32),
            sems(2),
            sems(e_local), sems(slots), sems(e_local), sems(slots),
            sems(slots), sems(slots), sems(slots), sems(slots),
            sems(1), sems(1), sems(slots), sems(slots), sems(1), sems(1),
            sems(slots, 2, PIECES), sems(ROW, PIECES), sems(depth), sems(depth), sems(1), sems(1),
            sems(2 * (CUT - BACK)), sems(CUT - BACK), pltpu.SemaphoreType.REGULAR,
        ],
        compiler_params=pltpu.CompilerParams(
            collective_id=0, has_side_effects=True, vmem_limit_bytes=50 << 20
        ),
    )(shifts, mode_weight, onsite[0], hop[0, 0], couple[0, 0], sigma_in[:, 0])
    return result[:, None]


def solution(mesh):
    in_specs = (
        P("mom", "slab", None),
        P("mom", "slab", None, None, None),
        P("mom", "slab", None, None, None),
        P("energy", "slab", None, None, None),
        P(),
        P(),
    )
    out_specs = P(None, "slab", None, "energy", None)
    return jax.shard_map(body, mesh=mesh, in_specs=in_specs, out_specs=out_specs, check_vma=False)
```

```python
import functools

import jax
import jax.numpy as jnp
from jax import lax
from jax.experimental import pallas as pl
from jax.experimental.pallas import tpu as pltpu
from jax.sharding import PartitionSpec as P

ETA = 0.5
ROW = 4
CUT = 6
BACK = 4
PIECES = 4
MESH = pl.DeviceIdType.MESH


def split(mat):
    top = mat.astype(jnp.bfloat16)
    return top, (mat - top.astype(jnp.float32)).astype(jnp.bfloat16)


def prep(pair):
    return split(pair[0]), split(pair[1]), split(pair[0] + pair[1])


def prep_adjoint(pair):
    return prep((pair[0].T, -pair[1].T))


def mul(left, right):
    outs = []
    for (left_top, left_low), (top, low) in zip(left, right):
        outs.append(
            jnp.dot(
                jnp.concatenate([left_top, left_top, left_low], axis=1),
                jnp.concatenate([top, low, top], axis=0),
                preferred_element_type=jnp.float32,
            )
        )
    return outs[0] - outs[1], outs[2] - (outs[0] + outs[1])


def eye_mask(size):
    shape = (size, size)
    return lax.broadcasted_iota(jnp.int32, shape, 0) == lax.broadcasted_iota(jnp.int32, shape, 1)


def on_diagonal(mat, change):
    half = mat.shape[0] // 2
    upper = jnp.concatenate([change(mat[:half, :half], 0), mat[:half, half:]], axis=1)
    lower = jnp.concatenate([mat[half:, :half], change(mat[half:, half:], 1)], axis=1)
    return jnp.concatenate([upper, lower], axis=0)


def newton_inverse(mat):
    half = mat[0].shape[0] // 2
    eye = eye_mask(half)
    blocks = [
        [jnp.where(eye, part[:half, :half], 0.0), jnp.where(eye, part[half:, half:], 0.0)]
        for part in mat
    ]

    def inverse(diag):
        scale = 1.0 / (diag[0] * diag[0] + diag[1] * diag[1])
        return diag[0] * scale, -diag[1] * scale

    row = inverse(
        [jnp.concatenate([jnp.sum(b, axis=0, keepdims=True) for b in pair], axis=1) for pair in blocks]
    )
    col = inverse(
        [jnp.concatenate([jnp.sum(b, axis=1, keepdims=True) for b in pair], axis=0) for pair in blocks]
    )
    off = [on_diagonal(part, lambda block, n: jnp.where(eye, 0.0, block)) for part in mat]
    first = (off[0] * row[0] - off[1] * row[1], off[0] * row[1] + off[1] * row[0])
    fixed = prep(first)
    second = mul(fixed, fixed)
    third = mul(prep(second), fixed)
    real = second[0] - first[0] - third[0]
    imag = second[1] - first[1] - third[1]
    real = on_diagonal(real, lambda block, n: block + jnp.where(eye, 1.0, 0.0))
    return col[0] * real - col[1] * imag, col[0] * imag + col[1] * real


def load(ref):
    return ref[0], ref[1]


def store(ref, pair):
    ref[0] = pair[0]
    ref[1] = pair[1]


def kernel(
    cut, turn_at, slabs, depth, e_local,
    shifts, weights, onsite, hop_in, couple, sigma_in, out,
    hop, sigma, outgoing, left, box_a, box_b, box_c, box_d, box_e, gathered, summed, mixed, total,
    mix, s_in,
    s_base, r_base, s_coup, r_coup, s_hcoup, r_hcoup, s_hgreen, r_hgreen,
    s_hop, r_hop, s_chain, r_chain, s_back, r_back, s_first, r_first,
    s_second, r_second, s_last, r_last, s_adopt, r_adopt, r_relay, token,
):
    base = h_coup = h_adj = box_a
    coup = h_green = h_first = box_b
    green = h_chain = box_c
    chain = h_second = box_d
    full = box_e
    slab = lax.axis_index("slab")
    plane = lax.axis_index("energy")
    mom = lax.axis_index("mom")
    y, x = slab // ROW, lax.rem(slab, ROW)
    other = 1 - mom
    width = hop.shape[-1]
    share = width // depth
    span = width // PIECES
    half = width // 2
    near, far = 0, 2 * ROW
    in_far = jnp.where(slab >= cut, 1, 0)
    host_row = jnp.where(slab >= cut, far, near)
    adopt = cut - turn_at
    wide = slabs - turn_at
    is_near, is_far = y == 0, y == 2
    is_host = jnp.logical_or(is_near, is_far)
    is_main = jnp.logical_and(is_host, x // e_local == mom)
    is_helper = jnp.logical_and(is_host, x // e_local != mom)
    at_start = slab == 0
    offset = jnp.where(is_near, 0, turn_at)
    count = jnp.where(is_near, turn_at, wide)
    reach = jnp.where(is_near, cut, wide)

    def send(src, dst, send_sem, recv_sem, **where):
        return pltpu.make_async_remote_copy(
            src_ref=src, dst_ref=dst, send_sem=send_sem, recv_sem=recv_sem,
            device_id=where, device_id_type=MESH,
        )

    def arrived(dst, recv_sem):
        send(dst, dst, s_hop.at[0], recv_sem, mom=other).wait_recv()

    hop_load = pltpu.make_async_copy(hop_in, hop, s_in.at[0])
    sigma_load = pltpu.make_async_copy(sigma_in, sigma, s_in.at[1])
    hop_load.start()
    sigma_load.start()
    barrier = pltpu.get_barrier_semaphore()

    def greet(**where):
        pl.semaphore_signal(barrier, inc=1, device_id=where, device_id_type=MESH)

    greet(mom=other)
    for turn in range(1, depth):
        greet(energy=lax.rem(plane + turn, depth))
    for c in range(ROW):

        @pl.when(jnp.logical_and(slab < cut, near + c != slab))
        def _():
            greet(slab=near + c, mom=c // e_local)

        @pl.when(jnp.logical_and(slab >= turn_at, far + c != slab))
        def _():
            greet(slab=far + c, mom=c // e_local)

    @pl.when(is_host)
    def _():
        greet(slab=far - y * ROW + x)

    @pl.when(jnp.logical_not(is_host))
    def _():
        for turn in range(1, ROW):
            greet(slab=y * ROW + lax.rem(x + turn, ROW))

    @pl.when(is_main)
    def _():
        def call(j, carry):
            @pl.when(offset + j != slab)
            def _():
                greet(slab=offset + j, mom=mom)
                greet(slab=offset + j, mom=other)

            return carry

        lax.fori_loop(0, reach, call, 0)

    expected = depth + ROW * (jnp.where(slab < cut, 1, 0) + jnp.where(slab >= turn_at, 1, 0))
    expected = expected + jnp.where(is_host, 0, ROW - 1)
    pl.semaphore_wait(barrier, expected + jnp.where(is_main, 2 * (reach - 1), 0))
    hop_load.wait()
    sigma_load.wait()
    eye = eye_mask(half)
    place = slab - in_far * turn_at

    def host_of(e):
        return host_row + e_local * mom + e

    def base_copy(e):
        return send(outgoing.at[e], base.at[place], s_base.at[e], r_base.at[place], slab=host_of(e))

    def coup_copy(e):
        return send(couple, coup.at[place], s_coup.at[e], r_coup.at[place], slab=host_of(e))

    def is_remote(e):
        return host_of(e) != slab

    def sends_coup(e):
        return jnp.logical_and(is_remote(e), jnp.logical_not(at_start))

    own_coup = pltpu.make_async_copy(couple, coup.at[place], s_in.at[0])

    @pl.when(is_main)
    def _():
        own_coup.start()

    for e in range(e_local):
        level = -0.5 + ((plane * e_local + e).astype(jnp.float32) + 0.5) / (depth * e_local) - onsite[...]
        real = on_diagonal(
            -hop[0] - sigma[e, 0],
            lambda block, n: block + jnp.where(eye, level[:, n * half : (n + 1) * half], 0.0),
        )
        imag = on_diagonal(
            -hop[1] - sigma[e, 1], lambda block, n: block + jnp.where(eye, ETA, 0.0)
        )

        @pl.when(is_remote(e))
        def _():
            store(outgoing.at[e], (real, imag))
            base_copy(e).start()

        @pl.when(jnp.logical_not(is_remote(e)))
        def _():
            store(base.at[place], (real, imag))

    for e in range(e_local):

        @pl.when(sends_coup(e))
        def _():
            coup_copy(e).start()

    def fill(e, carry):
        def entry(f, inner):
            value = jnp.float32(0.0)
            for mode in range(shifts.shape[0]):
                value = value + jnp.where(f == e + shifts[mode], weights[0, mode], 0.0)
                value = value + jnp.where(f == e - shifts[mode], weights[1, mode], 0.0)
            mix[e, f] = value * 0.5
            return inner

        return lax.fori_loop(0, depth * e_local, entry, carry)

    lax.fori_loop(0, depth * e_local, fill, 0)

    @pl.when(is_main)
    def _():
        own_coup.wait()

    def hcoup_copy(j):
        return send(coup.at[j], h_coup.at[j], s_hcoup.at[j], r_hcoup.at[j], mom=other)

    def hgreen_copy(j):
        return send(green.at[j + 1], h_green.at[j], s_hgreen.at[j], r_hgreen.at[j], mom=other)

    def hop_copy():
        return send(green.at[cut], green.at[adopt], s_hop.at[0], r_hop.at[0], slab=slab + far)

    def adopt_coup(a):
        return send(coup.at[turn_at + a], coup.at[a], s_adopt.at[a], r_coup.at[a], slab=slab + far)

    def adopt_green(a):
        return send(
            green.at[turn_at + a + 1], green.at[a + 1], s_adopt.at[adopt + a], r_adopt.at[a],
            slab=slab + far,
        )

    def used(j):
        return jnp.logical_and(
            jnp.logical_not(is_first(j)), jnp.logical_or(is_far, j < turn_at)
        )

    def held(j, part):
        late = offset + j >= slabs - ROW
        return jnp.logical_and(late, part == 1)

    def chain_copy(j):
        return send(h_chain.at[j + 1], chain.at[j], s_chain.at[j], r_chain.at[j], mom=other)

    def back_copy():
        return send(h_chain.at[0], h_chain.at[turn_at], s_back.at[0], r_back.at[0], slab=slab - far)

    def piece(n):
        return pl.ds(pl.multiple_of(lax.rem(plane * PIECES // depth + 1 + n, PIECES) * span, 8), span)

    def first_copy(j, part, n):
        return send(
            full.at[j, part, piece(n)], gathered.at[x, piece(n)], s_first.at[j, part, n],
            r_first.at[x, n], slab=offset + j, mom=part,
        )

    def relay_copy(j, part, side):
        where = pl.ds(side * half, half)
        return send(
            full.at[j, part, where], full.at[lax.rem(offset + j, ROW), part, where],
            s_first.at[j, part, side], r_relay.at[lax.rem(offset + j, ROW), side],
            slab=(offset + j) // ROW * ROW + x, mom=part,
        )

    def relayed(j):
        return jnp.logical_and(is_far, (offset + j) // ROW != 2)

    def pass_copy(r, part):
        where = pl.ds(part * span, span)
        order = lax.rem(part + 2 * PIECES - 1 - plane * PIECES // depth, PIECES)
        return send(
            full.at[r, mom, where], gathered.at[x, where], s_first.at[r, 0, part],
            r_first.at[x, order], slab=y * ROW + r,
        )

    def is_first(j):
        return jnp.logical_and(is_near, j == 0)

    def is_last(j):
        return jnp.logical_and(is_far, j == count - 1)

    def first_remote(j, part):
        return jnp.logical_or(offset + j != slab, part != mom)

    @pl.when(is_main)
    def _():
        @pl.when(is_far)
        def _():
            arrived(green.at[adopt], r_hop.at[0])

        def forward(j, carry):
            @pl.when(j != place)
            def _():
                arrived(base.at[j], r_base.at[j])

            @pl.when(is_first(j))
            def _():
                left[...] = jnp.zeros_like(left)

            @pl.when(jnp.logical_not(is_first(j)))
            def _():
                @pl.when(j != place)
                def _():
                    arrived(coup.at[j], r_coup.at[j])

                @pl.when(used(j))
                def _():
                    hcoup_copy(j).start()

                coupling = load(coup.at[j])
                half_way = mul(prep(load(green.at[j])), prep_adjoint(coupling))
                store(left, mul(prep(coupling), prep(half_way)))

            store(
                green.at[j + 1],
                newton_inverse((base[j, 0] - left[0], base[j, 1] - left[1])),
            )

            @pl.when(used(j))
            def _():
                hgreen_copy(j).start()

            @pl.when(jnp.logical_and(is_far, j == wide - 3))
            def _():
                for a in range(adopt):
                    arrived(coup.at[a], r_coup.at[a])
                    if a < adopt - 1:
                        arrived(green.at[a + 1], r_adopt.at[a])
                    hcoup_copy(a).start()
                    hgreen_copy(a).start()

            return carry

        lax.fori_loop(jnp.where(is_near, 0, adopt), reach, forward, 0)

        @pl.when(is_near)
        def _():
            hop_copy().start()
            hop_copy().wait_send()
            for a in range(adopt):
                adopt_coup(a).start()
                if a < adopt - 1:
                    adopt_green(a).start()

        def backward(turn, carry):
            j = count - 1 - turn

            @pl.when(is_last(j))
            def _():
                full[j] = green[j + 1]

            @pl.when(jnp.logical_not(is_last(j)))
            def _():
                arrived(chain.at[j], r_chain.at[j])
                pair = load(green.at[j + 1])
                ready = prep(pair)
                extra = mul(prep(mul(ready, prep(load(chain.at[j])))), ready)
                store(full.at[j], (pair[0] + extra[0], pair[1] + extra[1]))

            for n in range(PIECES):
                for part in range(2):
                    now = jnp.logical_and(is_far, jnp.logical_not(relayed(j)))
                    if n == 0:
                        now = jnp.logical_or(is_near, now)

                    @pl.when(jnp.logical_and(first_remote(j, part), now))
                    def _():
                        first_copy(j, part, n).start()

            for part in range(2):

                @pl.when(jnp.logical_and(relayed(j), jnp.logical_not(held(j, part))))
                def _():
                    for side in range(2):
                        relay_copy(j, part, side).start()

                @pl.when(jnp.logical_not(first_remote(j, part)))
                def _():
                    gathered[x] = full[j, part]

            return carry

        lax.fori_loop(0, count, backward, 0)

        @pl.when(is_near)
        def _():
            def sweep(n, act):
                def one(j, carry):
                    for part in range(2):

                        @pl.when(first_remote(j, part))
                        def _():
                            act(first_copy(j, part, n))

                    return carry

                lax.fori_loop(0, count, one, 0)

            for n in range(1, PIECES):
                sweep(n, lambda copy: copy.start())
                sweep(n - 1, lambda copy: copy.wait_send())
            sweep(PIECES - 1, lambda copy: copy.wait_send())

        @pl.when(is_far)
        def _():
            pl.semaphore_wait(token, 1)

            def release(j, carry):
                for part in range(2):

                    @pl.when(held(j, part))
                    def _():
                        for side in range(2):
                            relay_copy(j, part, side).start()

                return carry

            lax.fori_loop(0, count, release, 0)

    @pl.when(is_helper)
    def _():
        def forward(step, carry):
            early = wide - 2 - adopt
            late = jnp.where(step < early + adopt, step - early, step)
            j = jnp.where(is_near, step, jnp.where(step < early, step + adopt, late))

            @pl.when(jnp.logical_not(is_first(j)))
            def _():
                arrived(h_coup.at[j], r_hcoup.at[j])
                coupling = load(h_coup.at[j])
                adjoint = (coupling[0].T, -coupling[1].T)
                ready_left, ready_right = prep(adjoint), prep(coupling)
                store(h_adj.at[j], adjoint)
                arrived(h_green.at[j], r_hgreen.at[j])
                ready = prep(load(h_green.at[j]))
                store(h_first.at[j], mul(ready_left, ready))
                store(h_second.at[j], mul(ready, ready_right))

            return carry

        lax.fori_loop(0, count, forward, 0)

        @pl.when(is_far)
        def _():
            h_chain[wide] = jnp.zeros_like(h_chain.at[wide])

        @pl.when(is_near)
        def _():
            arrived(h_chain.at[turn_at], r_back.at[0])

        def backward(turn, carry):
            j = count - 1 - turn

            @pl.when(jnp.logical_not(is_last(j)))
            def _():
                chain_copy(j).start()

            @pl.when(jnp.logical_not(is_first(j)))
            def _():
                extra = mul(prep(load(h_first.at[j])), prep(load(h_chain.at[j + 1])))
                adjoint = load(h_adj.at[j])
                sums = (adjoint[0] + extra[0], adjoint[1] + extra[1])
                store(h_chain.at[j], mul(prep(sums), prep(load(h_second.at[j]))))

            return carry

        lax.fori_loop(0, count, backward, 0)

        @pl.when(is_far)
        def _():
            back_copy().start()
            back_copy().wait_send()
            pl.semaphore_signal(token, inc=1, device_id={"mom": other}, device_id_type=MESH)

    def second_copy(target):
        return send(
            summed.at[:, pl.ds(pl.multiple_of(target * share, 8), share)], mixed.at[plane],
            s_second.at[target], r_second.at[plane], energy=target,
        )

    @pl.when(jnp.logical_not(is_host))
    def _():
        def hand_on(turn, carry):
            r = ROW - 1 - turn
            for side in range(2):
                where = pl.ds(side * half, half)
                arrived(full.at[r, mom, where], r_relay.at[r, side])

                @pl.when(r != x)
                def _():
                    for part in range(side * PIECES // 2, (side + 1) * PIECES // 2):
                        pass_copy(r, part).start()

                @pl.when(r == x)
                def _():
                    gathered[x, where] = full[r, mom, where]

            return carry

        lax.fori_loop(0, ROW, hand_on, 0)

    local_first = jnp.logical_or(is_main, jnp.logical_not(is_host))
    per = depth // PIECES
    for n in range(PIECES):
        for c in range(ROW):

            @pl.when(jnp.logical_or(c != x, jnp.logical_not(local_first)))
            def _():
                arrived(gathered.at[c, piece(n)], r_first.at[c, n])

        for e in range(e_local):
            summed[e, piece(n)] = gathered[e, piece(n)] + gathered[e_local + e, piece(n)]
        for k in range(per):
            target = lax.rem(plane * PIECES // depth + 1 + n, PIECES) * per + k

            @pl.when(target != plane)
            def _():
                second_copy(target).start()

    def mixing(source, start):
        values = [mixed[source, e] for e in range(e_local)]

        for e in range(depth * e_local):
            value = mix[e, source * e_local] * values[0]
            for k in range(1, e_local):
                value = value + mix[e, source * e_local + k] * values[k]
            total[e] = value if start else total[e] + value

    mixed[plane] = summed[:, pl.ds(pl.multiple_of(plane * share, 8), share)]
    mixing(plane, True)
    order = [turn for step in range(1, depth // 2 + 1) for turn in sorted({step, depth - step})]
    for turn in order:
        source = lax.rem(plane + turn, depth)
        arrived(mixed.at[source], r_second.at[source])
        mixing(source, False)

    out[:, mom] = total[...]
    last_copy = send(total, out.at[:, mom], s_last.at[0], r_last.at[0], mom=other)
    last_copy.start()

    for e in range(e_local):

        @pl.when(is_remote(e))
        def _():
            base_copy(e).wait_send()

        @pl.when(sends_coup(e))
        def _():
            coup_copy(e).wait_send()

    @pl.when(is_main)
    def _():
        def drain(j, carry):
            @pl.when(used(j))
            def _():
                hcoup_copy(j).wait_send()
                hgreen_copy(j).wait_send()

            for part in range(2):

                direct = jnp.logical_and(is_far, jnp.logical_not(relayed(j)))

                @pl.when(jnp.logical_and(direct, first_remote(j, part)))
                def _():
                    for n in range(PIECES):
                        first_copy(j, part, n).wait_send()

                @pl.when(relayed(j))
                def _():
                    for side in range(2):
                        relay_copy(j, part, side).wait_send()

            return carry

        lax.fori_loop(0, count, drain, 0)

        @pl.when(is_near)
        def _():
            for a in range(adopt):
                adopt_coup(a).wait_send()
                if a < adopt - 1:
                    adopt_green(a).wait_send()

    @pl.when(jnp.logical_not(is_host))
    def _():
        for r in range(ROW):

            @pl.when(r != x)
            def _():
                for part in range(PIECES):
                    pass_copy(r, part).wait_send()

    @pl.when(is_helper)
    def _():
        def drain(j, carry):
            @pl.when(jnp.logical_not(is_last(j)))
            def _():
                chain_copy(j).wait_send()

            return carry

        lax.fori_loop(0, count, drain, 0)

    for turn in range(1, depth):
        second_copy(lax.rem(plane + turn, depth)).wait_send()
    last_copy.wait_send()
    arrived(out.at[:, other], r_last.at[0])


def body(onsite, hop, couple, sigma_in, shifts, mode_weight):
    e_local = sigma_in.shape[0]
    width = onsite.shape[-1]
    slabs = lax.axis_size("slab")
    depth = lax.axis_size("energy")
    total = e_local * depth
    share = width // depth
    block = (2, width, width)
    slots = max(CUT, slabs - BACK)

    def buffer(*shape):
        return pltpu.VMEM(shape, jnp.float32)

    def sems(*shape):
        return pltpu.SemaphoreType.DMA(shape)

    vmem = pl.BlockSpec(memory_space=pltpu.VMEM)
    smem = pl.BlockSpec(memory_space=pltpu.SMEM)
    stay = pl.BlockSpec(memory_space=pltpu.HBM)
    result = pl.pallas_call(
        functools.partial(kernel, CUT, BACK, slabs, depth, e_local),
        out_shape=jax.ShapeDtypeStruct((total, 2, share, width), jnp.float32),
        in_specs=[smem, smem, vmem, stay, stay, stay],
        out_specs=vmem,
        scratch_shapes=[
            buffer(*block),
            buffer(e_local, *block),
            buffer(e_local, *block),
            buffer(*block),
            buffer(slots, *block),
            buffer(slots, *block),
            buffer(slots + 1, *block),
            buffer(slots, *block),
            buffer(slots, *block),
            buffer(ROW, width, width),
            buffer(e_local, width, width),
            buffer(depth, e_local, share, width),
            buffer(total, share, width),
            pltpu.SMEM((total, total), jnp.float32),
            sems(2),
            sems(e_local), sems(slots), sems(e_local), sems(slots),
            sems(slots), sems(slots), sems(slots), sems(slots),
            sems(1), sems(1), sems(slots), sems(slots), sems(1), sems(1),
            sems(slots, 2, PIECES), sems(ROW, PIECES), sems(depth), sems(depth), sems(1), sems(1),
            sems(2 * (CUT - BACK)), sems(CUT - BACK), sems(ROW, 2), pltpu.SemaphoreType.REGULAR,
        ],
        compiler_params=pltpu.CompilerParams(
            collective_id=0, has_side_effects=True, vmem_limit_bytes=56 << 20
        ),
    )(shifts, mode_weight, onsite[0], hop[0, 0], couple[0, 0], sigma_in[:, 0])
    return result[:, None]


def solution(mesh):
    in_specs = (
        P("mom", "slab", None),
        P("mom", "slab", None, None, None),
        P("mom", "slab", None, None, None),
        P("energy", "slab", None, None, None),
        P(),
        P(),
    )
    out_specs = P(None, "slab", None, "energy", None)
    return jax.shard_map(body, mesh=mesh, in_specs=in_specs, out_specs=out_specs, check_vma=False)
```

```python
import functools

import jax
import jax.numpy as jnp
from jax import lax
from jax.experimental import pallas as pl
from jax.experimental.pallas import tpu as pltpu
from jax.sharding import PartitionSpec as P

ETA = 0.5
ROW = 4
CUT = 6
BACK = 5
PIECES = 4
MESH = pl.DeviceIdType.MESH


def split(mat):
    top = mat.astype(jnp.bfloat16)
    return top, (mat - top.astype(jnp.float32)).astype(jnp.bfloat16)


def prep(pair):
    return split(pair[0]), split(pair[1]), split(pair[0] + pair[1])


def prep_adjoint(pair):
    return prep((pair[0].T, -pair[1].T))


def mul(left, right):
    outs = []
    for (left_top, left_low), (top, low) in zip(left, right):
        outs.append(
            jnp.dot(
                jnp.concatenate([left_top, left_top, left_low], axis=1),
                jnp.concatenate([top, low, top], axis=0),
                preferred_element_type=jnp.float32,
            )
        )
    return outs[0] - outs[1], outs[2] - (outs[0] + outs[1])


def eye_mask(size):
    shape = (size, size)
    return lax.broadcasted_iota(jnp.int32, shape, 0) == lax.broadcasted_iota(jnp.int32, shape, 1)


def on_diagonal(mat, change):
    half = mat.shape[0] // 2
    upper = jnp.concatenate([change(mat[:half, :half], 0), mat[:half, half:]], axis=1)
    lower = jnp.concatenate([mat[half:, :half], change(mat[half:, half:], 1)], axis=1)
    return jnp.concatenate([upper, lower], axis=0)


def newton_inverse(mat):
    half = mat[0].shape[0] // 2
    eye = eye_mask(half)
    blocks = [
        [jnp.where(eye, part[:half, :half], 0.0), jnp.where(eye, part[half:, half:], 0.0)]
        for part in mat
    ]

    def inverse(diag):
        scale = 1.0 / (diag[0] * diag[0] + diag[1] * diag[1])
        return diag[0] * scale, -diag[1] * scale

    row = inverse(
        [jnp.concatenate([jnp.sum(b, axis=0, keepdims=True) for b in pair], axis=1) for pair in blocks]
    )
    col = inverse(
        [jnp.concatenate([jnp.sum(b, axis=1, keepdims=True) for b in pair], axis=0) for pair in blocks]
    )
    off = [on_diagonal(part, lambda block, n: jnp.where(eye, 0.0, block)) for part in mat]
    first = (off[0] * row[0] - off[1] * row[1], off[0] * row[1] + off[1] * row[0])
    fixed = prep(first)
    second = mul(fixed, fixed)
    third = mul(prep(second), fixed)
    real = second[0] - first[0] - third[0]
    imag = second[1] - first[1] - third[1]
    real = on_diagonal(real, lambda block, n: block + jnp.where(eye, 1.0, 0.0))
    return col[0] * real - col[1] * imag, col[0] * imag + col[1] * real


def load(ref):
    return ref[0], ref[1]


def store(ref, pair):
    ref[0] = pair[0]
    ref[1] = pair[1]


def kernel(
    cut, turn_at, slabs, depth, e_local,
    shifts, weights, onsite, hop_in, couple, sigma_in, out,
    hop, sigma, outgoing, left, box_a, box_b, box_c, box_d, box_e, gathered, summed, mixed, total,
    mix, s_in,
    s_base, r_base, s_coup, r_coup, s_hcoup, r_hcoup, s_hgreen, r_hgreen,
    s_hop, r_hop, s_chain, r_chain, s_back, r_back, s_first, r_first,
    s_second, r_second, s_last, r_last, s_adopt, r_adopt, r_relay, s_detour, r_detour, token,
):
    base = h_coup = h_adj = box_a
    coup = h_green = h_first = box_b
    green = h_chain = box_c
    chain = h_second = box_d
    full = box_e
    slab = lax.axis_index("slab")
    plane = lax.axis_index("energy")
    mom = lax.axis_index("mom")
    y, x = slab // ROW, lax.rem(slab, ROW)
    other = 1 - mom
    width = hop.shape[-1]
    share = width // depth
    span = width // PIECES
    half = width // 2
    near, far = 0, 2 * ROW
    in_far = jnp.where(slab >= cut, 1, 0)
    host_row = jnp.where(slab >= cut, far, near)
    adopt = cut - turn_at
    wide = slabs - turn_at
    is_near, is_far = y == 0, y == 2
    is_host = jnp.logical_or(is_near, is_far)
    is_main = jnp.logical_and(is_host, x // e_local == mom)
    is_helper = jnp.logical_and(is_host, x // e_local != mom)
    at_start = slab == 0
    offset = jnp.where(is_near, 0, turn_at)
    count = jnp.where(is_near, turn_at, wide)
    reach = jnp.where(is_near, cut, wide)

    def send(src, dst, send_sem, recv_sem, **where):
        return pltpu.make_async_remote_copy(
            src_ref=src, dst_ref=dst, send_sem=send_sem, recv_sem=recv_sem,
            device_id=where, device_id_type=MESH,
        )

    def arrived(dst, recv_sem):
        send(dst, dst, s_hop.at[0], recv_sem, mom=other).wait_recv()

    hop_load = pltpu.make_async_copy(hop_in, hop, s_in.at[0])
    sigma_load = pltpu.make_async_copy(sigma_in, sigma, s_in.at[1])
    hop_load.start()
    sigma_load.start()
    barrier = pltpu.get_barrier_semaphore()

    def greet(**where):
        pl.semaphore_signal(barrier, inc=1, device_id=where, device_id_type=MESH)

    in_upper, in_lower = slab < 2 * ROW, slab >= ROW
    opposite = lax.rem(x + 2, ROW)
    is_detour = opposite // e_local == mom
    is_relay = jnp.logical_and(y == 3, is_detour)
    starts_detour = jnp.logical_and(y == 0, is_detour)
    members = jnp.where(is_near, 2 * ROW, slabs - ROW)
    first_member = jnp.where(is_near, 0, ROW)
    greet(mom=other)
    for turn in range(1, depth):
        greet(energy=lax.rem(plane + turn, depth))
    for c in range(ROW):

        @pl.when(jnp.logical_and(in_upper, near + c != slab))
        def _():
            greet(slab=near + c, mom=c // e_local)

        @pl.when(jnp.logical_and(in_lower, far + c != slab))
        def _():
            greet(slab=far + c, mom=c // e_local)

    @pl.when(is_host)
    def _():
        greet(slab=far - y * ROW + x)

    @pl.when(jnp.logical_not(is_host))
    def _():
        for turn in range(1, ROW):
            greet(slab=y * ROW + lax.rem(x + turn, ROW))

    @pl.when(is_main)
    def _():
        def call(j, carry):
            @pl.when(first_member + j != slab)
            def _():
                greet(slab=first_member + j, mom=mom)
                greet(slab=first_member + j, mom=other)

            return carry

        lax.fori_loop(0, members, call, 0)

        @pl.when(is_near)
        def _():
            greet(slab=3 * ROW + opposite)

    @pl.when(starts_detour)
    def _():
        greet(slab=3 * ROW + x)

    @pl.when(is_relay)
    def _():
        greet(slab=x)
        greet(slab=opposite)

    expected = depth + ROW * (jnp.where(in_upper, 1, 0) + jnp.where(in_lower, 1, 0))
    expected = expected + jnp.where(is_host, 0, ROW - 1)
    expected = expected + jnp.where(jnp.logical_and(is_main, is_near), 1, 0)
    expected = expected + jnp.where(starts_detour, 1, 0) + jnp.where(is_relay, 2, 0)
    pl.semaphore_wait(barrier, expected + jnp.where(is_main, 2 * (members - 1), 0))
    hop_load.wait()
    sigma_load.wait()
    eye = eye_mask(half)
    place = slab - in_far * turn_at

    def host_of(e):
        return host_row + e_local * mom + e

    def base_copy(e):
        return send(outgoing.at[e], base.at[place], s_base.at[e], r_base.at[place], slab=host_of(e))

    def coup_copy(e):
        return send(couple, coup.at[place], s_coup.at[e], r_coup.at[place], slab=host_of(e))

    def is_remote(e):
        return host_of(e) != slab

    def detours(e):
        return jnp.logical_and(y == 0, host_of(e) == opposite)

    def straight(e):
        return jnp.logical_and(is_remote(e), jnp.logical_not(detours(e)))

    def sends_coup(e):
        return jnp.logical_and(straight(e), jnp.logical_not(at_start))

    def detour_copy(src, q):
        return send(
            src, box_a.at[q // 2, q % 2], s_detour.at[q], r_detour.at[q], slab=slab + 3 * ROW
        )

    def pass_in(q):
        target, sem = (base, r_base) if q < 2 else (coup, r_coup)
        return send(
            box_a.at[q // 2, q % 2], target.at[x, q % 2], s_detour.at[q], sem.at[x], slab=opposite
        )

    has_coup = x != 0

    own_coup = pltpu.make_async_copy(couple, coup.at[place], s_in.at[0])

    @pl.when(is_main)
    def _():
        own_coup.start()

    for e in range(e_local):
        level = -0.5 + ((plane * e_local + e).astype(jnp.float32) + 0.5) / (depth * e_local) - onsite[...]
        real = on_diagonal(
            -hop[0] - sigma[e, 0],
            lambda block, n: block + jnp.where(eye, level[:, n * half : (n + 1) * half], 0.0),
        )
        imag = on_diagonal(
            -hop[1] - sigma[e, 1], lambda block, n: block + jnp.where(eye, ETA, 0.0)
        )

        @pl.when(is_remote(e))
        def _():
            store(outgoing.at[e], (real, imag))

        @pl.when(jnp.logical_and(straight(e), jnp.logical_not(is_relay)))
        def _():
            base_copy(e).start()

        @pl.when(detours(e))
        def _():
            for part in range(2):
                detour_copy(outgoing.at[e, part], part).start()

        @pl.when(jnp.logical_not(is_remote(e)))
        def _():
            store(base.at[place], (real, imag))

    for e in range(e_local):

        @pl.when(jnp.logical_and(sends_coup(e), jnp.logical_not(is_relay)))
        def _():
            coup_copy(e).start()

        @pl.when(jnp.logical_and(detours(e), has_coup))
        def _():
            for part in range(2):
                detour_copy(couple.at[part], 2 + part).start()

    @pl.when(is_relay)
    def _():
        for q in range(4):

            @pl.when(jnp.logical_or(q < 2, has_coup))
            def _():
                arrived(box_a.at[q // 2, q % 2], r_detour.at[q])
                pass_in(q).start()

        for e in range(e_local):
            base_copy(e).start()
        for e in range(e_local):
            coup_copy(e).start()

    def fill(e, carry):
        def entry(f, inner):
            value = jnp.float32(0.0)
            for mode in range(shifts.shape[0]):
                value = value + jnp.where(f == e + shifts[mode], weights[0, mode], 0.0)
                value = value + jnp.where(f == e - shifts[mode], weights[1, mode], 0.0)
            mix[e, f] = value
            return inner

        return lax.fori_loop(0, depth * e_local, entry, carry)

    lax.fori_loop(0, depth * e_local, fill, 0)

    @pl.when(is_main)
    def _():
        own_coup.wait()

    def hcoup_copy(j):
        return send(coup.at[j], h_coup.at[j], s_hcoup.at[j], r_hcoup.at[j], mom=other)

    def hgreen_copy(j):
        return send(green.at[j + 1], h_green.at[j], s_hgreen.at[j], r_hgreen.at[j], mom=other)

    def hop_copy():
        return send(green.at[cut], green.at[adopt], s_hop.at[0], r_hop.at[0], slab=slab + far)

    def adopt_coup(a):
        return send(coup.at[turn_at + a], coup.at[a], s_adopt.at[a], r_coup.at[a], slab=slab + far)

    def adopt_green(a):
        return send(
            green.at[turn_at + a + 1], green.at[a + 1], s_adopt.at[adopt + a], r_adopt.at[a],
            slab=slab + far,
        )

    def used(j):
        return jnp.logical_and(
            jnp.logical_not(is_first(j)), jnp.logical_or(is_far, j < turn_at)
        )

    def held(j, part):
        late = offset + j >= slabs - ROW
        return jnp.logical_and(late, part == 1)

    def chain_copy(j):
        return send(h_chain.at[j + 1], chain.at[j], s_chain.at[j], r_chain.at[j], mom=other)

    def back_copy():
        return send(h_chain.at[0], h_chain.at[turn_at], s_back.at[0], r_back.at[0], slab=slab - far)

    def piece(n):
        return pl.ds(pl.multiple_of(lax.rem(plane * PIECES // depth + 1 + n, PIECES) * span, 8), span)

    def first_copy(j, part, n):
        return send(
            full.at[j, part, piece(n)], gathered.at[x, piece(n)], s_first.at[j, part, n],
            r_first.at[x, n], slab=offset + j, mom=part,
        )

    def relay_copy(j, part, side):
        where = pl.ds(side * half, half)
        return send(
            full.at[j, part, where], full.at[lax.rem(offset + j, ROW), part, where],
            s_first.at[j, part, side], r_relay.at[lax.rem(offset + j, ROW), side],
            slab=(offset + j) // ROW * ROW + x, mom=part,
        )

    def relayed(j):
        return (offset + j) // ROW != y

    def pass_copy(r, part):
        where = pl.ds(part * span, span)
        order = lax.rem(part + 2 * PIECES - 1 - plane * PIECES // depth, PIECES)
        return send(
            full.at[r, mom, where], gathered.at[x, where], s_first.at[r, 0, part],
            r_first.at[x, order], slab=y * ROW + r,
        )

    def is_first(j):
        return jnp.logical_and(is_near, j == 0)

    def is_last(j):
        return jnp.logical_and(is_far, j == count - 1)

    def first_remote(j, part):
        return jnp.logical_or(offset + j != slab, part != mom)

    @pl.when(is_main)
    def _():
        @pl.when(is_far)
        def _():
            arrived(green.at[adopt], r_hop.at[0])

        def forward(j, carry):
            @pl.when(j != place)
            def _():
                arrived(base.at[j], r_base.at[j])

            @pl.when(is_first(j))
            def _():
                left[...] = jnp.zeros_like(left)

            @pl.when(jnp.logical_not(is_first(j)))
            def _():
                @pl.when(j != place)
                def _():
                    arrived(coup.at[j], r_coup.at[j])

                @pl.when(used(j))
                def _():
                    hcoup_copy(j).start()

                coupling = load(coup.at[j])
                half_way = mul(prep(load(green.at[j])), prep_adjoint(coupling))
                store(left, mul(prep(coupling), prep(half_way)))

            store(
                green.at[j + 1],
                newton_inverse((base[j, 0] - left[0], base[j, 1] - left[1])),
            )

            @pl.when(used(j))
            def _():
                hgreen_copy(j).start()

            @pl.when(jnp.logical_and(is_far, j == wide - 3))
            def _():
                for a in range(adopt):
                    arrived(coup.at[a], r_coup.at[a])
                    if a < adopt - 1:
                        arrived(green.at[a + 1], r_adopt.at[a])
                    hcoup_copy(a).start()
                    hgreen_copy(a).start()

            return carry

        lax.fori_loop(jnp.where(is_near, 0, adopt), reach, forward, 0)

        @pl.when(is_near)
        def _():
            hop_copy().start()
            hop_copy().wait_send()
            for a in range(adopt):
                adopt_coup(a).start()
                if a < adopt - 1:
                    adopt_green(a).start()

        def backward(turn, carry):
            j = count - 1 - turn

            @pl.when(is_last(j))
            def _():
                full[j] = green[j + 1]

            @pl.when(jnp.logical_not(is_last(j)))
            def _():
                arrived(chain.at[j], r_chain.at[j])
                pair = load(green.at[j + 1])
                ready = prep(pair)
                extra = mul(prep(mul(ready, prep(load(chain.at[j])))), ready)
                store(full.at[j], (pair[0] + extra[0], pair[1] + extra[1]))

            for n in range(PIECES):
                for part in range(2):
                    now = jnp.logical_and(is_far, jnp.logical_not(relayed(j)))
                    if n == 0:
                        now = jnp.logical_or(jnp.logical_and(is_near, jnp.logical_not(relayed(j))), now)

                    @pl.when(jnp.logical_and(first_remote(j, part), now))
                    def _():
                        first_copy(j, part, n).start()

            for part in range(2):

                @pl.when(jnp.logical_and(relayed(j), jnp.logical_not(held(j, part))))
                def _():
                    for side in range(2):
                        relay_copy(j, part, side).start()

                @pl.when(jnp.logical_not(first_remote(j, part)))
                def _():
                    gathered[x] = full[j, part]

            return carry

        lax.fori_loop(0, count, backward, 0)

        @pl.when(is_near)
        def _():
            def sweep(n, act):
                def one(j, carry):
                    for part in range(2):

                        @pl.when(jnp.logical_and(first_remote(j, part), jnp.logical_not(relayed(j))))
                        def _():
                            act(first_copy(j, part, n))

                    return carry

                lax.fori_loop(0, count, one, 0)

            for n in range(1, PIECES):
                sweep(n, lambda copy: copy.start())
                sweep(n - 1, lambda copy: copy.wait_send())
            sweep(PIECES - 1, lambda copy: copy.wait_send())

        @pl.when(is_far)
        def _():
            pl.semaphore_wait(token, 1)

            def release(j, carry):
                for part in range(2):

                    @pl.when(held(j, part))
                    def _():
                        for side in range(2):
                            relay_copy(j, part, side).start()

                return carry

            lax.fori_loop(0, count, release, 0)

    @pl.when(is_helper)
    def _():
        def forward(step, carry):
            early = wide - 2 - adopt
            late = jnp.where(step < early + adopt, step - early, step)
            j = jnp.where(is_near, step, jnp.where(step < early, step + adopt, late))

            @pl.when(jnp.logical_not(is_first(j)))
            def _():
                arrived(h_coup.at[j], r_hcoup.at[j])
                coupling = load(h_coup.at[j])
                adjoint = (coupling[0].T, -coupling[1].T)
                ready_left, ready_right = prep(adjoint), prep(coupling)
                store(h_adj.at[j], adjoint)
                arrived(h_green.at[j], r_hgreen.at[j])
                ready = prep(load(h_green.at[j]))
                store(h_first.at[j], mul(ready_left, ready))
                store(h_second.at[j], mul(ready, ready_right))

            return carry

        lax.fori_loop(0, count, forward, 0)

        @pl.when(is_far)
        def _():
            h_chain[wide] = jnp.zeros_like(h_chain.at[wide])

        @pl.when(is_near)
        def _():
            arrived(h_chain.at[turn_at], r_back.at[0])

        def backward(turn, carry):
            j = count - 1 - turn

            @pl.when(jnp.logical_not(is_last(j)))
            def _():
                chain_copy(j).start()

            @pl.when(jnp.logical_not(is_first(j)))
            def _():
                extra = mul(prep(load(h_first.at[j])), prep(load(h_chain.at[j + 1])))
                adjoint = load(h_adj.at[j])
                sums = (adjoint[0] + extra[0], adjoint[1] + extra[1])
                store(h_chain.at[j], mul(prep(sums), prep(load(h_second.at[j]))))

            return carry

        lax.fori_loop(0, count, backward, 0)

        @pl.when(is_far)
        def _():
            back_copy().start()
            back_copy().wait_send()
            pl.semaphore_signal(token, inc=1, device_id={"mom": other}, device_id_type=MESH)

    def second_copy(target):
        return send(
            summed.at[:, pl.ds(pl.multiple_of(target * share, 8), share)], mixed.at[plane],
            s_second.at[target], r_second.at[plane], energy=target,
        )

    @pl.when(jnp.logical_not(is_host))
    def _():
        def hand_on(turn, carry):
            r = ROW - 1 - turn
            for side in range(2):
                where = pl.ds(side * half, half)
                arrived(full.at[r, mom, where], r_relay.at[r, side])

                @pl.when(r != x)
                def _():
                    for part in range(side * PIECES // 2, (side + 1) * PIECES // 2):
                        pass_copy(r, part).start()

                @pl.when(r == x)
                def _():
                    gathered[x, where] = full[r, mom, where]

            return carry

        lax.fori_loop(0, ROW, hand_on, 0)

    local_first = jnp.logical_or(is_main, jnp.logical_not(is_host))
    per = depth // PIECES
    for n in range(PIECES):
        for c in range(ROW):

            @pl.when(jnp.logical_or(c != x, jnp.logical_not(local_first)))
            def _():
                arrived(gathered.at[c, piece(n)], r_first.at[c, n])

        for e in range(e_local):
            summed[e, piece(n)] = gathered[e, piece(n)] + gathered[e_local + e, piece(n)]
        for k in range(per):
            target = lax.rem(plane * PIECES // depth + 1 + n, PIECES) * per + k

            @pl.when(target != plane)
            def _():
                second_copy(target).start()

    def mixing(source, start):
        values = [mixed[source, e] for e in range(e_local)]

        for e in range(depth * e_local):
            value = mix[e, source * e_local] * values[0]
            for k in range(1, e_local):
                value = value + mix[e, source * e_local + k] * values[k]
            total[e] = value if start else total[e] + value

    mixed[plane] = summed[:, pl.ds(pl.multiple_of(plane * share, 8), share)]
    mixing(plane, True)
    order = [turn for step in range(1, depth // 2 + 1) for turn in sorted({step, depth - step})]
    for turn in order:
        source = lax.rem(plane + turn, depth)
        arrived(mixed.at[source], r_second.at[source])
        mixing(source, False)

    out[:, mom] = total[...]
    last_copy = send(total, out.at[:, mom], s_last.at[0], r_last.at[0], mom=other)
    last_copy.start()

    for e in range(e_local):

        @pl.when(straight(e))
        def _():
            base_copy(e).wait_send()

        @pl.when(detours(e))
        def _():
            for q in range(4):

                @pl.when(jnp.logical_or(q < 2, has_coup))
                def _():
                    detour_copy(outgoing.at[e, q % 2], q).wait_send()

        @pl.when(sends_coup(e))
        def _():
            coup_copy(e).wait_send()

    @pl.when(is_main)
    def _():
        def drain(j, carry):
            @pl.when(used(j))
            def _():
                hcoup_copy(j).wait_send()
                hgreen_copy(j).wait_send()

            for part in range(2):

                direct = jnp.logical_and(is_far, jnp.logical_not(relayed(j)))

                @pl.when(jnp.logical_and(direct, first_remote(j, part)))
                def _():
                    for n in range(PIECES):
                        first_copy(j, part, n).wait_send()

                @pl.when(relayed(j))
                def _():
                    for side in range(2):
                        relay_copy(j, part, side).wait_send()

            return carry

        lax.fori_loop(0, count, drain, 0)

        @pl.when(is_near)
        def _():
            for a in range(adopt):
                adopt_coup(a).wait_send()
                if a < adopt - 1:
                    adopt_green(a).wait_send()

    @pl.when(is_relay)
    def _():
        for q in range(4):

            @pl.when(jnp.logical_or(q < 2, has_coup))
            def _():
                pass_in(q).wait_send()

    @pl.when(jnp.logical_not(is_host))
    def _():
        for r in range(ROW):

            @pl.when(r != x)
            def _():
                for part in range(PIECES):
                    pass_copy(r, part).wait_send()

    @pl.when(is_helper)
    def _():
        def drain(j, carry):
            @pl.when(jnp.logical_not(is_last(j)))
            def _():
                chain_copy(j).wait_send()

            return carry

        lax.fori_loop(0, count, drain, 0)

    for turn in range(1, depth):
        second_copy(lax.rem(plane + turn, depth)).wait_send()
    last_copy.wait_send()
    arrived(out.at[:, other], r_last.at[0])


def body(onsite, hop, couple, sigma_in, shifts, mode_weight):
    e_local = sigma_in.shape[0]
    width = onsite.shape[-1]
    slabs = lax.axis_size("slab")
    depth = lax.axis_size("energy")
    total = e_local * depth
    share = width // depth
    block = (2, width, width)
    slots = max(CUT, slabs - BACK)

    def buffer(*shape):
        return pltpu.VMEM(shape, jnp.float32)

    def sems(*shape):
        return pltpu.SemaphoreType.DMA(shape)

    vmem = pl.BlockSpec(memory_space=pltpu.VMEM)
    smem = pl.BlockSpec(memory_space=pltpu.SMEM)
    stay = pl.BlockSpec(memory_space=pltpu.HBM)
    result = pl.pallas_call(
        functools.partial(kernel, CUT, BACK, slabs, depth, e_local),
        out_shape=jax.ShapeDtypeStruct((total, 2, share, width), jnp.float32),
        in_specs=[smem, smem, vmem, stay, stay, stay],
        out_specs=vmem,
        scratch_shapes=[
            buffer(*block),
            buffer(e_local, *block),
            buffer(e_local, *block),
            buffer(*block),
            buffer(slots, *block),
            buffer(slots, *block),
            buffer(slots + 1, *block),
            buffer(slots, *block),
            buffer(slots, *block),
            buffer(ROW, width, width),
            buffer(e_local, width, width),
            buffer(depth, e_local, share, width),
            buffer(total, share, width),
            pltpu.SMEM((total, total), jnp.float32),
            sems(2),
            sems(e_local), sems(slots), sems(e_local), sems(slots),
            sems(slots), sems(slots), sems(slots), sems(slots),
            sems(1), sems(1), sems(slots), sems(slots), sems(1), sems(1),
            sems(slots, 2, PIECES), sems(ROW, PIECES), sems(depth), sems(depth), sems(1), sems(1),
            sems(2 * (CUT - BACK)), sems(CUT - BACK), sems(ROW, 2), sems(4), sems(4), pltpu.SemaphoreType.REGULAR,
        ],
        compiler_params=pltpu.CompilerParams(
            collective_id=0, has_side_effects=True, vmem_limit_bytes=56 << 20
        ),
    )(shifts, mode_weight, onsite[0], hop[0, 0], couple[0, 0], sigma_in[:, 0])
    return result[:, None] / lax.axis_size("mom")


def solution(mesh):
    in_specs = (
        P("mom", "slab", None),
        P("mom", "slab", None, None, None),
        P("mom", "slab", None, None, None),
        P("energy", "slab", None, None, None),
        P(),
        P(),
    )
    out_specs = P(None, "slab", None, "energy", None)
    return jax.shard_map(body, mesh=mesh, in_specs=in_specs, out_specs=out_specs, check_vma=False)
```

```python
import functools

import jax
import jax.numpy as jnp
from jax import lax
from jax.experimental import pallas as pl
from jax.experimental.pallas import tpu as pltpu
from jax.sharding import PartitionSpec as P

ETA = 0.5
ROW = 4
CUT = 6
BACK = 5
PIECES = 4
FINAL = 8
MESH = pl.DeviceIdType.MESH


def split(mat):
    top = mat.astype(jnp.bfloat16)
    return top, (mat - top.astype(jnp.float32)).astype(jnp.bfloat16)


def prep(pair):
    return split(pair[0]), split(pair[1]), split(pair[0] + pair[1])


def prep_adjoint(pair):
    return prep((pair[0].T, -pair[1].T))


def mul(left, right):
    outs = []
    for (left_top, left_low), (top, low) in zip(left, right):
        outs.append(
            jnp.dot(
                jnp.concatenate([left_top, left_top, left_low], axis=1),
                jnp.concatenate([top, low, top], axis=0),
                preferred_element_type=jnp.float32,
            )
        )
    return outs[0] - outs[1], outs[2] - (outs[0] + outs[1])


def eye_mask(size):
    shape = (size, size)
    return lax.broadcasted_iota(jnp.int32, shape, 0) == lax.broadcasted_iota(jnp.int32, shape, 1)


def on_diagonal(mat, change):
    half = mat.shape[0] // 2
    upper = jnp.concatenate([change(mat[:half, :half], 0), mat[:half, half:]], axis=1)
    lower = jnp.concatenate([mat[half:, :half], change(mat[half:, half:], 1)], axis=1)
    return jnp.concatenate([upper, lower], axis=0)


def newton_inverse(mat):
    half = mat[0].shape[0] // 2
    eye = eye_mask(half)
    blocks = [
        [jnp.where(eye, part[:half, :half], 0.0), jnp.where(eye, part[half:, half:], 0.0)]
        for part in mat
    ]

    def inverse(diag):
        scale = 1.0 / (diag[0] * diag[0] + diag[1] * diag[1])
        return diag[0] * scale, -diag[1] * scale

    row = inverse(
        [jnp.concatenate([jnp.sum(b, axis=0, keepdims=True) for b in pair], axis=1) for pair in blocks]
    )
    col = inverse(
        [jnp.concatenate([jnp.sum(b, axis=1, keepdims=True) for b in pair], axis=0) for pair in blocks]
    )
    off = [on_diagonal(part, lambda block, n: jnp.where(eye, 0.0, block)) for part in mat]
    first = (off[0] * row[0] - off[1] * row[1], off[0] * row[1] + off[1] * row[0])
    fixed = prep(first)
    second = mul(fixed, fixed)
    third = mul(prep(second), fixed)
    real = second[0] - first[0] - third[0]
    imag = second[1] - first[1] - third[1]
    real = on_diagonal(real, lambda block, n: block + jnp.where(eye, 1.0, 0.0))
    return col[0] * real - col[1] * imag, col[0] * imag + col[1] * real


def load(ref):
    return ref[0], ref[1]


def store(ref, pair):
    ref[0] = pair[0]
    ref[1] = pair[1]


def kernel(
    cut, turn_at, slabs, depth, e_local,
    shifts, weights, onsite, hop_in, couple, sigma_in, out,
    hop, sigma, outgoing, left, box_a, box_b, box_c, box_d, box_e, gathered, summed, mixed, total,
    mix, s_in,
    s_base, r_base, s_coup, r_coup, s_hcoup, r_hcoup, s_hgreen, r_hgreen,
    s_hop, r_hop, s_chain, r_chain, s_back, r_back, s_first, r_first,
    s_second, r_second, s_last, r_last, s_adopt, r_adopt, r_relay, s_detour, r_detour, token,
):
    base = h_coup = h_adj = box_a
    coup = h_green = h_first = box_b
    green = h_chain = box_c
    chain = h_second = box_d
    full = box_e
    slab = lax.axis_index("slab")
    plane = lax.axis_index("energy")
    mom = lax.axis_index("mom")
    y, x = slab // ROW, lax.rem(slab, ROW)
    other = 1 - mom
    width = hop.shape[-1]
    share = width // depth
    span = width // PIECES
    half = width // 2
    near, far = 0, 2 * ROW
    in_far = jnp.where(slab >= cut, 1, 0)
    host_row = jnp.where(slab >= cut, far, near)
    adopt = cut - turn_at
    wide = slabs - turn_at
    is_near, is_far = y == 0, y == 2
    is_host = jnp.logical_or(is_near, is_far)
    is_main = jnp.logical_and(is_host, x // e_local == mom)
    is_helper = jnp.logical_and(is_host, x // e_local != mom)
    at_start = slab == 0
    offset = jnp.where(is_near, 0, turn_at)
    count = jnp.where(is_near, turn_at, wide)
    reach = jnp.where(is_near, cut, wide)

    def send(src, dst, send_sem, recv_sem, **where):
        return pltpu.make_async_remote_copy(
            src_ref=src, dst_ref=dst, send_sem=send_sem, recv_sem=recv_sem,
            device_id=where, device_id_type=MESH,
        )

    def arrived(dst, recv_sem):
        send(dst, dst, s_hop.at[0], recv_sem, mom=other).wait_recv()

    hop_load = pltpu.make_async_copy(hop_in, hop, s_in.at[0])
    sigma_load = pltpu.make_async_copy(sigma_in, sigma, s_in.at[1])
    hop_load.start()
    sigma_load.start()
    barrier = pltpu.get_barrier_semaphore()

    def greet(**where):
        pl.semaphore_signal(barrier, inc=1, device_id=where, device_id_type=MESH)

    opposite = lax.rem(x + 2, ROW)
    is_detour = opposite // e_local == mom
    is_relay = jnp.logical_and(y == 3, is_detour)
    starts_detour = jnp.logical_and(y == 0, jnp.logical_and(is_detour, x != 0))
    passes = jnp.logical_and(is_relay, x != 0)
    greet(mom=other)
    for turn in range(1, depth):
        greet(energy=lax.rem(plane + turn, depth))

    @pl.when(is_main)
    def _():
        first_source = jnp.where(is_near, 0, cut)

        def call(j, carry):
            @pl.when(first_source + j != slab)
            def _():
                greet(slab=first_source + j)

            return carry

        lax.fori_loop(0, jnp.where(is_near, cut, slabs - cut), call, 0)

        @pl.when(jnp.logical_and(is_near, x != 2))
        def _():
            greet(slab=3 * ROW + opposite)

        @pl.when(is_far)
        def _():
            greet(slab=x)

    @pl.when(jnp.logical_and(is_near, jnp.logical_not(is_main)))
    def _():
        greet(slab=far + x)

    @pl.when(passes)
    def _():
        greet(slab=x)

    for c in range(ROW):

        @pl.when(jnp.logical_and(is_host, x != c))
        def _():
            greet(slab=y * ROW + c, mom=c // e_local)

    @pl.when(jnp.logical_not(is_host))
    def _():
        greet(slab=far + x, mom=x // e_local)
        for turn in range(1, ROW):
            greet(slab=y * ROW + lax.rem(x + turn, ROW))

    @pl.when(y == 1)
    def _():
        greet(slab=near + x, mom=x // e_local)

    hop_load.wait()
    sigma_load.wait()
    eye = eye_mask(half)
    place = slab - in_far * turn_at

    def host_of(e):
        return host_row + e_local * mom + e

    def base_copy(e):
        return send(outgoing.at[e], base.at[place], s_base.at[e], r_base.at[place], slab=host_of(e))

    def coup_copy(e):
        return send(couple, coup.at[place], s_coup.at[e], r_coup.at[place], slab=host_of(e))

    def is_remote(e):
        return host_of(e) != slab

    def detours(e):
        return jnp.logical_and(y == 0, host_of(e) == opposite)

    def sends_coup(e):
        direct = jnp.logical_and(is_remote(e), jnp.logical_not(detours(e)))
        return jnp.logical_and(direct, jnp.logical_not(at_start))

    def detour_copy(part):
        return send(
            couple.at[part], box_a.at[0, part], s_detour.at[part], r_detour.at[part],
            slab=slab + 3 * ROW,
        )

    def pass_in(part):
        return send(
            box_a.at[0, part], coup.at[x, part], s_detour.at[part], r_coup.at[x], slab=opposite
        )

    own_coup = pltpu.make_async_copy(couple, coup.at[place], s_in.at[0])

    for e in range(e_local):
        level = -0.5 + ((plane * e_local + e).astype(jnp.float32) + 0.5) / (depth * e_local) - onsite[...]
        real = on_diagonal(
            -hop[0] - sigma[e, 0],
            lambda block, n: block + jnp.where(eye, level[:, n * half : (n + 1) * half], 0.0),
        )
        imag = on_diagonal(
            -hop[1] - sigma[e, 1], lambda block, n: block + jnp.where(eye, ETA, 0.0)
        )
        store(outgoing.at[e], (real, imag))

    def one(flag):
        return jnp.where(flag, 1, 0)

    expected = depth + jnp.where(is_host, 0, ROW - 1) + one(starts_detour) + one(passes)
    for e in range(e_local):
        expected = expected + one(is_remote(e))
    outputs = 2 * (ROW - 1) + jnp.where(is_near, 3, 4)
    expected = expected + jnp.where(is_main, outputs, one(is_far))
    pl.semaphore_wait(barrier, expected)

    @pl.when(starts_detour)
    def _():
        for part in range(2):
            detour_copy(part).start()

    for e in range(e_local):

        @pl.when(is_remote(e))
        def _():
            base_copy(e).start()

    for e in range(e_local):

        @pl.when(jnp.logical_and(sends_coup(e), jnp.logical_not(passes)))
        def _():
            coup_copy(e).start()

    for e in range(e_local):

        @pl.when(jnp.logical_not(is_remote(e)))
        def _():
            base[place] = outgoing[e]
            own_coup.start()

    @pl.when(passes)
    def _():
        for part in range(2):
            arrived(box_a.at[0, part], r_detour.at[part])
            pass_in(part).start()
        for e in range(e_local):
            coup_copy(e).start()

    def fill(e, carry):
        def entry(f, inner):
            value = jnp.float32(0.0)
            for mode in range(shifts.shape[0]):
                value = value + jnp.where(f == e + shifts[mode], weights[0, mode], 0.0)
                value = value + jnp.where(f == e - shifts[mode], weights[1, mode], 0.0)
            mix[e, f] = value * 0.5
            return inner

        return lax.fori_loop(0, depth * e_local, entry, carry)

    lax.fori_loop(0, depth * e_local, fill, 0)

    @pl.when(is_main)
    def _():
        own_coup.wait()

    def hcoup_copy(j):
        return send(coup.at[j], h_coup.at[j], s_hcoup.at[j], r_hcoup.at[j], mom=other)

    def hgreen_copy(j):
        return send(green.at[j + 1], h_green.at[j], s_hgreen.at[j], r_hgreen.at[j], mom=other)

    def hop_copy():
        return send(green.at[cut], green.at[adopt], s_hop.at[0], r_hop.at[0], slab=slab + far)

    def adopt_coup(a):
        return send(coup.at[turn_at + a], coup.at[a], s_adopt.at[a], r_coup.at[a], slab=slab + far)

    def adopt_green(a):
        return send(
            green.at[turn_at + a + 1], green.at[a + 1], s_adopt.at[adopt + a], r_adopt.at[a],
            slab=slab + far,
        )

    def used(j):
        return jnp.logical_and(
            jnp.logical_not(is_first(j)), jnp.logical_or(is_far, j < turn_at)
        )

    def held(j, part):
        late = offset + j >= slabs - ROW
        return jnp.logical_and(late, part == 1)

    def chain_copy(j):
        return send(h_chain.at[j + 1], chain.at[j], s_chain.at[j], r_chain.at[j], mom=other)

    def back_copy():
        return send(h_chain.at[0], h_chain.at[turn_at], s_back.at[0], r_back.at[0], slab=slab - far)

    def piece(n):
        return pl.ds(pl.multiple_of(lax.rem(plane * PIECES // depth + 1 + n, PIECES) * span, 8), span)

    def first_copy(j, part, n):
        return send(
            full.at[j, part, piece(n)], gathered.at[x, piece(n)], s_first.at[j, part, n],
            r_first.at[x, n], slab=offset + j, mom=part,
        )

    def relay_copy(j, part, side):
        where = pl.ds(side * half, half)
        return send(
            full.at[j, part, where], full.at[lax.rem(offset + j, ROW), part, where],
            s_first.at[j, part, side], r_relay.at[lax.rem(offset + j, ROW), side],
            slab=(offset + j) // ROW * ROW + x, mom=part,
        )

    def relayed(j):
        return (offset + j) // ROW != y

    def pass_copy(r, part):
        where = pl.ds(part * span, span)
        order = lax.rem(part + 2 * PIECES - 1 - plane * PIECES // depth, PIECES)
        return send(
            full.at[r, mom, where], gathered.at[x, where], s_first.at[r, 0, part],
            r_first.at[x, order], slab=y * ROW + r,
        )

    def is_first(j):
        return jnp.logical_and(is_near, j == 0)

    def is_last(j):
        return jnp.logical_and(is_far, j == count - 1)

    def first_remote(j, part):
        return jnp.logical_or(offset + j != slab, part != mom)

    @pl.when(is_main)
    def _():
        @pl.when(is_far)
        def _():
            arrived(green.at[adopt], r_hop.at[0])

        def forward(j, carry):
            @pl.when(j != place)
            def _():
                arrived(base.at[j], r_base.at[j])

            @pl.when(is_first(j))
            def _():
                left[...] = jnp.zeros_like(left)

            @pl.when(jnp.logical_not(is_first(j)))
            def _():
                @pl.when(j != place)
                def _():
                    arrived(coup.at[j], r_coup.at[j])

                @pl.when(used(j))
                def _():
                    hcoup_copy(j).start()

                coupling = load(coup.at[j])
                half_way = mul(prep(load(green.at[j])), prep_adjoint(coupling))
                store(left, mul(prep(coupling), prep(half_way)))

            store(
                green.at[j + 1],
                newton_inverse((base[j, 0] - left[0], base[j, 1] - left[1])),
            )

            @pl.when(used(j))
            def _():
                hgreen_copy(j).start()

            @pl.when(jnp.logical_and(is_far, j == wide - 3))
            def _():
                for a in range(adopt):
                    arrived(coup.at[a], r_coup.at[a])
                    if a < adopt - 1:
                        arrived(green.at[a + 1], r_adopt.at[a])
                    hcoup_copy(a).start()
                    hgreen_copy(a).start()

            return carry

        lax.fori_loop(jnp.where(is_near, 0, adopt), reach, forward, 0)

        @pl.when(is_near)
        def _():
            hop_copy().start()
            hop_copy().wait_send()
            for a in range(adopt):
                adopt_coup(a).start()
                if a < adopt - 1:
                    adopt_green(a).start()

        def backward(turn, carry):
            j = count - 1 - turn

            @pl.when(is_last(j))
            def _():
                full[j] = green[j + 1]

            @pl.when(jnp.logical_not(is_last(j)))
            def _():
                arrived(chain.at[j], r_chain.at[j])
                pair = load(green.at[j + 1])
                ready = prep(pair)
                extra = mul(prep(mul(ready, prep(load(chain.at[j])))), ready)
                store(full.at[j], (pair[0] + extra[0], pair[1] + extra[1]))

            for n in range(PIECES):
                for part in range(2):
                    now = jnp.logical_and(is_far, jnp.logical_not(relayed(j)))
                    if n == 0:
                        now = jnp.logical_or(jnp.logical_and(is_near, jnp.logical_not(relayed(j))), now)

                    @pl.when(jnp.logical_and(first_remote(j, part), now))
                    def _():
                        first_copy(j, part, n).start()

            for part in range(2):

                @pl.when(jnp.logical_and(relayed(j), jnp.logical_not(held(j, part))))
                def _():
                    for side in range(2):
                        relay_copy(j, part, side).start()

                @pl.when(jnp.logical_not(first_remote(j, part)))
                def _():
                    gathered[x] = full[j, part]

            return carry

        lax.fori_loop(0, count, backward, 0)

        @pl.when(is_near)
        def _():
            def sweep(n, act):
                def one(j, carry):
                    for part in range(2):

                        @pl.when(jnp.logical_and(first_remote(j, part), jnp.logical_not(relayed(j))))
                        def _():
                            act(first_copy(j, part, n))

                    return carry

                lax.fori_loop(0, count, one, 0)

            for n in range(1, PIECES):
                sweep(n, lambda copy: copy.start())
                sweep(n - 1, lambda copy: copy.wait_send())
            sweep(PIECES - 1, lambda copy: copy.wait_send())

        @pl.when(is_far)
        def _():
            pl.semaphore_wait(token, 1)

            def release(j, carry):
                for part in range(2):

                    @pl.when(held(j, part))
                    def _():
                        for side in range(2):
                            relay_copy(j, part, side).start()

                return carry

            lax.fori_loop(0, count, release, 0)

    @pl.when(is_helper)
    def _():
        def forward(step, carry):
            early = wide - 2 - adopt
            late = jnp.where(step < early + adopt, step - early, step)
            j = jnp.where(is_near, step, jnp.where(step < early, step + adopt, late))

            @pl.when(jnp.logical_not(is_first(j)))
            def _():
                arrived(h_coup.at[j], r_hcoup.at[j])
                coupling = load(h_coup.at[j])
                adjoint = (coupling[0].T, -coupling[1].T)
                ready_left, ready_right = prep(adjoint), prep(coupling)
                store(h_adj.at[j], adjoint)
                arrived(h_green.at[j], r_hgreen.at[j])
                ready = prep(load(h_green.at[j]))
                store(h_first.at[j], mul(ready_left, ready))
                store(h_second.at[j], mul(ready, ready_right))

            return carry

        lax.fori_loop(0, count, forward, 0)

        @pl.when(is_far)
        def _():
            h_chain[wide] = jnp.zeros_like(h_chain.at[wide])

        @pl.when(is_near)
        def _():
            arrived(h_chain.at[turn_at], r_back.at[0])

        def backward(turn, carry):
            j = count - 1 - turn

            @pl.when(jnp.logical_not(is_last(j)))
            def _():
                chain_copy(j).start()

            @pl.when(jnp.logical_not(is_first(j)))
            def _():
                extra = mul(prep(load(h_first.at[j])), prep(load(h_chain.at[j + 1])))
                adjoint = load(h_adj.at[j])
                sums = (adjoint[0] + extra[0], adjoint[1] + extra[1])
                store(h_chain.at[j], mul(prep(sums), prep(load(h_second.at[j]))))

            return carry

        lax.fori_loop(0, count, backward, 0)

        @pl.when(is_far)
        def _():
            back_copy().start()
            back_copy().wait_send()
            pl.semaphore_signal(token, inc=1, device_id={"mom": other}, device_id_type=MESH)

    def second_copy(target):
        return send(
            summed.at[:, pl.ds(pl.multiple_of(target * share, 8), share)], mixed.at[plane],
            s_second.at[target], r_second.at[plane], energy=target,
        )

    @pl.when(jnp.logical_not(is_host))
    def _():
        def hand_on(turn, carry):
            r = ROW - 1 - turn
            for side in range(2):
                where = pl.ds(side * half, half)
                arrived(full.at[r, mom, where], r_relay.at[r, side])

                @pl.when(r != x)
                def _():
                    for part in range(side * PIECES // 2, (side + 1) * PIECES // 2):
                        pass_copy(r, part).start()

                @pl.when(r == x)
                def _():
                    gathered[x, where] = full[r, mom, where]

            return carry

        lax.fori_loop(0, ROW, hand_on, 0)

    local_first = jnp.logical_or(is_main, jnp.logical_not(is_host))
    per = depth // PIECES
    for n in range(PIECES):
        for c in range(ROW):

            @pl.when(jnp.logical_or(c != x, jnp.logical_not(local_first)))
            def _():
                arrived(gathered.at[c, piece(n)], r_first.at[c, n])

        for e in range(e_local):
            summed[e, piece(n)] = gathered[e, piece(n)] + gathered[e_local + e, piece(n)]
        for k in range(per):
            target = lax.rem(plane * PIECES // depth + 1 + n, PIECES) * per + k

            @pl.when(target != plane)
            def _():
                second_copy(target).start()

    def mixing(source, start):
        values = [mixed[source, e] for e in range(e_local)]

        for e in range(depth * e_local):
            value = mix[e, source * e_local] * values[0]
            for k in range(1, e_local):
                value = value + mix[e, source * e_local + k] * values[k]
            total[e] = value if start else total[e] + value

    mixed[plane] = summed[:, pl.ds(pl.multiple_of(plane * share, 8), share)]
    mixing(plane, True)
    order = [turn for step in range(1, depth // 2 + 1) for turn in sorted({step, depth - step})]
    for turn in order:
        source = lax.rem(plane + turn, depth)
        arrived(mixed.at[source], r_second.at[source])
        mixing(source, False)

    out[:, mom] = total[...]
    last_copy = send(total, out.at[:, mom], s_last.at[0], r_last.at[0], mom=other)
    last_copy.start()

    for e in range(e_local):

        @pl.when(is_remote(e))
        def _():
            base_copy(e).wait_send()

        @pl.when(sends_coup(e))
        def _():
            coup_copy(e).wait_send()

    @pl.when(is_main)
    def _():
        def drain(j, carry):
            @pl.when(used(j))
            def _():
                hcoup_copy(j).wait_send()
                hgreen_copy(j).wait_send()

            for part in range(2):

                direct = jnp.logical_and(is_far, jnp.logical_not(relayed(j)))

                @pl.when(jnp.logical_and(direct, first_remote(j, part)))
                def _():
                    for n in range(PIECES):
                        first_copy(j, part, n).wait_send()

                @pl.when(relayed(j))
                def _():
                    for side in range(2):
                        relay_copy(j, part, side).wait_send()

            return carry

        lax.fori_loop(0, count, drain, 0)

        @pl.when(is_near)
        def _():
            for a in range(adopt):
                adopt_coup(a).wait_send()
                if a < adopt - 1:
                    adopt_green(a).wait_send()

    @pl.when(starts_detour)
    def _():
        for part in range(2):
            detour_copy(part).wait_send()

    @pl.when(passes)
    def _():
        for part in range(2):
            pass_in(part).wait_send()

    @pl.when(jnp.logical_not(is_host))
    def _():
        for r in range(ROW):

            @pl.when(r != x)
            def _():
                for part in range(PIECES):
                    pass_copy(r, part).wait_send()

    @pl.when(is_helper)
    def _():
        def drain(j, carry):
            @pl.when(jnp.logical_not(is_last(j)))
            def _():
                chain_copy(j).wait_send()

            return carry

        lax.fori_loop(0, count, drain, 0)

    for turn in range(1, depth):
        second_copy(lax.rem(plane + turn, depth)).wait_send()
    last_copy.wait_send()
    arrived(out.at[:, other], r_last.at[0])


def finish(source, target, done):
    step = source.shape[0] // FINAL
    copies = [
        pltpu.make_async_copy(
            source.at[n * step : (n + 1) * step], target.at[n * step : (n + 1) * step], done.at[n]
        )
        for n in range(FINAL)
    ]
    for copy in copies:
        copy.start()
    for copy in copies:
        copy.wait()


def body(onsite, hop, couple, sigma_in, shifts, mode_weight):
    e_local = sigma_in.shape[0]
    width = onsite.shape[-1]
    slabs = lax.axis_size("slab")
    depth = lax.axis_size("energy")
    total = e_local * depth
    share = width // depth
    block = (2, width, width)
    slots = max(CUT, slabs - BACK)

    def buffer(*shape):
        return pltpu.VMEM(shape, jnp.float32)

    def sems(*shape):
        return pltpu.SemaphoreType.DMA(shape)

    vmem = pl.BlockSpec(memory_space=pltpu.VMEM)
    smem = pl.BlockSpec(memory_space=pltpu.SMEM)
    stay = pl.BlockSpec(memory_space=pltpu.HBM)
    result = pl.pallas_call(
        functools.partial(kernel, CUT, BACK, slabs, depth, e_local),
        out_shape=jax.ShapeDtypeStruct((total, 2, share, width), jnp.float32),
        in_specs=[smem, smem, vmem, stay, stay, stay],
        out_specs=vmem,
        scratch_shapes=[
            buffer(*block),
            buffer(e_local, *block),
            buffer(e_local, *block),
            buffer(*block),
            buffer(slots, *block),
            buffer(slots, *block),
            buffer(slots + 1, *block),
            buffer(slots, *block),
            buffer(slots, *block),
            buffer(ROW, width, width),
            buffer(e_local, width, width),
            buffer(depth, e_local, share, width),
            buffer(total, share, width),
            pltpu.SMEM((total, total), jnp.float32),
            sems(2),
            sems(e_local), sems(slots), sems(e_local), sems(slots),
            sems(slots), sems(slots), sems(slots), sems(slots),
            sems(1), sems(1), sems(slots), sems(slots), sems(1), sems(1),
            sems(slots, 2, PIECES), sems(ROW, PIECES), sems(depth), sems(depth), sems(1), sems(1),
            sems(2 * (CUT - BACK)), sems(CUT - BACK), sems(ROW, 2), sems(2), sems(2), pltpu.SemaphoreType.REGULAR,
        ],
        compiler_params=pltpu.CompilerParams(
            collective_id=0, has_side_effects=True, vmem_limit_bytes=56 << 20
        ),
    )(shifts, mode_weight, onsite[0], hop[0, 0], couple[0, 0], sigma_in[:, 0])
    final = pl.pallas_call(
        finish,
        out_shape=jax.ShapeDtypeStruct(result.shape, jnp.float32),
        in_specs=[stay],
        out_specs=stay,
        scratch_shapes=[sems(FINAL)],
    )(result)
    return final[:, None]


def solution(mesh):
    in_specs = (
        P("mom", "slab", None),
        P("mom", "slab", None, None, None),
        P("mom", "slab", None, None, None),
        P("energy", "slab", None, None, None),
        P(),
        P(),
    )
    out_specs = P(None, "slab", None, "energy", None)
    return jax.shard_map(body, mesh=mesh, in_specs=in_specs, out_specs=out_specs, check_vma=False)
```

```python
import functools

import jax
import jax.numpy as jnp
from jax import lax
from jax.experimental import pallas as pl
from jax.experimental.pallas import tpu as pltpu
from jax.sharding import PartitionSpec as P

ETA = 0.5
ROW = 4
CUT = 6
BACK = 5
PIECES = 4
ORDER = (2, 1, 3, 0)
HASTE = 0
MESH = pl.DeviceIdType.MESH


def split(mat):
    top = mat.astype(jnp.bfloat16)
    return top, (mat - top.astype(jnp.float32)).astype(jnp.bfloat16)


def prep(pair):
    return split(pair[0]), split(pair[1]), split(pair[0] + pair[1])


def prep_adjoint(pair):
    return prep((pair[0].T, -pair[1].T))


def mul(left, right):
    outs = []
    for (left_top, left_low), (top, low) in zip(left, right):
        outs.append(
            jnp.dot(
                jnp.concatenate([left_top, left_top, left_low], axis=1),
                jnp.concatenate([top, low, top], axis=0),
                preferred_element_type=jnp.float32,
            )
        )
    return outs[0] - outs[1], outs[2] - (outs[0] + outs[1])


def eye_mask(size):
    shape = (size, size)
    return lax.broadcasted_iota(jnp.int32, shape, 0) == lax.broadcasted_iota(jnp.int32, shape, 1)


def on_diagonal(mat, change):
    half = mat.shape[0] // 2
    upper = jnp.concatenate([change(mat[:half, :half], 0), mat[:half, half:]], axis=1)
    lower = jnp.concatenate([mat[half:, :half], change(mat[half:, half:], 1)], axis=1)
    return jnp.concatenate([upper, lower], axis=0)


def newton_inverse(mat):
    half = mat[0].shape[0] // 2
    eye = eye_mask(half)
    blocks = [
        [jnp.where(eye, part[:half, :half], 0.0), jnp.where(eye, part[half:, half:], 0.0)]
        for part in mat
    ]

    def inverse(diag):
        scale = 1.0 / (diag[0] * diag[0] + diag[1] * diag[1])
        return diag[0] * scale, -diag[1] * scale

    row = inverse(
        [jnp.concatenate([jnp.sum(b, axis=0, keepdims=True) for b in pair], axis=1) for pair in blocks]
    )
    col = inverse(
        [jnp.concatenate([jnp.sum(b, axis=1, keepdims=True) for b in pair], axis=0) for pair in blocks]
    )
    off = [on_diagonal(part, lambda block, n: jnp.where(eye, 0.0, block)) for part in mat]
    first = (off[0] * row[0] - off[1] * row[1], off[0] * row[1] + off[1] * row[0])
    fixed = prep(first)
    second = mul(fixed, fixed)
    third = mul(prep(second), fixed)
    real = second[0] - first[0] - third[0]
    imag = second[1] - first[1] - third[1]
    real = on_diagonal(real, lambda block, n: block + jnp.where(eye, 1.0, 0.0))
    return col[0] * real - col[1] * imag, col[0] * imag + col[1] * real


def load(ref):
    return ref[0], ref[1]


def store(ref, pair):
    ref[0] = pair[0]
    ref[1] = pair[1]


def kernel(
    cut, turn_at, slabs, depth, e_local,
    shifts, weights, onsite, hop_in, couple, sigma_in, out,
    hop, sigma, outgoing, left, box_a, box_b, box_c, box_d, box_e, gathered, summed, mixed, total,
    mix, s_in,
    s_base, r_base, s_coup, r_coup, s_hcoup, r_hcoup, s_hgreen, r_hgreen,
    s_hop, r_hop, s_chain, r_chain, s_back, r_back, s_first, r_first,
    s_second, r_second, s_last, r_last, s_adopt, r_adopt, r_relay, s_detour, r_detour, token,
):
    base = h_coup = h_adj = box_a
    coup = h_green = h_first = box_b
    green = h_chain = box_c
    chain = h_second = box_d
    full = box_e
    slab = lax.axis_index("slab")
    plane = lax.axis_index("energy")
    mom = lax.axis_index("mom")
    y, x = slab // ROW, lax.rem(slab, ROW)
    other = 1 - mom
    width = hop.shape[-1]
    share = width // depth
    span = width // PIECES
    half = width // 2
    near, far = 0, 2 * ROW
    in_far = jnp.where(slab >= cut, 1, 0)
    host_row = jnp.where(slab >= cut, far, near)
    adopt = cut - turn_at
    wide = slabs - turn_at
    is_near, is_far = y == 0, y == 2
    is_host = jnp.logical_or(is_near, is_far)
    is_main = jnp.logical_and(is_host, x // e_local == mom)
    is_helper = jnp.logical_and(is_host, x // e_local != mom)
    at_start = slab == 0
    offset = jnp.where(is_near, 0, turn_at)
    count = jnp.where(is_near, turn_at, wide)
    reach = jnp.where(is_near, cut, wide)

    def send(src, dst, send_sem, recv_sem, **where):
        return pltpu.make_async_remote_copy(
            src_ref=src, dst_ref=dst, send_sem=send_sem, recv_sem=recv_sem,
            device_id=where, device_id_type=MESH,
        )

    def arrived(dst, recv_sem):
        send(dst, dst, s_hop.at[0], recv_sem, mom=other).wait_recv()

    loads = []
    for part in range(2):
        loads.append(pltpu.make_async_copy(hop_in.at[part], hop.at[part], s_in.at[part]))
        for e in range(e_local):
            sem = s_in.at[2 + e * 2 + part]
            loads.append(pltpu.make_async_copy(sigma_in.at[e, part], sigma.at[e, part], sem))
    for item in loads:
        item.start()
    barrier = pltpu.get_barrier_semaphore()

    def greet(**where):
        pl.semaphore_signal(barrier, inc=1, device_id=where, device_id_type=MESH)

    opposite = lax.rem(x + 2, ROW)
    is_detour = opposite // e_local == mom
    is_relay = jnp.logical_and(y == 3, is_detour)
    starts_detour = jnp.logical_and(y == 0, jnp.logical_and(is_detour, x != 0))
    passes = jnp.logical_and(is_relay, x != 0)
    greet(mom=other)
    for turn in range(1, depth):
        greet(energy=lax.rem(plane + turn, depth))

    @pl.when(is_main)
    def _():
        first_source = jnp.where(is_near, 0, cut)

        def call(j, carry):
            @pl.when(first_source + j != slab)
            def _():
                greet(slab=first_source + j)

            return carry

        lax.fori_loop(0, jnp.where(is_near, cut, slabs - cut), call, 0)

        @pl.when(jnp.logical_and(is_near, x != 2))
        def _():
            greet(slab=3 * ROW + opposite)

        @pl.when(is_far)
        def _():
            greet(slab=x)

    @pl.when(jnp.logical_and(is_near, jnp.logical_not(is_main)))
    def _():
        greet(slab=far + x)

    @pl.when(passes)
    def _():
        greet(slab=x)

    for c in range(ROW):

        @pl.when(jnp.logical_and(is_host, x != c))
        def _():
            greet(slab=y * ROW + c, mom=c // e_local)

    @pl.when(jnp.logical_not(is_host))
    def _():
        greet(slab=far + x, mom=x // e_local)
        for turn in range(1, ROW):
            greet(slab=y * ROW + lax.rem(x + turn, ROW))

    @pl.when(y == 1)
    def _():
        greet(slab=near + x, mom=x // e_local)

    for item in loads:
        item.wait()
    eye = eye_mask(half)
    place = slab - in_far * turn_at

    def host_of(e):
        return host_row + e_local * mom + e

    def base_copy(e):
        return send(outgoing.at[e], base.at[place], s_base.at[e], r_base.at[place], slab=host_of(e))

    def coup_copy(e):
        return send(couple, coup.at[place], s_coup.at[e], r_coup.at[place], slab=host_of(e))

    def is_remote(e):
        return host_of(e) != slab

    def detours(e):
        return jnp.logical_and(y == 0, host_of(e) == opposite)

    def sends_coup(e):
        direct = jnp.logical_and(is_remote(e), jnp.logical_not(detours(e)))
        return jnp.logical_and(direct, jnp.logical_not(at_start))

    def detour_copy(part):
        return send(
            couple.at[part], box_a.at[0, part], s_detour.at[part], r_detour.at[part],
            slab=slab + 3 * ROW,
        )

    def pass_in(part):
        return send(
            box_a.at[0, part], coup.at[x, part], s_detour.at[part], r_coup.at[x], slab=opposite
        )

    own_coup = pltpu.make_async_copy(couple, coup.at[place], s_in.at[0])

    for e in range(e_local):
        level = -0.5 + ((plane * e_local + e).astype(jnp.float32) + 0.5) / (depth * e_local) - onsite[...]
        real = on_diagonal(
            -hop[0] - sigma[e, 0],
            lambda block, n: block + jnp.where(eye, level[:, n * half : (n + 1) * half], 0.0),
        )
        imag = on_diagonal(
            -hop[1] - sigma[e, 1], lambda block, n: block + jnp.where(eye, ETA, 0.0)
        )
        store(outgoing.at[e], (real, imag))

    def one(flag):
        return jnp.where(flag, 1, 0)

    expected = depth + jnp.where(is_host, 0, ROW - 1) + one(starts_detour) + one(passes)
    for e in range(e_local):
        expected = expected + one(is_remote(e))
    outputs = 2 * (ROW - 1) + jnp.where(is_near, 3, 4)
    expected = expected + jnp.where(is_main, outputs, one(is_far))
    pl.semaphore_wait(barrier, expected)

    @pl.when(starts_detour)
    def _():
        for part in range(2):
            detour_copy(part).start()

    for e in range(e_local):

        @pl.when(jnp.logical_and(is_remote(e), jnp.logical_not(passes)))
        def _():
            base_copy(e).start()

    for e in range(e_local):

        @pl.when(jnp.logical_and(sends_coup(e), jnp.logical_not(passes)))
        def _():
            coup_copy(e).start()

    for e in range(e_local):

        @pl.when(jnp.logical_not(is_remote(e)))
        def _():
            base[place] = outgoing[e]
            own_coup.start()

    @pl.when(passes)
    def _():
        for part in range(2):
            arrived(box_a.at[0, part], r_detour.at[part])
            pass_in(part).start()
        for part in range(2):
            pass_in(part).wait_send()
        for e in range(e_local):
            base_copy(e).start()
        for e in range(e_local):
            coup_copy(e).start()

    def fill(e, carry):
        def entry(f, inner):
            value = jnp.float32(0.0)
            for mode in range(shifts.shape[0]):
                value = value + jnp.where(f == e + shifts[mode], weights[0, mode], 0.0)
                value = value + jnp.where(f == e - shifts[mode], weights[1, mode], 0.0)
            mix[e, f] = value * 0.5
            return inner

        return lax.fori_loop(0, depth * e_local, entry, carry)

    lax.fori_loop(0, depth * e_local, fill, 0)

    @pl.when(is_main)
    def _():
        own_coup.wait()

    def hcoup_copy(j):
        return send(coup.at[j], h_coup.at[j], s_hcoup.at[j], r_hcoup.at[j], mom=other)

    def hgreen_copy(j):
        return send(green.at[j + 1], h_green.at[j], s_hgreen.at[j], r_hgreen.at[j], mom=other)

    def hop_copy():
        return send(green.at[cut], green.at[adopt], s_hop.at[0], r_hop.at[0], slab=slab + far)

    def adopt_coup(a):
        return send(coup.at[turn_at + a], coup.at[a], s_adopt.at[a], r_coup.at[a], slab=slab + far)

    def adopt_green(a):
        return send(
            green.at[turn_at + a + 1], green.at[a + 1], s_adopt.at[adopt + a], r_adopt.at[a],
            slab=slab + far,
        )

    def used(j):
        return jnp.logical_and(
            jnp.logical_not(is_first(j)), jnp.logical_or(is_far, j < turn_at)
        )

    def held(j, part):
        late = jnp.logical_and(offset + j >= slabs - ROW, offset + j < slabs - HASTE)
        return jnp.logical_and(late, part == 1)

    def chain_copy(j):
        return send(h_chain.at[j + 1], chain.at[j], s_chain.at[j], r_chain.at[j], mom=other)

    def back_copy():
        return send(h_chain.at[0], h_chain.at[turn_at], s_back.at[0], r_back.at[0], slab=slab - far)

    def piece(n):
        return pl.ds(pl.multiple_of(lax.rem(plane * PIECES // depth + ORDER[n], PIECES) * span, 8), span)

    def first_copy(j, part, n):
        return send(
            full.at[j, part, piece(n)], gathered.at[x, piece(n)], s_first.at[j, part, n],
            r_first.at[x, n], slab=offset + j, mom=part,
        )

    def relay_copy(j, part, n):
        where = piece(n)
        return send(
            full.at[j, part, where], full.at[lax.rem(offset + j, ROW), part, where],
            s_first.at[j, part, n], r_relay.at[lax.rem(offset + j, ROW), n],
            slab=(offset + j) // ROW * ROW + x, mom=part,
        )

    def relayed(j):
        return (offset + j) // ROW != y

    def pass_copy(r, n):
        return send(
            full.at[r, mom, piece(n)], gathered.at[x, piece(n)], s_first.at[r, 0, n],
            r_first.at[x, n], slab=y * ROW + r,
        )

    def is_first(j):
        return jnp.logical_and(is_near, j == 0)

    def is_last(j):
        return jnp.logical_and(is_far, j == count - 1)

    def first_remote(j, part):
        return jnp.logical_or(offset + j != slab, part != mom)

    @pl.when(is_main)
    def _():
        @pl.when(is_far)
        def _():
            arrived(green.at[adopt], r_hop.at[0])

        def forward(j, carry):
            @pl.when(j != place)
            def _():
                arrived(base.at[j], r_base.at[j])

            @pl.when(is_first(j))
            def _():
                left[...] = jnp.zeros_like(left)

            @pl.when(jnp.logical_not(is_first(j)))
            def _():
                @pl.when(j != place)
                def _():
                    arrived(coup.at[j], r_coup.at[j])

                @pl.when(used(j))
                def _():
                    hcoup_copy(j).start()

                coupling = load(coup.at[j])
                half_way = mul(prep(load(green.at[j])), prep_adjoint(coupling))
                store(left, mul(prep(coupling), prep(half_way)))

            store(
                green.at[j + 1],
                newton_inverse((base[j, 0] - left[0], base[j, 1] - left[1])),
            )

            @pl.when(used(j))
            def _():
                hgreen_copy(j).start()

            @pl.when(jnp.logical_and(is_far, j == wide - 3))
            def _():
                for a in range(adopt):
                    arrived(coup.at[a], r_coup.at[a])
                    if a < adopt - 1:
                        arrived(green.at[a + 1], r_adopt.at[a])
                    hcoup_copy(a).start()
                    hgreen_copy(a).start()

            return carry

        lax.fori_loop(jnp.where(is_near, 0, adopt), reach, forward, 0)

        @pl.when(is_near)
        def _():
            hop_copy().start()
            hop_copy().wait_send()
            for a in range(adopt):
                adopt_coup(a).start()
                if a < adopt - 1:
                    adopt_green(a).start()

        def backward(turn, carry):
            j = count - 1 - turn

            @pl.when(is_last(j))
            def _():
                full[j] = green[j + 1]

            @pl.when(jnp.logical_not(is_last(j)))
            def _():
                arrived(chain.at[j], r_chain.at[j])
                pair = load(green.at[j + 1])
                ready = prep(pair)
                extra = mul(prep(mul(ready, prep(load(chain.at[j])))), ready)
                store(full.at[j], (pair[0] + extra[0], pair[1] + extra[1]))

            for n in range(PIECES):
                for part in range(2):
                    now = jnp.logical_and(is_far, jnp.logical_not(relayed(j)))
                    if n == 0:
                        now = jnp.logical_or(jnp.logical_and(is_near, jnp.logical_not(relayed(j))), now)

                    @pl.when(jnp.logical_and(first_remote(j, part), now))
                    def _():
                        first_copy(j, part, n).start()

            for part in range(2):

                @pl.when(jnp.logical_and(relayed(j), jnp.logical_not(held(j, part))))
                def _():
                    for n in range(PIECES):
                        relay_copy(j, part, n).start()

                @pl.when(jnp.logical_not(first_remote(j, part)))
                def _():
                    gathered[x] = full[j, part]

            return carry

        lax.fori_loop(0, count, backward, 0)

        @pl.when(is_near)
        def _():
            def sweep(n, act):
                def one(j, carry):
                    for part in range(2):

                        @pl.when(jnp.logical_and(first_remote(j, part), jnp.logical_not(relayed(j))))
                        def _():
                            act(first_copy(j, part, n))

                    return carry

                lax.fori_loop(0, count, one, 0)

            for n in range(1, PIECES):
                sweep(n, lambda copy: copy.start())
                sweep(n - 1, lambda copy: copy.wait_send())
            sweep(PIECES - 1, lambda copy: copy.wait_send())

        @pl.when(is_far)
        def _():
            pl.semaphore_wait(token, 1)

            def release(j, carry):
                for part in range(2):

                    @pl.when(held(j, part))
                    def _():
                        for n in range(PIECES):
                            relay_copy(j, part, n).start()

                return carry

            lax.fori_loop(0, count, release, 0)

    @pl.when(is_helper)
    def _():
        def forward(step, carry):
            early = wide - 2 - adopt
            late = jnp.where(step < early + adopt, step - early, step)
            j = jnp.where(is_near, step, jnp.where(step < early, step + adopt, late))

            @pl.when(jnp.logical_not(is_first(j)))
            def _():
                arrived(h_coup.at[j], r_hcoup.at[j])
                coupling = load(h_coup.at[j])
                adjoint = (coupling[0].T, -coupling[1].T)
                ready_left, ready_right = prep(adjoint), prep(coupling)
                store(h_adj.at[j], adjoint)
                arrived(h_green.at[j], r_hgreen.at[j])
                ready = prep(load(h_green.at[j]))
                store(h_first.at[j], mul(ready_left, ready))
                store(h_second.at[j], mul(ready, ready_right))

            return carry

        lax.fori_loop(0, count, forward, 0)

        @pl.when(is_far)
        def _():
            h_chain[wide] = jnp.zeros_like(h_chain.at[wide])

        @pl.when(is_near)
        def _():
            arrived(h_chain.at[turn_at], r_back.at[0])

        def backward(turn, carry):
            j = count - 1 - turn

            @pl.when(jnp.logical_not(is_last(j)))
            def _():
                chain_copy(j).start()

            @pl.when(jnp.logical_not(is_first(j)))
            def _():
                extra = mul(prep(load(h_first.at[j])), prep(load(h_chain.at[j + 1])))
                adjoint = load(h_adj.at[j])
                sums = (adjoint[0] + extra[0], adjoint[1] + extra[1])
                store(h_chain.at[j], mul(prep(sums), prep(load(h_second.at[j]))))

            return carry

        lax.fori_loop(0, count, backward, 0)

        @pl.when(is_far)
        def _():
            back_copy().start()
            back_copy().wait_send()
            pl.semaphore_signal(token, inc=1, device_id={"mom": other}, device_id_type=MESH)

    def second_copy(target):
        return send(
            summed.at[:, pl.ds(pl.multiple_of(target * share, 8), share)], mixed.at[plane],
            s_second.at[target], r_second.at[plane], energy=target,
        )

    @pl.when(jnp.logical_not(is_host))
    def _():
        def hand_on(turn, carry):
            r = ROW - 1 - turn
            for n in range(PIECES):
                arrived(full.at[r, mom, piece(n)], r_relay.at[r, n])

                @pl.when(r != x)
                def _():
                    pass_copy(r, n).start()

                @pl.when(r == x)
                def _():
                    gathered[x, piece(n)] = full[r, mom, piece(n)]

            return carry

        lax.fori_loop(0, ROW, hand_on, 0)

    local_first = jnp.logical_or(is_main, jnp.logical_not(is_host))
    per = depth // PIECES
    for n in range(PIECES):
        for c in range(ROW):

            @pl.when(jnp.logical_or(c != x, jnp.logical_not(local_first)))
            def _():
                arrived(gathered.at[c, piece(n)], r_first.at[c, n])

        for e in range(e_local):
            summed[e, piece(n)] = gathered[e, piece(n)] + gathered[e_local + e, piece(n)]
        for k in range(per):
            target = lax.rem(plane * PIECES // depth + ORDER[n], PIECES) * per + k

            @pl.when(target != plane)
            def _():
                second_copy(target).start()

    def mixing(source, start):
        values = [mixed[source, e] for e in range(e_local)]

        for e in range(depth * e_local):
            value = mix[e, source * e_local] * values[0]
            for k in range(1, e_local):
                value = value + mix[e, source * e_local + k] * values[k]
            total[e] = value if start else total[e] + value

    mixed[plane] = summed[:, pl.ds(pl.multiple_of(plane * share, 8), share)]
    mixing(plane, True)
    order = [turn for step in range(1, depth // 2 + 1) for turn in sorted({step, depth - step})]
    for turn in order:
        source = lax.rem(plane + turn, depth)
        arrived(mixed.at[source], r_second.at[source])
        mixing(source, False)

    last_copy = send(total, out.at[:, mom], s_last.at[0], r_last.at[0], mom=other)
    last_copy.start()
    own_last = pltpu.make_async_copy(total, out.at[:, mom], s_last.at[1])
    own_last.start()

    for e in range(e_local):

        @pl.when(is_remote(e))
        def _():
            base_copy(e).wait_send()

        @pl.when(sends_coup(e))
        def _():
            coup_copy(e).wait_send()

    @pl.when(is_main)
    def _():
        def drain(j, carry):
            @pl.when(used(j))
            def _():
                hcoup_copy(j).wait_send()
                hgreen_copy(j).wait_send()

            for part in range(2):

                direct = jnp.logical_and(is_far, jnp.logical_not(relayed(j)))

                @pl.when(jnp.logical_and(direct, first_remote(j, part)))
                def _():
                    for n in range(PIECES):
                        first_copy(j, part, n).wait_send()

                @pl.when(relayed(j))
                def _():
                    for n in range(PIECES):
                        relay_copy(j, part, n).wait_send()

            return carry

        lax.fori_loop(0, count, drain, 0)

        @pl.when(is_near)
        def _():
            for a in range(adopt):
                adopt_coup(a).wait_send()
                if a < adopt - 1:
                    adopt_green(a).wait_send()

    @pl.when(starts_detour)
    def _():
        for part in range(2):
            detour_copy(part).wait_send()

    @pl.when(jnp.logical_not(is_host))
    def _():
        for r in range(ROW):

            @pl.when(r != x)
            def _():
                for n in range(PIECES):
                    pass_copy(r, n).wait_send()

    @pl.when(is_helper)
    def _():
        def drain(j, carry):
            @pl.when(jnp.logical_not(is_last(j)))
            def _():
                chain_copy(j).wait_send()

            return carry

        lax.fori_loop(0, count, drain, 0)

    for turn in range(1, depth):
        second_copy(lax.rem(plane + turn, depth)).wait_send()
    last_copy.wait_send()
    own_last.wait()
    arrived(out.at[:, other], r_last.at[0])


def body(onsite, hop, couple, sigma_in, shifts, mode_weight):
    e_local = sigma_in.shape[0]
    width = onsite.shape[-1]
    slabs = lax.axis_size("slab")
    depth = lax.axis_size("energy")
    total = e_local * depth
    share = width // depth
    block = (2, width, width)
    slots = max(CUT, slabs - BACK)

    def buffer(*shape):
        return pltpu.VMEM(shape, jnp.float32)

    def sems(*shape):
        return pltpu.SemaphoreType.DMA(shape)

    vmem = pl.BlockSpec(memory_space=pltpu.VMEM)
    smem = pl.BlockSpec(memory_space=pltpu.SMEM)
    stay = pl.BlockSpec(memory_space=pltpu.HBM)
    result = pl.pallas_call(
        functools.partial(kernel, CUT, BACK, slabs, depth, e_local),
        out_shape=jax.ShapeDtypeStruct((total, 2, share, width), jnp.float32),
        in_specs=[smem, smem, vmem, stay, stay, stay],
        out_specs=stay,
        scratch_shapes=[
            buffer(*block),
            buffer(e_local, *block),
            buffer(e_local, *block),
            buffer(*block),
            buffer(slots, *block),
            buffer(slots, *block),
            buffer(slots + 1, *block),
            buffer(slots, *block),
            buffer(slots, *block),
            buffer(ROW, width, width),
            buffer(e_local, width, width),
            buffer(depth, e_local, share, width),
            buffer(total, share, width),
            pltpu.SMEM((total, total), jnp.float32),
            sems(2 + 2 * e_local),
            sems(e_local), sems(slots), sems(e_local), sems(slots),
            sems(slots), sems(slots), sems(slots), sems(slots),
            sems(1), sems(1), sems(slots), sems(slots), sems(1), sems(1),
            sems(slots, 2, PIECES), sems(ROW, PIECES), sems(depth), sems(depth), sems(2), sems(1),
            sems(2 * (CUT - BACK)), sems(CUT - BACK), sems(ROW, PIECES), sems(2), sems(2), pltpu.SemaphoreType.REGULAR,
        ],
        compiler_params=pltpu.CompilerParams(
            collective_id=0, has_side_effects=True, vmem_limit_bytes=56 << 20
        ),
    )(shifts, mode_weight, onsite[0], hop[0, 0], couple[0, 0], sigma_in[:, 0])
    return result[:, None]


def solution(mesh):
    in_specs = (
        P("mom", "slab", None),
        P("mom", "slab", None, None, None),
        P("mom", "slab", None, None, None),
        P("energy", "slab", None, None, None),
        P(),
        P(),
    )
    out_specs = P(None, "slab", None, "energy", None)
    return jax.shard_map(body, mesh=mesh, in_specs=in_specs, out_specs=out_specs, check_vma=False)
```

```python
import functools

import jax
import jax.numpy as jnp
from jax import lax
from jax.experimental import pallas as pl
from jax.experimental.pallas import tpu as pltpu
from jax.sharding import PartitionSpec as P

ETA = 0.5
ROW = 4
CUT = 6
BACK = 5
PIECES = 4
ORDER = (2, 1, 3, 0)
HASTE = 3
MESH = pl.DeviceIdType.MESH


def split(mat):
    top = mat.astype(jnp.bfloat16)
    return top, (mat - top.astype(jnp.float32)).astype(jnp.bfloat16)


def prep(pair):
    return split(pair[0]), split(pair[1]), split(pair[0] + pair[1])


def prep_adjoint(pair):
    return prep((pair[0].T, -pair[1].T))


def mul(left, right):
    outs = []
    for (left_top, left_low), (top, low) in zip(left, right):
        outs.append(
            jnp.dot(
                jnp.concatenate([left_top, left_top, left_low], axis=1),
                jnp.concatenate([top, low, top], axis=0),
                preferred_element_type=jnp.float32,
            )
        )
    return outs[0] - outs[1], outs[2] - (outs[0] + outs[1])


def eye_mask(size):
    shape = (size, size)
    return lax.broadcasted_iota(jnp.int32, shape, 0) == lax.broadcasted_iota(jnp.int32, shape, 1)


def on_diagonal(mat, change):
    half = mat.shape[0] // 2
    upper = jnp.concatenate([change(mat[:half, :half], 0), mat[:half, half:]], axis=1)
    lower = jnp.concatenate([mat[half:, :half], change(mat[half:, half:], 1)], axis=1)
    return jnp.concatenate([upper, lower], axis=0)


def newton_inverse(mat):
    half = mat[0].shape[0] // 2
    eye = eye_mask(half)
    blocks = [
        [jnp.where(eye, part[:half, :half], 0.0), jnp.where(eye, part[half:, half:], 0.0)]
        for part in mat
    ]

    def inverse(diag):
        scale = 1.0 / (diag[0] * diag[0] + diag[1] * diag[1])
        return diag[0] * scale, -diag[1] * scale

    row = inverse(
        [jnp.concatenate([jnp.sum(b, axis=0, keepdims=True) for b in pair], axis=1) for pair in blocks]
    )
    col = inverse(
        [jnp.concatenate([jnp.sum(b, axis=1, keepdims=True) for b in pair], axis=0) for pair in blocks]
    )
    off = [on_diagonal(part, lambda block, n: jnp.where(eye, 0.0, block)) for part in mat]
    first = (off[0] * row[0] - off[1] * row[1], off[0] * row[1] + off[1] * row[0])
    fixed = prep(first)
    second = mul(fixed, fixed)
    third = mul(prep(second), fixed)
    real = second[0] - first[0] - third[0]
    imag = second[1] - first[1] - third[1]
    real = on_diagonal(real, lambda block, n: block + jnp.where(eye, 1.0, 0.0))
    return col[0] * real - col[1] * imag, col[0] * imag + col[1] * real


def load(ref):
    return ref[0], ref[1]


def keep(ref, ready):
    for n, parts in enumerate(ready):
        ref[2 * n] = parts[0]
        ref[2 * n + 1] = parts[1]


def fetch(ref):
    return tuple((ref[2 * n], ref[2 * n + 1]) for n in range(3))


def store(ref, pair):
    ref[0] = pair[0]
    ref[1] = pair[1]


def kernel(
    cut, turn_at, slabs, depth, e_local,
    shifts, weights, onsite, hop_in, couple, sigma_in, out,
    hop, sigma, outgoing, left, box_a, box_b, box_c, box_d, box_e, h_first, h_second, gathered, summed, mixed, total,
    mix, s_in,
    s_base, r_base, s_coup, r_coup, s_hcoup, r_hcoup, s_hgreen, r_hgreen,
    s_hop, r_hop, s_chain, r_chain, s_back, r_back, s_first, r_first,
    s_second, r_second, s_last, r_last, s_adopt, r_adopt, r_relay, s_detour, r_detour, token,
):
    base = h_coup = h_adj = box_a
    coup = h_green = box_b
    green = h_chain = box_c
    chain = box_d
    full = box_e
    slab = lax.axis_index("slab")
    plane = lax.axis_index("energy")
    mom = lax.axis_index("mom")
    y, x = slab // ROW, lax.rem(slab, ROW)
    other = 1 - mom
    width = hop.shape[-1]
    share = width // depth
    span = width // PIECES
    half = width // 2
    near, far = 0, 2 * ROW
    in_far = jnp.where(slab >= cut, 1, 0)
    host_row = jnp.where(slab >= cut, far, near)
    adopt = cut - turn_at
    wide = slabs - turn_at
    is_near, is_far = y == 0, y == 2
    is_host = jnp.logical_or(is_near, is_far)
    is_main = jnp.logical_and(is_host, x // e_local == mom)
    is_helper = jnp.logical_and(is_host, x // e_local != mom)
    at_start = slab == 0
    offset = jnp.where(is_near, 0, turn_at)
    count = jnp.where(is_near, turn_at, wide)
    reach = jnp.where(is_near, cut, wide)

    def send(src, dst, send_sem, recv_sem, **where):
        return pltpu.make_async_remote_copy(
            src_ref=src, dst_ref=dst, send_sem=send_sem, recv_sem=recv_sem,
            device_id=where, device_id_type=MESH,
        )

    def arrived(dst, recv_sem):
        send(dst, dst, s_hop.at[0], recv_sem, mom=other).wait_recv()

    loads = []
    for part in range(2):
        loads.append(pltpu.make_async_copy(hop_in.at[part], hop.at[part], s_in.at[part]))
        for e in range(e_local):
            sem = s_in.at[2 + e * 2 + part]
            loads.append(pltpu.make_async_copy(sigma_in.at[e, part], sigma.at[e, part], sem))
    for item in loads:
        item.start()
    barrier = pltpu.get_barrier_semaphore()

    def greet(**where):
        pl.semaphore_signal(barrier, inc=1, device_id=where, device_id_type=MESH)

    opposite = lax.rem(x + 2, ROW)
    is_detour = opposite // e_local == mom
    is_relay = jnp.logical_and(y == 3, is_detour)
    starts_detour = jnp.logical_and(y == 0, jnp.logical_and(is_detour, x != 0))
    passes = jnp.logical_and(is_relay, x != 0)
    greet(mom=other)
    for turn in range(1, depth):
        greet(energy=lax.rem(plane + turn, depth))

    @pl.when(is_main)
    def _():
        first_source = jnp.where(is_near, 0, cut)

        def call(j, carry):
            @pl.when(first_source + j != slab)
            def _():
                greet(slab=first_source + j)

            return carry

        lax.fori_loop(0, jnp.where(is_near, cut, slabs - cut), call, 0)

        @pl.when(jnp.logical_and(is_near, x != 2))
        def _():
            greet(slab=3 * ROW + opposite)

        @pl.when(is_far)
        def _():
            greet(slab=x)

    @pl.when(jnp.logical_and(is_near, jnp.logical_not(is_main)))
    def _():
        greet(slab=far + x)

    @pl.when(passes)
    def _():
        greet(slab=x)

    for c in range(ROW):

        @pl.when(jnp.logical_and(is_host, x != c))
        def _():
            greet(slab=y * ROW + c, mom=c // e_local)

    @pl.when(jnp.logical_not(is_host))
    def _():
        greet(slab=far + x, mom=x // e_local)
        for turn in range(1, ROW):
            greet(slab=y * ROW + lax.rem(x + turn, ROW))

    @pl.when(y == 1)
    def _():
        greet(slab=near + x, mom=x // e_local)

    for item in loads:
        item.wait()
    eye = eye_mask(half)
    place = slab - in_far * turn_at

    def host_of(e):
        return host_row + e_local * mom + e

    def base_copy(e):
        return send(outgoing.at[e], base.at[place], s_base.at[e], r_base.at[place], slab=host_of(e))

    def coup_copy(e):
        return send(couple, coup.at[place], s_coup.at[e], r_coup.at[place], slab=host_of(e))

    def is_remote(e):
        return host_of(e) != slab

    def detours(e):
        return jnp.logical_and(y == 0, host_of(e) == opposite)

    def sends_coup(e):
        direct = jnp.logical_and(is_remote(e), jnp.logical_not(detours(e)))
        return jnp.logical_and(direct, jnp.logical_not(at_start))

    def detour_copy(part):
        return send(
            couple.at[part], box_a.at[0, part], s_detour.at[part], r_detour.at[part],
            slab=slab + 3 * ROW,
        )

    def pass_in(part):
        return send(
            box_a.at[0, part], coup.at[x, part], s_detour.at[part], r_coup.at[x], slab=opposite
        )

    own_coup = pltpu.make_async_copy(couple, coup.at[place], s_in.at[0])

    for e in range(e_local):
        level = -0.5 + ((plane * e_local + e).astype(jnp.float32) + 0.5) / (depth * e_local) - onsite[...]
        real = on_diagonal(
            -hop[0] - sigma[e, 0],
            lambda block, n: block + jnp.where(eye, level[:, n * half : (n + 1) * half], 0.0),
        )
        imag = on_diagonal(
            -hop[1] - sigma[e, 1], lambda block, n: block + jnp.where(eye, ETA, 0.0)
        )
        store(outgoing.at[e], (real, imag))

    def one(flag):
        return jnp.where(flag, 1, 0)

    expected = depth + jnp.where(is_host, 0, ROW - 1) + one(starts_detour) + one(passes)
    for e in range(e_local):
        expected = expected + one(is_remote(e))
    outputs = 2 * (ROW - 1) + jnp.where(is_near, 3, 4)
    expected = expected + jnp.where(is_main, outputs, one(is_far))
    pl.semaphore_wait(barrier, expected)

    @pl.when(starts_detour)
    def _():
        for part in range(2):
            detour_copy(part).start()

    for e in range(e_local):

        @pl.when(jnp.logical_and(is_remote(e), jnp.logical_not(passes)))
        def _():
            base_copy(e).start()

    for e in range(e_local):

        @pl.when(jnp.logical_and(sends_coup(e), jnp.logical_not(passes)))
        def _():
            coup_copy(e).start()

    for e in range(e_local):

        @pl.when(jnp.logical_not(is_remote(e)))
        def _():
            base[place] = outgoing[e]
            own_coup.start()

    @pl.when(passes)
    def _():
        for part in range(2):
            arrived(box_a.at[0, part], r_detour.at[part])
            pass_in(part).start()
        for part in range(2):
            pass_in(part).wait_send()
        for e in range(e_local):
            base_copy(e).start()
        for e in range(e_local):
            coup_copy(e).start()

    def fill(e, carry):
        def entry(f, inner):
            value = jnp.float32(0.0)
            for mode in range(shifts.shape[0]):
                value = value + jnp.where(f == e + shifts[mode], weights[0, mode], 0.0)
                value = value + jnp.where(f == e - shifts[mode], weights[1, mode], 0.0)
            mix[e, f] = value * 0.5
            return inner

        return lax.fori_loop(0, depth * e_local, entry, carry)

    lax.fori_loop(0, depth * e_local, fill, 0)

    @pl.when(is_main)
    def _():
        own_coup.wait()

    def hcoup_copy(j):
        return send(coup.at[j], h_coup.at[j], s_hcoup.at[j], r_hcoup.at[j], mom=other)

    def hgreen_copy(j):
        return send(green.at[j + 1], h_green.at[j], s_hgreen.at[j], r_hgreen.at[j], mom=other)

    def hop_copy():
        return send(green.at[cut], green.at[adopt], s_hop.at[0], r_hop.at[0], slab=slab + far)

    def adopt_coup(a):
        return send(coup.at[turn_at + a], coup.at[a], s_adopt.at[a], r_coup.at[a], slab=slab + far)

    def adopt_green(a):
        return send(
            green.at[turn_at + a + 1], green.at[a + 1], s_adopt.at[adopt + a], r_adopt.at[a],
            slab=slab + far,
        )

    def used(j):
        return jnp.logical_and(
            jnp.logical_not(is_first(j)), jnp.logical_or(is_far, j < turn_at)
        )

    def held(j, part):
        late = offset + j >= slabs - ROW
        return jnp.logical_and(late, jnp.logical_or(part == 1, offset + j < slabs - HASTE))

    def chain_copy(j):
        return send(h_chain.at[j + 1], chain.at[j], s_chain.at[j], r_chain.at[j], mom=other)

    def back_copy():
        return send(h_chain.at[0], h_chain.at[turn_at], s_back.at[0], r_back.at[0], slab=slab - far)

    def piece(n):
        return pl.ds(pl.multiple_of(lax.rem(plane * PIECES // depth + ORDER[n], PIECES) * span, 8), span)

    def first_copy(j, part, n):
        return send(
            full.at[j, part, piece(n)], gathered.at[x, piece(n)], s_first.at[j, part, n],
            r_first.at[x, n], slab=offset + j, mom=part,
        )

    def relay_copy(j, part, n):
        where = piece(n)
        return send(
            full.at[j, part, where], full.at[lax.rem(offset + j, ROW), part, where],
            s_first.at[j, part, n], r_relay.at[lax.rem(offset + j, ROW), n],
            slab=(offset + j) // ROW * ROW + x, mom=part,
        )

    def relayed(j):
        return (offset + j) // ROW != y

    def pass_copy(r, n):
        return send(
            full.at[r, mom, piece(n)], gathered.at[x, piece(n)], s_first.at[r, 0, n],
            r_first.at[x, n], slab=y * ROW + r,
        )

    def is_first(j):
        return jnp.logical_and(is_near, j == 0)

    def is_last(j):
        return jnp.logical_and(is_far, j == count - 1)

    def first_remote(j, part):
        return jnp.logical_or(offset + j != slab, part != mom)

    @pl.when(is_main)
    def _():
        @pl.when(is_far)
        def _():
            arrived(green.at[adopt], r_hop.at[0])

        def forward(j, carry):
            @pl.when(j != place)
            def _():
                arrived(base.at[j], r_base.at[j])

            @pl.when(is_first(j))
            def _():
                left[...] = jnp.zeros_like(left)

            @pl.when(jnp.logical_not(is_first(j)))
            def _():
                @pl.when(j != place)
                def _():
                    arrived(coup.at[j], r_coup.at[j])

                @pl.when(used(j))
                def _():
                    hcoup_copy(j).start()

                coupling = load(coup.at[j])
                half_way = mul(prep(load(green.at[j])), prep_adjoint(coupling))
                store(left, mul(prep(coupling), prep(half_way)))

            store(
                green.at[j + 1],
                newton_inverse((base[j, 0] - left[0], base[j, 1] - left[1])),
            )

            @pl.when(used(j))
            def _():
                hgreen_copy(j).start()

            @pl.when(jnp.logical_and(is_far, j == wide - 3))
            def _():
                for a in range(adopt):
                    arrived(coup.at[a], r_coup.at[a])
                    if a < adopt - 1:
                        arrived(green.at[a + 1], r_adopt.at[a])
                    hcoup_copy(a).start()
                    hgreen_copy(a).start()

            return carry

        lax.fori_loop(jnp.where(is_near, 0, adopt), reach, forward, 0)

        @pl.when(is_near)
        def _():
            hop_copy().start()
            hop_copy().wait_send()
            for a in range(adopt):
                adopt_coup(a).start()
                if a < adopt - 1:
                    adopt_green(a).start()

        def backward(turn, carry):
            j = count - 1 - turn

            @pl.when(is_last(j))
            def _():
                full[j] = green[j + 1]

            @pl.when(jnp.logical_not(is_last(j)))
            def _():
                pair = load(green.at[j + 1])
                ready = prep(pair)
                arrived(chain.at[j], r_chain.at[j])
                extra = mul(prep(mul(ready, prep(load(chain.at[j])))), ready)
                store(full.at[j], (pair[0] + extra[0], pair[1] + extra[1]))

            for n in range(PIECES):
                for part in range(2):
                    now = jnp.logical_and(is_far, jnp.logical_not(relayed(j)))
                    if n == 0:
                        now = jnp.logical_or(jnp.logical_and(is_near, jnp.logical_not(relayed(j))), now)

                    @pl.when(jnp.logical_and(first_remote(j, part), now))
                    def _():
                        first_copy(j, part, n).start()

            for part in range(2):

                @pl.when(jnp.logical_and(relayed(j), jnp.logical_not(held(j, part))))
                def _():
                    for n in range(PIECES):
                        relay_copy(j, part, n).start()

                @pl.when(jnp.logical_not(first_remote(j, part)))
                def _():
                    gathered[x] = full[j, part]

            return carry

        lax.fori_loop(0, count, backward, 0)

        @pl.when(is_near)
        def _():
            def sweep(n, act):
                def one(j, carry):
                    for part in range(2):

                        @pl.when(jnp.logical_and(first_remote(j, part), jnp.logical_not(relayed(j))))
                        def _():
                            act(first_copy(j, part, n))

                    return carry

                lax.fori_loop(0, count, one, 0)

            for n in range(1, PIECES):
                sweep(n, lambda copy: copy.start())
                sweep(n - 1, lambda copy: copy.wait_send())
            sweep(PIECES - 1, lambda copy: copy.wait_send())

        @pl.when(is_far)
        def _():
            pl.semaphore_wait(token, 1)

            def release(turn, carry):
                j = count - 1 - turn
                for part in range(2):

                    @pl.when(held(j, part))
                    def _():
                        for n in range(PIECES):
                            relay_copy(j, part, n).start()

                return carry

            lax.fori_loop(0, count, release, 0)

    @pl.when(is_helper)
    def _():
        def forward(step, carry):
            early = wide - 2 - adopt
            late = jnp.where(step < early + adopt, step - early, step)
            j = jnp.where(is_near, step, jnp.where(step < early, step + adopt, late))

            @pl.when(jnp.logical_not(is_first(j)))
            def _():
                arrived(h_coup.at[j], r_hcoup.at[j])
                coupling = load(h_coup.at[j])
                adjoint = (coupling[0].T, -coupling[1].T)
                ready_left, ready_right = prep(adjoint), prep(coupling)
                store(h_adj.at[j], adjoint)
                arrived(h_green.at[j], r_hgreen.at[j])
                ready = prep(load(h_green.at[j]))
                keep(h_first.at[j], prep(mul(ready_left, ready)))
                keep(h_second.at[j], prep(mul(ready, ready_right)))

            return carry

        lax.fori_loop(0, count, forward, 0)

        @pl.when(is_far)
        def _():
            h_chain[wide] = jnp.zeros_like(h_chain.at[wide])

        @pl.when(is_near)
        def _():
            arrived(h_chain.at[turn_at], r_back.at[0])

        def backward(turn, carry):
            j = count - 1 - turn

            @pl.when(jnp.logical_not(is_last(j)))
            def _():
                chain_copy(j).start()

            @pl.when(jnp.logical_not(is_first(j)))
            def _():
                extra = mul(fetch(h_first.at[j]), prep(load(h_chain.at[j + 1])))
                adjoint = load(h_adj.at[j])
                sums = (adjoint[0] + extra[0], adjoint[1] + extra[1])
                store(h_chain.at[j], mul(prep(sums), fetch(h_second.at[j])))

            return carry

        lax.fori_loop(0, count, backward, 0)

        @pl.when(is_far)
        def _():
            back_copy().start()
            back_copy().wait_send()
            pl.semaphore_signal(token, inc=1, device_id={"mom": other}, device_id_type=MESH)

    def second_copy(target):
        return send(
            summed.at[:, pl.ds(pl.multiple_of(target * share, 8), share)], mixed.at[plane],
            s_second.at[target], r_second.at[plane], energy=target,
        )

    @pl.when(jnp.logical_not(is_host))
    def _():
        def hand_on(turn, carry):
            r = jnp.where(jnp.logical_and(y == 1, turn >= 2), turn - 2, ROW - 1 - turn)
            for n in range(PIECES):
                arrived(full.at[r, mom, piece(n)], r_relay.at[r, n])

                @pl.when(r != x)
                def _():
                    pass_copy(r, n).start()

                @pl.when(r == x)
                def _():
                    gathered[x, piece(n)] = full[r, mom, piece(n)]

            return carry

        lax.fori_loop(0, ROW, hand_on, 0)

    local_first = jnp.logical_or(is_main, jnp.logical_not(is_host))
    per = depth // PIECES
    for n in range(PIECES):
        for c in range(ROW):

            @pl.when(jnp.logical_or(c != x, jnp.logical_not(local_first)))
            def _():
                arrived(gathered.at[c, piece(n)], r_first.at[c, n])

        for e in range(e_local):
            summed[e, piece(n)] = gathered[e, piece(n)] + gathered[e_local + e, piece(n)]
        for k in range(per):
            target = lax.rem(plane * PIECES // depth + ORDER[n], PIECES) * per + k

            @pl.when(target != plane)
            def _():
                second_copy(target).start()

    def mixing(source, start):
        values = [mixed[source, e] for e in range(e_local)]

        for e in range(depth * e_local):
            value = mix[e, source * e_local] * values[0]
            for k in range(1, e_local):
                value = value + mix[e, source * e_local + k] * values[k]
            total[e] = value if start else total[e] + value

    mixed[plane] = summed[:, pl.ds(pl.multiple_of(plane * share, 8), share)]
    mixing(plane, True)
    order = [turn for step in range(1, depth // 2 + 1) for turn in sorted({step, depth - step})]
    for turn in order:
        source = lax.rem(plane + turn, depth)
        arrived(mixed.at[source], r_second.at[source])
        mixing(source, False)

    last_copy = send(total, out.at[:, mom], s_last.at[0], r_last.at[0], mom=other)
    last_copy.start()
    own_last = pltpu.make_async_copy(total, out.at[:, mom], s_last.at[1])
    own_last.start()

    for e in range(e_local):

        @pl.when(is_remote(e))
        def _():
            base_copy(e).wait_send()

        @pl.when(sends_coup(e))
        def _():
            coup_copy(e).wait_send()

    @pl.when(is_main)
    def _():
        def drain(j, carry):
            @pl.when(used(j))
            def _():
                hcoup_copy(j).wait_send()
                hgreen_copy(j).wait_send()

            for part in range(2):

                direct = jnp.logical_and(is_far, jnp.logical_not(relayed(j)))

                @pl.when(jnp.logical_and(direct, first_remote(j, part)))
                def _():
                    for n in range(PIECES):
                        first_copy(j, part, n).wait_send()

                @pl.when(relayed(j))
                def _():
                    for n in range(PIECES):
                        relay_copy(j, part, n).wait_send()

            return carry

        lax.fori_loop(0, count, drain, 0)

        @pl.when(is_near)
        def _():
            for a in range(adopt):
                adopt_coup(a).wait_send()
                if a < adopt - 1:
                    adopt_green(a).wait_send()

    @pl.when(starts_detour)
    def _():
        for part in range(2):
            detour_copy(part).wait_send()

    @pl.when(jnp.logical_not(is_host))
    def _():
        for r in range(ROW):

            @pl.when(r != x)
            def _():
                for n in range(PIECES):
                    pass_copy(r, n).wait_send()

    @pl.when(is_helper)
    def _():
        def drain(j, carry):
            @pl.when(jnp.logical_not(is_last(j)))
            def _():
                chain_copy(j).wait_send()

            return carry

        lax.fori_loop(0, count, drain, 0)

    for turn in range(1, depth):
        second_copy(lax.rem(plane + turn, depth)).wait_send()
    last_copy.wait_send()
    own_last.wait()
    arrived(out.at[:, other], r_last.at[0])


def body(onsite, hop, couple, sigma_in, shifts, mode_weight):
    e_local = sigma_in.shape[0]
    width = onsite.shape[-1]
    slabs = lax.axis_size("slab")
    depth = lax.axis_size("energy")
    total = e_local * depth
    share = width // depth
    block = (2, width, width)
    slots = max(CUT, slabs - BACK)
    spare = max(1, CUT - BACK)

    def buffer(*shape):
        return pltpu.VMEM(shape, jnp.float32)

    def sems(*shape):
        return pltpu.SemaphoreType.DMA(shape)

    vmem = pl.BlockSpec(memory_space=pltpu.VMEM)
    smem = pl.BlockSpec(memory_space=pltpu.SMEM)
    stay = pl.BlockSpec(memory_space=pltpu.HBM)
    result = pl.pallas_call(
        functools.partial(kernel, CUT, BACK, slabs, depth, e_local),
        out_shape=jax.ShapeDtypeStruct((total, 2, share, width), jnp.float32),
        in_specs=[smem, smem, vmem, stay, stay, stay],
        out_specs=stay,
        scratch_shapes=[
            buffer(*block),
            buffer(e_local, *block),
            buffer(e_local, *block),
            buffer(*block),
            buffer(slots, *block),
            buffer(slots, *block),
            buffer(slots + 1, *block),
            buffer(slots, *block),
            buffer(slots, *block),
            pltpu.VMEM((slots, 6, width, width), jnp.bfloat16),
            pltpu.VMEM((slots, 6, width, width), jnp.bfloat16),
            buffer(ROW, width, width),
            buffer(e_local, width, width),
            buffer(depth, e_local, share, width),
            buffer(total, share, width),
            pltpu.SMEM((total, total), jnp.float32),
            sems(2 + 2 * e_local),
            sems(e_local), sems(slots), sems(e_local), sems(slots),
            sems(slots), sems(slots), sems(slots), sems(slots),
            sems(1), sems(1), sems(slots), sems(slots), sems(1), sems(1),
            sems(slots, 2, PIECES), sems(ROW, PIECES), sems(depth), sems(depth), sems(2), sems(1),
            sems(2 * spare), sems(spare), sems(ROW, PIECES), sems(2), sems(2), pltpu.SemaphoreType.REGULAR,
        ],
        compiler_params=pltpu.CompilerParams(
            collective_id=0, has_side_effects=True, vmem_limit_bytes=56 << 20
        ),
    )(shifts, mode_weight, onsite[0], hop[0, 0], couple[0, 0], sigma_in[:, 0])
    return result[:, None]


def solution(mesh):
    in_specs = (
        P("mom", "slab", None),
        P("mom", "slab", None, None, None),
        P("mom", "slab", None, None, None),
        P("energy", "slab", None, None, None),
        P(),
        P(),
    )
    out_specs = P(None, "slab", None, "energy", None)
    return jax.shard_map(body, mesh=mesh, in_specs=in_specs, out_specs=out_specs, check_vma=False)
```

```python
import functools

import jax
import jax.numpy as jnp
from jax import lax
from jax.experimental import pallas as pl
from jax.experimental.pallas import tpu as pltpu
from jax.sharding import PartitionSpec as P

ETA = 0.5
ROW = 4
CUT = 6
BACK = 5
PIECES = 4
ORDER = (2, 1, 3, 0)
HASTE = 3
MESH = pl.DeviceIdType.MESH


def split(mat):
    top = mat.astype(jnp.bfloat16)
    return top, (mat - top.astype(jnp.float32)).astype(jnp.bfloat16)


def prep(pair):
    return split(pair[0]), split(pair[1]), split(pair[0] + pair[1])


def prep_adjoint(pair):
    return prep((pair[0].T, -pair[1].T))


def mul(left, right):
    outs = []
    for (left_top, left_low), (top, low) in zip(left, right):
        outs.append(
            jnp.dot(
                jnp.concatenate([left_top, left_top, left_low], axis=1),
                jnp.concatenate([top, low, top], axis=0),
                preferred_element_type=jnp.float32,
            )
        )
    return outs[0] - outs[1], outs[2] - (outs[0] + outs[1])


def eye_mask(size):
    shape = (size, size)
    return lax.broadcasted_iota(jnp.int32, shape, 0) == lax.broadcasted_iota(jnp.int32, shape, 1)


def on_diagonal(mat, change):
    half = mat.shape[0] // 2
    upper = jnp.concatenate([change(mat[:half, :half], 0), mat[:half, half:]], axis=1)
    lower = jnp.concatenate([mat[half:, :half], change(mat[half:, half:], 1)], axis=1)
    return jnp.concatenate([upper, lower], axis=0)


def newton_inverse(mat):
    half = mat[0].shape[0] // 2
    eye = eye_mask(half)
    blocks = [
        [jnp.where(eye, part[:half, :half], 0.0), jnp.where(eye, part[half:, half:], 0.0)]
        for part in mat
    ]

    def inverse(diag):
        scale = 1.0 / (diag[0] * diag[0] + diag[1] * diag[1])
        return diag[0] * scale, -diag[1] * scale

    row = inverse(
        [jnp.concatenate([jnp.sum(b, axis=0, keepdims=True) for b in pair], axis=1) for pair in blocks]
    )
    col = inverse(
        [jnp.concatenate([jnp.sum(b, axis=1, keepdims=True) for b in pair], axis=0) for pair in blocks]
    )
    off = [on_diagonal(part, lambda block, n: jnp.where(eye, 0.0, block)) for part in mat]
    first = (off[0] * row[0] - off[1] * row[1], off[0] * row[1] + off[1] * row[0])
    fixed = prep(first)
    second = mul(fixed, fixed)
    third = mul(prep(second), fixed)
    real = second[0] - first[0] - third[0]
    imag = second[1] - first[1] - third[1]
    real = on_diagonal(real, lambda block, n: block + jnp.where(eye, 1.0, 0.0))
    return col[0] * real - col[1] * imag, col[0] * imag + col[1] * real


def load(ref):
    return ref[0], ref[1]


def keep(ref, ready):
    for n, parts in enumerate(ready):
        ref[2 * n] = parts[0]
        ref[2 * n + 1] = parts[1]


def fetch(ref):
    return tuple((ref[2 * n], ref[2 * n + 1]) for n in range(3))


def store(ref, pair):
    ref[0] = pair[0]
    ref[1] = pair[1]


def kernel(
    cut, turn_at, slabs, depth, e_local,
    shifts, weights, onsite, hop_in, couple, sigma_in, out,
    hop, sigma, outgoing, left, box_a, box_b, box_c, box_d, box_e, h_first, h_second, gathered, summed, mixed, total,
    mix, s_in,
    s_base, r_base, s_coup, r_coup, s_hcoup, r_hcoup, s_hgreen, r_hgreen,
    s_hop, r_hop, s_chain, r_chain, s_back, r_back, s_first, r_first,
    s_second, r_second, s_last, r_last, s_adopt, r_adopt, r_relay, s_detour, r_detour, token,
):
    base = h_coup = h_adj = box_a
    coup = h_green = box_b
    green = h_chain = box_c
    chain = box_d
    full = box_e
    slab = lax.axis_index("slab")
    plane = lax.axis_index("energy")
    mom = lax.axis_index("mom")
    y, x = slab // ROW, lax.rem(slab, ROW)
    other = 1 - mom
    width = hop.shape[-1]
    share = width // depth
    span = width // PIECES
    half = width // 2
    near, far = 0, 2 * ROW
    in_far = jnp.where(slab >= cut, 1, 0)
    host_row = jnp.where(slab >= cut, far, near)
    adopt = cut - turn_at
    wide = slabs - turn_at
    is_near, is_far = y == 0, y == 2
    is_host = jnp.logical_or(is_near, is_far)
    is_main = jnp.logical_and(is_host, x // e_local == mom)
    is_helper = jnp.logical_and(is_host, x // e_local != mom)
    at_start = slab == 0
    offset = jnp.where(is_near, 0, turn_at)
    count = jnp.where(is_near, turn_at, wide)
    reach = jnp.where(is_near, cut, wide)

    def send(src, dst, send_sem, recv_sem, **where):
        return pltpu.make_async_remote_copy(
            src_ref=src, dst_ref=dst, send_sem=send_sem, recv_sem=recv_sem,
            device_id=where, device_id_type=MESH,
        )

    def arrived(dst, recv_sem):
        send(dst, dst, s_hop.at[0], recv_sem, mom=other).wait_recv()

    loads = []
    for part in range(2):
        loads.append(pltpu.make_async_copy(hop_in.at[part], hop.at[part], s_in.at[part]))
        for e in range(e_local):
            sem = s_in.at[2 + e * 2 + part]
            loads.append(pltpu.make_async_copy(sigma_in.at[e, part], sigma.at[e, part], sem))
    for item in loads:
        item.start()
    barrier = pltpu.get_barrier_semaphore()

    def greet(**where):
        pl.semaphore_signal(barrier, inc=1, device_id=where, device_id_type=MESH)

    opposite = lax.rem(x + 2, ROW)
    is_detour = opposite // e_local == mom
    is_relay = jnp.logical_and(y == 3, is_detour)
    starts_detour = jnp.logical_and(y == 0, jnp.logical_and(is_detour, x != 0))
    passes = jnp.logical_and(is_relay, x != 0)
    greet(mom=other)
    for turn in range(1, depth):
        greet(energy=lax.rem(plane + turn, depth))

    @pl.when(is_main)
    def _():
        first_source = jnp.where(is_near, 0, cut)

        def call(j, carry):
            @pl.when(first_source + j != slab)
            def _():
                greet(slab=first_source + j)

            return carry

        lax.fori_loop(0, jnp.where(is_near, cut, slabs - cut), call, 0)

        @pl.when(jnp.logical_and(is_near, x != 2))
        def _():
            greet(slab=3 * ROW + opposite)

        @pl.when(is_far)
        def _():
            greet(slab=x)

    @pl.when(jnp.logical_and(is_near, jnp.logical_not(is_main)))
    def _():
        greet(slab=far + x)

    @pl.when(passes)
    def _():
        greet(slab=x)

    for c in range(ROW):

        @pl.when(jnp.logical_and(is_host, x != c))
        def _():
            greet(slab=y * ROW + c, mom=c // e_local)

    @pl.when(jnp.logical_not(is_host))
    def _():
        greet(slab=far + x, mom=x // e_local)
        for turn in range(1, ROW):
            greet(slab=y * ROW + lax.rem(x + turn, ROW))

    @pl.when(y == 1)
    def _():
        greet(slab=near + x, mom=x // e_local)

    for item in loads:
        item.wait()
    eye = eye_mask(half)
    place = slab - in_far * turn_at

    def host_of(e):
        return host_row + e_local * mom + e

    def base_copy(e):
        return send(outgoing.at[e], base.at[place], s_base.at[e], r_base.at[place], slab=host_of(e))

    def coup_copy(e):
        return send(couple, coup.at[place], s_coup.at[e], r_coup.at[place], slab=host_of(e))

    def is_remote(e):
        return host_of(e) != slab

    def detours(e):
        return jnp.logical_and(y == 0, host_of(e) == opposite)

    def sends_coup(e):
        direct = jnp.logical_and(is_remote(e), jnp.logical_not(detours(e)))
        return jnp.logical_and(direct, jnp.logical_not(at_start))

    def detour_copy(part):
        return send(
            couple.at[part], box_a.at[0, part], s_detour.at[part], r_detour.at[part],
            slab=slab + 3 * ROW,
        )

    def pass_in(part):
        return send(
            box_a.at[0, part], coup.at[x, part], s_detour.at[part], r_coup.at[x], slab=opposite
        )

    own_coup = pltpu.make_async_copy(couple, coup.at[place], s_in.at[0])

    for e in range(e_local):
        level = -0.5 + ((plane * e_local + e).astype(jnp.float32) + 0.5) / (depth * e_local) - onsite[...]
        real = on_diagonal(
            -hop[0] - sigma[e, 0],
            lambda block, n: block + jnp.where(eye, level[:, n * half : (n + 1) * half], 0.0),
        )
        imag = on_diagonal(
            -hop[1] - sigma[e, 1], lambda block, n: block + jnp.where(eye, ETA, 0.0)
        )
        store(outgoing.at[e], (real, imag))

    def one(flag):
        return jnp.where(flag, 1, 0)

    expected = depth + jnp.where(is_host, 0, ROW - 1) + one(starts_detour) + one(passes)
    for e in range(e_local):
        expected = expected + one(is_remote(e))
    outputs = 2 * (ROW - 1) + jnp.where(is_near, 3, 4)
    expected = expected + jnp.where(is_main, outputs, one(is_far))
    pl.semaphore_wait(barrier, expected)

    @pl.when(starts_detour)
    def _():
        for part in range(2):
            detour_copy(part).start()

    for e in range(e_local):

        @pl.when(jnp.logical_and(is_remote(e), jnp.logical_not(passes)))
        def _():
            base_copy(e).start()

    for e in range(e_local):

        @pl.when(jnp.logical_and(sends_coup(e), jnp.logical_not(passes)))
        def _():
            coup_copy(e).start()

    for e in range(e_local):

        @pl.when(jnp.logical_not(is_remote(e)))
        def _():
            base[place] = outgoing[e]
            own_coup.start()

    @pl.when(passes)
    def _():
        for part in range(2):
            arrived(box_a.at[0, part], r_detour.at[part])
            pass_in(part).start()
        for part in range(2):
            pass_in(part).wait_send()
        for e in range(e_local):
            base_copy(e).start()
        for e in range(e_local):
            coup_copy(e).start()

    def fill(e, carry):
        def entry(f, inner):
            value = jnp.float32(0.0)
            for mode in range(shifts.shape[0]):
                value = value + jnp.where(f == e + shifts[mode], weights[0, mode], 0.0)
                value = value + jnp.where(f == e - shifts[mode], weights[1, mode], 0.0)
            mix[e, f] = value * 0.5
            return inner

        return lax.fori_loop(0, depth * e_local, entry, carry)

    lax.fori_loop(0, depth * e_local, fill, 0)

    @pl.when(is_main)
    def _():
        own_coup.wait()

    def hcoup_copy(j):
        return send(coup.at[j], h_coup.at[j], s_hcoup.at[j], r_hcoup.at[j], mom=other)

    def hgreen_copy(j):
        return send(green.at[j + 1], h_green.at[j], s_hgreen.at[j], r_hgreen.at[j], mom=other)

    def hop_copy():
        return send(green.at[cut], green.at[adopt], s_hop.at[0], r_hop.at[0], slab=slab + far)

    def adopt_coup(a):
        return send(coup.at[turn_at + a], coup.at[a], s_adopt.at[a], r_coup.at[a], slab=slab + far)

    def adopt_green(a):
        return send(
            green.at[turn_at + a + 1], green.at[a + 1], s_adopt.at[adopt + a], r_adopt.at[a],
            slab=slab + far,
        )

    def used(j):
        return jnp.logical_and(
            jnp.logical_not(is_first(j)), jnp.logical_or(is_far, j < turn_at)
        )

    def held(j, part):
        late = offset + j >= slabs - ROW
        return jnp.logical_and(late, jnp.logical_or(part == 1, offset + j < slabs - HASTE))

    def chain_copy(j):
        return send(h_chain.at[j + 1], chain.at[j], s_chain.at[j], r_chain.at[j], mom=other)

    def back_copy():
        return send(h_chain.at[0], h_chain.at[turn_at], s_back.at[0], r_back.at[0], slab=slab - far)

    def piece(n):
        return pl.ds(pl.multiple_of(lax.rem(plane * PIECES // depth + ORDER[n], PIECES) * span, 8), span)

    def first_copy(j, part, n):
        return send(
            full.at[j, part, piece(n)], gathered.at[x, piece(n)], s_first.at[j, part, n],
            r_first.at[x, n], slab=offset + j, mom=part,
        )

    def relay_copy(j, part, n):
        where = piece(n)
        return send(
            full.at[j, part, where], full.at[lax.rem(offset + j, ROW), part, where],
            s_first.at[j, part, n], r_relay.at[lax.rem(offset + j, ROW), n],
            slab=(offset + j) // ROW * ROW + x, mom=part,
        )

    def relayed(j):
        return (offset + j) // ROW != y

    def pass_copy(r, n):
        return send(
            full.at[r, mom, piece(n)], gathered.at[x, piece(n)], s_first.at[r, 0, n],
            r_first.at[x, n], slab=y * ROW + r,
        )

    def is_first(j):
        return jnp.logical_and(is_near, j == 0)

    def is_last(j):
        return jnp.logical_and(is_far, j == count - 1)

    def first_remote(j, part):
        return jnp.logical_or(offset + j != slab, part != mom)

    @pl.when(is_main)
    def _():
        @pl.when(is_far)
        def _():
            arrived(green.at[adopt], r_hop.at[0])

        def forward(j, carry):
            @pl.when(j != place)
            def _():
                arrived(base.at[j], r_base.at[j])

            @pl.when(is_first(j))
            def _():
                left[...] = jnp.zeros_like(left)

            @pl.when(jnp.logical_not(is_first(j)))
            def _():
                @pl.when(j != place)
                def _():
                    arrived(coup.at[j], r_coup.at[j])

                @pl.when(used(j))
                def _():
                    hcoup_copy(j).start()

                coupling = load(coup.at[j])
                half_way = mul(prep(load(green.at[j])), prep_adjoint(coupling))
                store(left, mul(prep(coupling), prep(half_way)))

            store(
                green.at[j + 1],
                newton_inverse((base[j, 0] - left[0], base[j, 1] - left[1])),
            )

            @pl.when(used(j))
            def _():
                hgreen_copy(j).start()

            @pl.when(jnp.logical_and(is_far, j == wide - 3))
            def _():
                for a in range(adopt):
                    arrived(coup.at[a], r_coup.at[a])
                    if a < adopt - 1:
                        arrived(green.at[a + 1], r_adopt.at[a])
                    hcoup_copy(a).start()
                    hgreen_copy(a).start()

            return carry

        lax.fori_loop(jnp.where(is_near, 0, adopt), reach, forward, 0)

        @pl.when(is_near)
        def _():
            hop_copy().start()
            hop_copy().wait_send()
            for a in range(adopt):
                adopt_coup(a).start()
                if a < adopt - 1:
                    adopt_green(a).start()

        def backward(turn, carry):
            j = count - 1 - turn

            @pl.when(is_last(j))
            def _():
                full[j] = green[j + 1]

            @pl.when(jnp.logical_not(is_last(j)))
            def _():
                pair = load(green.at[j + 1])
                ready = prep(pair)
                arrived(chain.at[j], r_chain.at[j])
                extra = mul(prep(mul(ready, prep(load(chain.at[j])))), ready)
                store(full.at[j], (pair[0] + extra[0], pair[1] + extra[1]))

            for n in range(PIECES):
                for part in range(2):
                    now = jnp.logical_and(is_far, jnp.logical_not(relayed(j)))
                    if n == 0:
                        now = jnp.logical_or(jnp.logical_and(is_near, jnp.logical_not(relayed(j))), now)

                    @pl.when(jnp.logical_and(first_remote(j, part), now))
                    def _():
                        first_copy(j, part, n).start()

            for part in range(2):

                @pl.when(jnp.logical_and(relayed(j), jnp.logical_not(held(j, part))))
                def _():
                    for n in range(PIECES):
                        relay_copy(j, part, n).start()

                @pl.when(jnp.logical_not(first_remote(j, part)))
                def _():
                    gathered[x] = full[j, part]

            return carry

        lax.fori_loop(0, count, backward, 0)

        @pl.when(is_near)
        def _():
            def sweep(n, act):
                def one(j, carry):
                    for part in range(2):

                        @pl.when(jnp.logical_and(first_remote(j, part), jnp.logical_not(relayed(j))))
                        def _():
                            act(first_copy(j, part, n))

                    return carry

                lax.fori_loop(0, count, one, 0)

            for n in range(1, PIECES):
                sweep(n, lambda copy: copy.start())
                sweep(n - 1, lambda copy: copy.wait_send())
            sweep(PIECES - 1, lambda copy: copy.wait_send())

        @pl.when(is_far)
        def _():
            pl.semaphore_wait(token, 1)

            def release(turn, carry):
                j = lax.rem(2 * count - 1 - turn, count)
                for part in range(2):
                    mine = jnp.logical_and(held(j, part), turn // count == part)

                    @pl.when(mine)
                    def _():
                        for n in range(PIECES):
                            relay_copy(j, part, n).start()

                return carry

            lax.fori_loop(0, 2 * count, release, 0)

    @pl.when(is_helper)
    def _():
        def forward(step, carry):
            early = wide - 2 - adopt
            late = jnp.where(step < early + adopt, step - early, step)
            j = jnp.where(is_near, step, jnp.where(step < early, step + adopt, late))

            @pl.when(jnp.logical_not(is_first(j)))
            def _():
                arrived(h_coup.at[j], r_hcoup.at[j])
                coupling = load(h_coup.at[j])
                adjoint = (coupling[0].T, -coupling[1].T)
                ready_left, ready_right = prep(adjoint), prep(coupling)
                store(h_adj.at[j], adjoint)
                arrived(h_green.at[j], r_hgreen.at[j])
                ready = prep(load(h_green.at[j]))
                keep(h_first.at[j], prep(mul(ready_left, ready)))
                keep(h_second.at[j], prep(mul(ready, ready_right)))

            return carry

        lax.fori_loop(0, count, forward, 0)

        @pl.when(is_far)
        def _():
            h_chain[wide] = jnp.zeros_like(h_chain.at[wide])

        @pl.when(is_near)
        def _():
            arrived(h_chain.at[turn_at], r_back.at[0])

        def backward(turn, carry):
            j = count - 1 - turn

            @pl.when(jnp.logical_not(is_last(j)))
            def _():
                chain_copy(j).start()

            @pl.when(jnp.logical_not(is_first(j)))
            def _():
                extra = mul(fetch(h_first.at[j]), prep(load(h_chain.at[j + 1])))
                adjoint = load(h_adj.at[j])
                sums = (adjoint[0] + extra[0], adjoint[1] + extra[1])
                store(h_chain.at[j], mul(prep(sums), fetch(h_second.at[j])))

            return carry

        lax.fori_loop(0, count, backward, 0)

        @pl.when(is_far)
        def _():
            back_copy().start()
            back_copy().wait_send()
            pl.semaphore_signal(token, inc=1, device_id={"mom": other}, device_id_type=MESH)

    def second_copy(target):
        return send(
            summed.at[:, pl.ds(pl.multiple_of(target * share, 8), share)], mixed.at[plane],
            s_second.at[target], r_second.at[plane], energy=target,
        )

    @pl.when(jnp.logical_not(is_host))
    def _():
        def hand_on(turn, carry):
            r = jnp.where(jnp.logical_and(y == 1, turn >= 2), turn - 2, ROW - 1 - turn)
            for n in range(PIECES):
                arrived(full.at[r, mom, piece(n)], r_relay.at[r, n])

                @pl.when(r != x)
                def _():
                    pass_copy(r, n).start()

                @pl.when(r == x)
                def _():
                    gathered[x, piece(n)] = full[r, mom, piece(n)]

            return carry

        lax.fori_loop(0, ROW, hand_on, 0)

    local_first = jnp.logical_or(is_main, jnp.logical_not(is_host))
    per = depth // PIECES
    for n in range(PIECES):
        for c in range(ROW):

            @pl.when(jnp.logical_or(c != x, jnp.logical_not(local_first)))
            def _():
                arrived(gathered.at[c, piece(n)], r_first.at[c, n])

        for e in range(e_local):
            summed[e, piece(n)] = gathered[e, piece(n)] + gathered[e_local + e, piece(n)]
        for k in range(per):
            target = lax.rem(plane * PIECES // depth + ORDER[n], PIECES) * per + k

            @pl.when(target != plane)
            def _():
                second_copy(target).start()

    def mixing(source, start):
        values = [mixed[source, e] for e in range(e_local)]

        for e in range(depth * e_local):
            value = mix[e, source * e_local] * values[0]
            for k in range(1, e_local):
                value = value + mix[e, source * e_local + k] * values[k]
            total[e] = value if start else total[e] + value

    mixed[plane] = summed[:, pl.ds(pl.multiple_of(plane * share, 8), share)]
    mixing(plane, True)
    order = [turn for step in range(1, depth // 2 + 1) for turn in sorted({step, depth - step})]
    for turn in order:
        source = lax.rem(plane + turn, depth)
        arrived(mixed.at[source], r_second.at[source])
        mixing(source, False)

    last_copy = send(total, out.at[:, mom], s_last.at[0], r_last.at[0], mom=other)
    last_copy.start()
    own_last = pltpu.make_async_copy(total, out.at[:, mom], s_last.at[1])
    own_last.start()

    for e in range(e_local):

        @pl.when(is_remote(e))
        def _():
            base_copy(e).wait_send()

        @pl.when(sends_coup(e))
        def _():
            coup_copy(e).wait_send()

    @pl.when(is_main)
    def _():
        def drain(j, carry):
            @pl.when(used(j))
            def _():
                hcoup_copy(j).wait_send()
                hgreen_copy(j).wait_send()

            for part in range(2):

                direct = jnp.logical_and(is_far, jnp.logical_not(relayed(j)))

                @pl.when(jnp.logical_and(direct, first_remote(j, part)))
                def _():
                    for n in range(PIECES):
                        first_copy(j, part, n).wait_send()

                @pl.when(relayed(j))
                def _():
                    for n in range(PIECES):
                        relay_copy(j, part, n).wait_send()

            return carry

        lax.fori_loop(0, count, drain, 0)

        @pl.when(is_near)
        def _():
            for a in range(adopt):
                adopt_coup(a).wait_send()
                if a < adopt - 1:
                    adopt_green(a).wait_send()

    @pl.when(starts_detour)
    def _():
        for part in range(2):
            detour_copy(part).wait_send()

    @pl.when(jnp.logical_not(is_host))
    def _():
        for r in range(ROW):

            @pl.when(r != x)
            def _():
                for n in range(PIECES):
                    pass_copy(r, n).wait_send()

    @pl.when(is_helper)
    def _():
        def drain(j, carry):
            @pl.when(jnp.logical_not(is_last(j)))
            def _():
                chain_copy(j).wait_send()

            return carry

        lax.fori_loop(0, count, drain, 0)

    for turn in range(1, depth):
        second_copy(lax.rem(plane + turn, depth)).wait_send()
    last_copy.wait_send()
    own_last.wait()
    arrived(out.at[:, other], r_last.at[0])


def body(onsite, hop, couple, sigma_in, shifts, mode_weight):
    e_local = sigma_in.shape[0]
    width = onsite.shape[-1]
    slabs = lax.axis_size("slab")
    depth = lax.axis_size("energy")
    total = e_local * depth
    share = width // depth
    block = (2, width, width)
    slots = max(CUT, slabs - BACK)
    spare = max(1, CUT - BACK)

    def buffer(*shape):
        return pltpu.VMEM(shape, jnp.float32)

    def sems(*shape):
        return pltpu.SemaphoreType.DMA(shape)

    vmem = pl.BlockSpec(memory_space=pltpu.VMEM)
    smem = pl.BlockSpec(memory_space=pltpu.SMEM)
    stay = pl.BlockSpec(memory_space=pltpu.HBM)
    result = pl.pallas_call(
        functools.partial(kernel, CUT, BACK, slabs, depth, e_local),
        out_shape=jax.ShapeDtypeStruct((total, 2, share, width), jnp.float32),
        in_specs=[smem, smem, vmem, stay, stay, stay],
        out_specs=stay,
        scratch_shapes=[
            buffer(*block),
            buffer(e_local, *block),
            buffer(e_local, *block),
            buffer(*block),
            buffer(slots, *block),
            buffer(slots, *block),
            buffer(slots + 1, *block),
            buffer(slots, *block),
            buffer(slots, *block),
            pltpu.VMEM((slots, 6, width, width), jnp.bfloat16),
            pltpu.VMEM((slots, 6, width, width), jnp.bfloat16),
            buffer(ROW, width, width),
            buffer(e_local, width, width),
            buffer(depth, e_local, share, width),
            buffer(total, share, width),
            pltpu.SMEM((total, total), jnp.float32),
            sems(2 + 2 * e_local),
            sems(e_local), sems(slots), sems(e_local), sems(slots),
            sems(slots), sems(slots), sems(slots), sems(slots),
            sems(1), sems(1), sems(slots), sems(slots), sems(1), sems(1),
            sems(slots, 2, PIECES), sems(ROW, PIECES), sems(depth), sems(depth), sems(2), sems(1),
            sems(2 * spare), sems(spare), sems(ROW, PIECES), sems(2), sems(2), pltpu.SemaphoreType.REGULAR,
        ],
        compiler_params=pltpu.CompilerParams(
            collective_id=0, has_side_effects=True, vmem_limit_bytes=56 << 20
        ),
    )(shifts, mode_weight, onsite[0], hop[0, 0], couple[0, 0], sigma_in[:, 0])
    return result[:, None]


def solution(mesh):
    in_specs = (
        P("mom", "slab", None),
        P("mom", "slab", None, None, None),
        P("mom", "slab", None, None, None),
        P("energy", "slab", None, None, None),
        P(),
        P(),
    )
    out_specs = P(None, "slab", None, "energy", None)
    return jax.shard_map(body, mesh=mesh, in_specs=in_specs, out_specs=out_specs, check_vma=False)
```

```python
import functools

import jax
import jax.numpy as jnp
from jax import lax
from jax.experimental import pallas as pl
from jax.experimental.pallas import tpu as pltpu
from jax.sharding import PartitionSpec as P

ETA = 0.5
ROW = 4
CUT = 6
BACK = 5
PIECES = 4
ORDER = (2, 1, 3, 0)
HASTE = 3
MESH = pl.DeviceIdType.MESH


def split(mat):
    top = mat.astype(jnp.bfloat16)
    return top, (mat - top.astype(jnp.float32)).astype(jnp.bfloat16)


def prep(pair):
    return split(pair[0]), split(pair[1]), split(pair[0] + pair[1])


def prep_adjoint(pair):
    return prep((pair[0].T, -pair[1].T))


def mul(left, right):
    outs = []
    for (left_top, left_low), (top, low) in zip(left, right):
        outs.append(
            jnp.dot(
                jnp.concatenate([left_top, left_top, left_low], axis=1),
                jnp.concatenate([top, low, top], axis=0),
                preferred_element_type=jnp.float32,
            )
        )
    return outs[0] - outs[1], outs[2] - (outs[0] + outs[1])


def eye_mask(size):
    shape = (size, size)
    return lax.broadcasted_iota(jnp.int32, shape, 0) == lax.broadcasted_iota(jnp.int32, shape, 1)


def on_diagonal(mat, change):
    half = mat.shape[0] // 2
    upper = jnp.concatenate([change(mat[:half, :half], 0), mat[:half, half:]], axis=1)
    lower = jnp.concatenate([mat[half:, :half], change(mat[half:, half:], 1)], axis=1)
    return jnp.concatenate([upper, lower], axis=0)


def newton_inverse(mat):
    half = mat[0].shape[0] // 2
    eye = eye_mask(half)
    blocks = [
        [jnp.where(eye, part[:half, :half], 0.0), jnp.where(eye, part[half:, half:], 0.0)]
        for part in mat
    ]

    def inverse(diag):
        scale = 1.0 / (diag[0] * diag[0] + diag[1] * diag[1])
        return diag[0] * scale, -diag[1] * scale

    row = inverse(
        [jnp.concatenate([jnp.sum(b, axis=0, keepdims=True) for b in pair], axis=1) for pair in blocks]
    )
    col = inverse(
        [jnp.concatenate([jnp.sum(b, axis=1, keepdims=True) for b in pair], axis=0) for pair in blocks]
    )
    off = [on_diagonal(part, lambda block, n: jnp.where(eye, 0.0, block)) for part in mat]
    first = (off[0] * row[0] - off[1] * row[1], off[0] * row[1] + off[1] * row[0])
    fixed = prep(first)
    second = mul(fixed, fixed)
    third = mul(prep(second), fixed)
    real = second[0] - first[0] - third[0]
    imag = second[1] - first[1] - third[1]
    real = on_diagonal(real, lambda block, n: block + jnp.where(eye, 1.0, 0.0))
    return col[0] * real - col[1] * imag, col[0] * imag + col[1] * real


def load(ref):
    return ref[0], ref[1]


def keep(ref, ready):
    for n, parts in enumerate(ready):
        ref[2 * n] = parts[0]
        ref[2 * n + 1] = parts[1]


def fetch(ref):
    return tuple((ref[2 * n], ref[2 * n + 1]) for n in range(3))


def store(ref, pair):
    ref[0] = pair[0]
    ref[1] = pair[1]


def kernel(
    cut, turn_at, slabs, depth, e_local,
    shifts, weights, onsite, hop_in, couple, sigma_in, out,
    hop, sigma, outgoing, left, box_a, box_b, box_c, box_d, box_e, h_first, h_second, gathered, summed, mixed, total,
    mix, s_in,
    s_base, r_base, s_coup, r_coup, s_hcoup, r_hcoup, s_hgreen, r_hgreen,
    s_hop, r_hop, s_chain, r_chain, s_back, r_back, s_first, r_first,
    s_second, r_second, s_last, r_last, s_adopt, r_adopt, r_relay, s_detour, r_detour, token,
):
    base = h_coup = h_adj = box_a
    coup = h_green = box_b
    green = h_chain = box_c
    chain = box_d
    full = box_e
    slab = lax.axis_index("slab")
    plane = lax.axis_index("energy")
    mom = lax.axis_index("mom")
    y, x = slab // ROW, lax.rem(slab, ROW)
    other = 1 - mom
    width = hop.shape[-1]
    share = width // depth
    span = width // PIECES
    half = width // 2
    near, far = 0, 2 * ROW
    in_far = jnp.where(slab >= cut, 1, 0)
    host_row = jnp.where(slab >= cut, far, near)
    adopt = cut - turn_at
    wide = slabs - turn_at
    is_near, is_far = y == 0, y == 2
    is_host = jnp.logical_or(is_near, is_far)
    is_main = jnp.logical_and(is_host, x // e_local == mom)
    is_helper = jnp.logical_and(is_host, x // e_local != mom)
    at_start = slab == 0
    offset = jnp.where(is_near, 0, turn_at)
    count = jnp.where(is_near, turn_at, wide)
    reach = jnp.where(is_near, cut, wide)

    def send(src, dst, send_sem, recv_sem, **where):
        return pltpu.make_async_remote_copy(
            src_ref=src, dst_ref=dst, send_sem=send_sem, recv_sem=recv_sem,
            device_id=where, device_id_type=MESH,
        )

    def arrived(dst, recv_sem):
        send(dst, dst, s_hop.at[0], recv_sem, mom=other).wait_recv()

    loads = []
    for part in range(2):
        loads.append(pltpu.make_async_copy(hop_in.at[part], hop.at[part], s_in.at[part]))
        for e in range(e_local):
            sem = s_in.at[2 + e * 2 + part]
            loads.append(pltpu.make_async_copy(sigma_in.at[e, part], sigma.at[e, part], sem))
    for item in loads:
        item.start()
    barrier = pltpu.get_barrier_semaphore()

    def greet(**where):
        pl.semaphore_signal(barrier, inc=1, device_id=where, device_id_type=MESH)

    opposite = lax.rem(x + 2, ROW)
    is_detour = opposite // e_local == mom
    is_relay = jnp.logical_and(y == 3, is_detour)
    starts_detour = jnp.logical_and(y == 0, jnp.logical_and(is_detour, x != 0))
    passes = jnp.logical_and(is_relay, x != 0)
    greet(mom=other)
    for turn in range(1, depth):
        greet(energy=lax.rem(plane + turn, depth))

    @pl.when(is_main)
    def _():
        first_source = jnp.where(is_near, 0, cut)

        def call(j, carry):
            @pl.when(first_source + j != slab)
            def _():
                greet(slab=first_source + j)

            return carry

        lax.fori_loop(0, jnp.where(is_near, cut, slabs - cut), call, 0)

        @pl.when(jnp.logical_and(is_near, x != 2))
        def _():
            greet(slab=3 * ROW + opposite)

        @pl.when(is_far)
        def _():
            greet(slab=x)

    @pl.when(jnp.logical_and(is_near, jnp.logical_not(is_main)))
    def _():
        greet(slab=far + x)

    @pl.when(passes)
    def _():
        greet(slab=x)

    for c in range(ROW):

        @pl.when(jnp.logical_and(is_host, x != c))
        def _():
            greet(slab=y * ROW + c, mom=c // e_local)

    @pl.when(jnp.logical_not(is_host))
    def _():
        greet(slab=far + x, mom=x // e_local)
        for turn in range(1, ROW):
            greet(slab=y * ROW + lax.rem(x + turn, ROW))

    @pl.when(y == 1)
    def _():
        greet(slab=near + x, mom=x // e_local)

    for item in loads:
        item.wait()
    eye = eye_mask(half)
    place = slab - in_far * turn_at

    def host_of(e):
        return host_row + e_local * mom + e

    def base_copy(e):
        return send(outgoing.at[e], base.at[place], s_base.at[e], r_base.at[place], slab=host_of(e))

    def coup_copy(e):
        return send(couple, coup.at[place], s_coup.at[e], r_coup.at[place], slab=host_of(e))

    def is_remote(e):
        return host_of(e) != slab

    def detours(e):
        return jnp.logical_and(y == 0, host_of(e) == opposite)

    def sends_coup(e):
        direct = jnp.logical_and(is_remote(e), jnp.logical_not(detours(e)))
        return jnp.logical_and(direct, jnp.logical_not(at_start))

    def detour_copy(part):
        return send(
            couple.at[part], box_a.at[0, part], s_detour.at[part], r_detour.at[part],
            slab=slab + 3 * ROW,
        )

    def pass_in(part):
        return send(
            box_a.at[0, part], coup.at[x, part], s_detour.at[part], r_coup.at[x], slab=opposite
        )

    own_coup = pltpu.make_async_copy(couple, coup.at[place], s_in.at[0])

    for e in range(e_local):
        level = -0.5 + ((plane * e_local + e).astype(jnp.float32) + 0.5) / (depth * e_local) - onsite[...]
        real = on_diagonal(
            -hop[0] - sigma[e, 0],
            lambda block, n: block + jnp.where(eye, level[:, n * half : (n + 1) * half], 0.0),
        )
        imag = on_diagonal(
            -hop[1] - sigma[e, 1], lambda block, n: block + jnp.where(eye, ETA, 0.0)
        )
        store(outgoing.at[e], (real, imag))

    def one(flag):
        return jnp.where(flag, 1, 0)

    expected = depth + jnp.where(is_host, 0, ROW - 1) + one(starts_detour) + one(passes)
    for e in range(e_local):
        expected = expected + one(is_remote(e))
    outputs = 2 * (ROW - 1) + jnp.where(is_near, 3, 4)
    expected = expected + jnp.where(is_main, outputs, one(is_far))
    pl.semaphore_wait(barrier, expected)

    @pl.when(starts_detour)
    def _():
        for part in range(2):
            detour_copy(part).start()

    for e in range(e_local):

        @pl.when(jnp.logical_and(is_remote(e), jnp.logical_not(passes)))
        def _():
            base_copy(e).start()

    for e in range(e_local):

        @pl.when(jnp.logical_and(sends_coup(e), jnp.logical_not(passes)))
        def _():
            coup_copy(e).start()

    for e in range(e_local):

        @pl.when(jnp.logical_not(is_remote(e)))
        def _():
            base[place] = outgoing[e]
            own_coup.start()

    @pl.when(passes)
    def _():
        for part in range(2):
            arrived(box_a.at[0, part], r_detour.at[part])
            pass_in(part).start()
        for part in range(2):
            pass_in(part).wait_send()
        for e in range(e_local):
            base_copy(e).start()
        for e in range(e_local):
            coup_copy(e).start()

    def fill(e, carry):
        def entry(f, inner):
            value = jnp.float32(0.0)
            for mode in range(shifts.shape[0]):
                value = value + jnp.where(f == e + shifts[mode], weights[0, mode], 0.0)
                value = value + jnp.where(f == e - shifts[mode], weights[1, mode], 0.0)
            mix[e, f] = value * 0.5
            return inner

        return lax.fori_loop(0, depth * e_local, entry, carry)

    lax.fori_loop(0, depth * e_local, fill, 0)

    @pl.when(is_main)
    def _():
        own_coup.wait()

    def hcoup_copy(j):
        return send(coup.at[j], h_coup.at[j], s_hcoup.at[j], r_hcoup.at[j], mom=other)

    def hgreen_copy(j):
        return send(green.at[j + 1], h_green.at[j], s_hgreen.at[j], r_hgreen.at[j], mom=other)

    def hop_copy():
        return send(green.at[cut], green.at[adopt], s_hop.at[0], r_hop.at[0], slab=slab + far)

    def adopt_coup(a):
        return send(coup.at[turn_at + a], coup.at[a], s_adopt.at[a], r_coup.at[a], slab=slab + far)

    def adopt_green(a):
        return send(
            green.at[turn_at + a + 1], green.at[a + 1], s_adopt.at[adopt + a], r_adopt.at[a],
            slab=slab + far,
        )

    def used(j):
        return jnp.logical_and(
            jnp.logical_not(is_first(j)), jnp.logical_or(is_far, j < turn_at)
        )

    def held(j, part):
        late = offset + j >= slabs - ROW
        return jnp.logical_and(late, jnp.logical_or(part == 1, offset + j < slabs - HASTE))

    def chain_copy(j):
        return send(h_chain.at[j + 1], chain.at[j], s_chain.at[j], r_chain.at[j], mom=other)

    def back_copy():
        return send(h_chain.at[0], h_chain.at[turn_at], s_back.at[0], r_back.at[0], slab=slab - far)

    def piece(n):
        return pl.ds(pl.multiple_of(lax.rem(plane * PIECES // depth + ORDER[n], PIECES) * span, 8), span)

    def first_copy(j, part, n):
        return send(
            full.at[j, part, piece(n)], gathered.at[x, piece(n)], s_first.at[j, part, n],
            r_first.at[x, n], slab=offset + j, mom=part,
        )

    def relay_copy(j, part, n):
        where = piece(n)
        return send(
            full.at[j, part, where], full.at[lax.rem(offset + j, ROW), part, where],
            s_first.at[j, part, n], r_relay.at[lax.rem(offset + j, ROW), n],
            slab=(offset + j) // ROW * ROW + x, mom=part,
        )

    def relayed(j):
        return (offset + j) // ROW != y

    def pass_copy(r, n):
        return send(
            full.at[r, mom, piece(n)], gathered.at[x, piece(n)], s_first.at[r, 0, n],
            r_first.at[x, n], slab=y * ROW + r,
        )

    def is_first(j):
        return jnp.logical_and(is_near, j == 0)

    def is_last(j):
        return jnp.logical_and(is_far, j == count - 1)

    def first_remote(j, part):
        return jnp.logical_or(offset + j != slab, part != mom)

    @pl.when(is_main)
    def _():
        @pl.when(is_far)
        def _():
            arrived(green.at[adopt], r_hop.at[0])

        def forward(j, carry):
            @pl.when(j != place)
            def _():
                arrived(base.at[j], r_base.at[j])

            @pl.when(is_first(j))
            def _():
                left[...] = jnp.zeros_like(left)

            @pl.when(jnp.logical_not(is_first(j)))
            def _():
                @pl.when(j != place)
                def _():
                    arrived(coup.at[j], r_coup.at[j])

                @pl.when(used(j))
                def _():
                    hcoup_copy(j).start()

                coupling = load(coup.at[j])
                half_way = mul(prep(load(green.at[j])), prep_adjoint(coupling))
                store(left, mul(prep(coupling), prep(half_way)))

            store(
                green.at[j + 1],
                newton_inverse((base[j, 0] - left[0], base[j, 1] - left[1])),
            )

            @pl.when(used(j))
            def _():
                hgreen_copy(j).start()

            @pl.when(jnp.logical_and(is_far, j == wide - 3))
            def _():
                for a in range(adopt):
                    arrived(coup.at[a], r_coup.at[a])
                    if a < adopt - 1:
                        arrived(green.at[a + 1], r_adopt.at[a])
                    hcoup_copy(a).start()
                    hgreen_copy(a).start()

            return carry

        lax.fori_loop(jnp.where(is_near, 0, adopt), reach, forward, 0)

        @pl.when(is_near)
        def _():
            hop_copy().start()
            hop_copy().wait_send()
            for a in range(adopt):
                adopt_coup(a).start()
                if a < adopt - 1:
                    adopt_green(a).start()

        def backward(turn, carry):
            j = count - 1 - turn

            @pl.when(is_last(j))
            def _():
                full[j] = green[j + 1]

            @pl.when(jnp.logical_not(is_last(j)))
            def _():
                pair = load(green.at[j + 1])
                ready = prep(pair)
                arrived(chain.at[j], r_chain.at[j])
                extra = mul(prep(mul(ready, prep(load(chain.at[j])))), ready)
                store(full.at[j], (pair[0] + extra[0], pair[1] + extra[1]))

            for n in range(PIECES):
                for part in range(2):
                    now = jnp.logical_and(is_far, jnp.logical_not(relayed(j)))
                    if n < 2:
                        now = jnp.logical_or(jnp.logical_and(is_near, jnp.logical_not(relayed(j))), now)

                    @pl.when(jnp.logical_and(first_remote(j, part), now))
                    def _():
                        first_copy(j, part, n).start()

            for part in range(2):

                @pl.when(jnp.logical_and(relayed(j), jnp.logical_not(held(j, part))))
                def _():
                    for n in range(PIECES):
                        relay_copy(j, part, n).start()

                @pl.when(jnp.logical_not(first_remote(j, part)))
                def _():
                    gathered[x] = full[j, part]

            return carry

        lax.fori_loop(0, count, backward, 0)

        @pl.when(is_near)
        def _():
            def sweep(n, act):
                def one(j, carry):
                    for part in range(2):

                        @pl.when(jnp.logical_and(first_remote(j, part), jnp.logical_not(relayed(j))))
                        def _():
                            act(first_copy(j, part, n))

                    return carry

                lax.fori_loop(0, count, one, 0)

            for n in range(2, PIECES):
                sweep(n, lambda copy: copy.start())
                sweep(n - 2, lambda copy: copy.wait_send())
            sweep(PIECES - 2, lambda copy: copy.wait_send())
            sweep(PIECES - 1, lambda copy: copy.wait_send())

        @pl.when(is_far)
        def _():
            pl.semaphore_wait(token, 1)

            def release(turn, carry):
                j = lax.rem(2 * count - 1 - turn, count)
                for part in range(2):
                    mine = jnp.logical_and(held(j, part), turn // count == part)

                    @pl.when(mine)
                    def _():
                        for n in range(PIECES):
                            relay_copy(j, part, n).start()

                return carry

            lax.fori_loop(0, 2 * count, release, 0)

    @pl.when(is_helper)
    def _():
        def forward(step, carry):
            early = wide - 2 - adopt
            late = jnp.where(step < early + adopt, step - early, step)
            j = jnp.where(is_near, step, jnp.where(step < early, step + adopt, late))

            @pl.when(jnp.logical_not(is_first(j)))
            def _():
                arrived(h_coup.at[j], r_hcoup.at[j])
                coupling = load(h_coup.at[j])
                adjoint = (coupling[0].T, -coupling[1].T)
                ready_left, ready_right = prep(adjoint), prep(coupling)
                store(h_adj.at[j], adjoint)
                arrived(h_green.at[j], r_hgreen.at[j])
                ready = prep(load(h_green.at[j]))
                keep(h_first.at[j], prep(mul(ready_left, ready)))
                keep(h_second.at[j], prep(mul(ready, ready_right)))

            return carry

        lax.fori_loop(0, count, forward, 0)

        @pl.when(is_far)
        def _():
            h_chain[wide] = jnp.zeros_like(h_chain.at[wide])

        @pl.when(is_near)
        def _():
            arrived(h_chain.at[turn_at], r_back.at[0])

        def backward(turn, carry):
            j = count - 1 - turn

            @pl.when(jnp.logical_not(is_last(j)))
            def _():
                chain_copy(j).start()

            @pl.when(jnp.logical_not(is_first(j)))
            def _():
                extra = mul(fetch(h_first.at[j]), prep(load(h_chain.at[j + 1])))
                adjoint = load(h_adj.at[j])
                sums = (adjoint[0] + extra[0], adjoint[1] + extra[1])
                store(h_chain.at[j], mul(prep(sums), fetch(h_second.at[j])))

            return carry

        lax.fori_loop(0, count, backward, 0)

        @pl.when(is_far)
        def _():
            back_copy().start()
            back_copy().wait_send()
            pl.semaphore_signal(token, inc=1, device_id={"mom": other}, device_id_type=MESH)

    def second_copy(target):
        return send(
            summed.at[:, pl.ds(pl.multiple_of(target * share, 8), share)], mixed.at[plane],
            s_second.at[target], r_second.at[plane], energy=target,
        )

    @pl.when(jnp.logical_not(is_host))
    def _():
        def hand_on(turn, carry):
            r = jnp.where(jnp.logical_and(y == 1, turn >= 2), turn - 2, ROW - 1 - turn)
            for n in range(PIECES):
                arrived(full.at[r, mom, piece(n)], r_relay.at[r, n])

                @pl.when(r != x)
                def _():
                    pass_copy(r, n).start()

                @pl.when(r == x)
                def _():
                    gathered[x, piece(n)] = full[r, mom, piece(n)]

            return carry

        lax.fori_loop(0, ROW, hand_on, 0)

    local_first = jnp.logical_or(is_main, jnp.logical_not(is_host))
    per = depth // PIECES
    for n in range(PIECES):
        for c in range(ROW):

            @pl.when(jnp.logical_or(c != x, jnp.logical_not(local_first)))
            def _():
                arrived(gathered.at[c, piece(n)], r_first.at[c, n])

        for e in range(e_local):
            summed[e, piece(n)] = gathered[e, piece(n)] + gathered[e_local + e, piece(n)]
        for k in range(per):
            target = lax.rem(plane * PIECES // depth + ORDER[n], PIECES) * per + k

            @pl.when(target != plane)
            def _():
                second_copy(target).start()

    def mixing(source, start):
        values = [mixed[source, e] for e in range(e_local)]

        for e in range(depth * e_local):
            value = mix[e, source * e_local] * values[0]
            for k in range(1, e_local):
                value = value + mix[e, source * e_local + k] * values[k]
            total[e] = value if start else total[e] + value

    mixed[plane] = summed[:, pl.ds(pl.multiple_of(plane * share, 8), share)]
    mixing(plane, True)
    order = [turn for step in range(1, depth // 2 + 1) for turn in sorted({step, depth - step})]
    for turn in order:
        source = lax.rem(plane + turn, depth)
        arrived(mixed.at[source], r_second.at[source])
        mixing(source, False)

    last_copy = send(total, out.at[:, mom], s_last.at[0], r_last.at[0], mom=other)
    last_copy.start()
    own_last = pltpu.make_async_copy(total, out.at[:, mom], s_last.at[1])
    own_last.start()

    for e in range(e_local):

        @pl.when(is_remote(e))
        def _():
            base_copy(e).wait_send()

        @pl.when(sends_coup(e))
        def _():
            coup_copy(e).wait_send()

    @pl.when(is_main)
    def _():
        def drain(j, carry):
            @pl.when(used(j))
            def _():
                hcoup_copy(j).wait_send()
                hgreen_copy(j).wait_send()

            for part in range(2):

                direct = jnp.logical_and(is_far, jnp.logical_not(relayed(j)))

                @pl.when(jnp.logical_and(direct, first_remote(j, part)))
                def _():
                    for n in range(PIECES):
                        first_copy(j, part, n).wait_send()

                @pl.when(relayed(j))
                def _():
                    for n in range(PIECES):
                        relay_copy(j, part, n).wait_send()

            return carry

        lax.fori_loop(0, count, drain, 0)

        @pl.when(is_near)
        def _():
            for a in range(adopt):
                adopt_coup(a).wait_send()
                if a < adopt - 1:
                    adopt_green(a).wait_send()

    @pl.when(starts_detour)
    def _():
        for part in range(2):
            detour_copy(part).wait_send()

    @pl.when(jnp.logical_not(is_host))
    def _():
        for r in range(ROW):

            @pl.when(r != x)
            def _():
                for n in range(PIECES):
                    pass_copy(r, n).wait_send()

    @pl.when(is_helper)
    def _():
        def drain(j, carry):
            @pl.when(jnp.logical_not(is_last(j)))
            def _():
                chain_copy(j).wait_send()

            return carry

        lax.fori_loop(0, count, drain, 0)

    for turn in range(1, depth):
        second_copy(lax.rem(plane + turn, depth)).wait_send()
    last_copy.wait_send()
    own_last.wait()
    arrived(out.at[:, other], r_last.at[0])


def body(onsite, hop, couple, sigma_in, shifts, mode_weight):
    e_local = sigma_in.shape[0]
    width = onsite.shape[-1]
    slabs = lax.axis_size("slab")
    depth = lax.axis_size("energy")
    total = e_local * depth
    share = width // depth
    block = (2, width, width)
    slots = max(CUT, slabs - BACK)
    spare = max(1, CUT - BACK)

    def buffer(*shape):
        return pltpu.VMEM(shape, jnp.float32)

    def sems(*shape):
        return pltpu.SemaphoreType.DMA(shape)

    vmem = pl.BlockSpec(memory_space=pltpu.VMEM)
    smem = pl.BlockSpec(memory_space=pltpu.SMEM)
    stay = pl.BlockSpec(memory_space=pltpu.HBM)
    result = pl.pallas_call(
        functools.partial(kernel, CUT, BACK, slabs, depth, e_local),
        out_shape=jax.ShapeDtypeStruct((total, 2, share, width), jnp.float32),
        in_specs=[smem, smem, vmem, stay, stay, stay],
        out_specs=stay,
        scratch_shapes=[
            buffer(*block),
            buffer(e_local, *block),
            buffer(e_local, *block),
            buffer(*block),
            buffer(slots, *block),
            buffer(slots, *block),
            buffer(slots + 1, *block),
            buffer(slots, *block),
            buffer(slots, *block),
            pltpu.VMEM((slots, 6, width, width), jnp.bfloat16),
            pltpu.VMEM((slots, 6, width, width), jnp.bfloat16),
            buffer(ROW, width, width),
            buffer(e_local, width, width),
            buffer(depth, e_local, share, width),
            buffer(total, share, width),
            pltpu.SMEM((total, total), jnp.float32),
            sems(2 + 2 * e_local),
            sems(e_local), sems(slots), sems(e_local), sems(slots),
            sems(slots), sems(slots), sems(slots), sems(slots),
            sems(1), sems(1), sems(slots), sems(slots), sems(1), sems(1),
            sems(slots, 2, PIECES), sems(ROW, PIECES), sems(depth), sems(depth), sems(2), sems(1),
            sems(2 * spare), sems(spare), sems(ROW, PIECES), sems(2), sems(2), pltpu.SemaphoreType.REGULAR,
        ],
        compiler_params=pltpu.CompilerParams(
            collective_id=0, has_side_effects=True, vmem_limit_bytes=56 << 20
        ),
    )(shifts, mode_weight, onsite[0], hop[0, 0], couple[0, 0], sigma_in[:, 0])
    return result[:, None]


def solution(mesh):
    in_specs = (
        P("mom", "slab", None),
        P("mom", "slab", None, None, None),
        P("mom", "slab", None, None, None),
        P("energy", "slab", None, None, None),
        P(),
        P(),
    )
    out_specs = P(None, "slab", None, "energy", None)
    return jax.shard_map(body, mesh=mesh, in_specs=in_specs, out_specs=out_specs, check_vma=False)
```
